32 devices in a mesh: section: 2 (over x), img: 4 (over z), ch: 4 (over y, core).
Axes of the slice: x: 2, y: 2, z: 4, core: 2. Of those that a mesh axis runs over, the one named last changes fastest.
Arguments:
- pixels: bfloat16 [8, 32, 28, 640], P('img', 'ch'), may hold values from -6 to 6
- first_gain: float32 [640], replicated, may hold values from 0.25 to 1.75
- first_shift: float32 [640], replicated, may hold values from -3 to 3
- first_kernel: bfloat16 [3, 3, 640, 640], P(None, None, 'img'), may hold values from -0.078125 to 0.078125
- projection: bfloat16 [640, 2560], P('img'), may hold values from -0.25 to 0.25
- second_gain: float32 [2560], replicated, may hold values from 0.25 to 1.75
- second_shift: float32 [2560], replicated, may hold values from -3 to 3
- second_kernel: bfloat16 [3, 3, 2560, 2560], P(None, None, ('img', 'ch')), may hold values from -0.0390625 to 0.0390625
Outputs:
- section_outputs: bfloat16 [2, 8, 16, 14, 2560], P('section', 'img', 'ch')
The draws below stay inside these ranges and needn't reach their ends.
All inputs are finite; a program needn't handle non-finite values.
Results may differ from the reference program's by a relative error of at most 0.013.
Values may be sent and summed in bfloat16 or wider, within the bound.
No kernel may reach another device: no remote copies, remote signals or barrier semaphores. Data moves between devices by JAX's collectives and lax.ppermute only.
A program may use at most 128 MiB of HBM per device.

```python
import jax
import jax.numpy as jnp
from jax import lax

C1 = 640
C2 = 2560
W = 28
H = 32
HO = 16
WO = 14
IMAGES = 8


def shard_levels(rng, extent, cuts, low, high):
    level = 1.0
    for dim, blocks in cuts:
        draws = jax.random.uniform(jax.random.fold_in(jax.random.fold_in(rng, 6), dim), (blocks,), jnp.float32, low / len(cuts), high / len(cuts))
        level = level * jnp.repeat(jnp.exp(draws), extent[dim] // blocks).reshape((-1,) + (1,) * (len(extent) - 1 - dim))
    return level


def centred(rng, shape, width, bound, cuts=(), dtype=jnp.bfloat16):
    drawn = width * jax.random.normal(rng, shape, jnp.float32)
    if cuts:
        drawn = drawn * shard_levels(rng, shape, cuts, -0.22, 0.18)
    return jnp.clip(drawn, -bound, bound).astype(dtype)


def setup_inputs(seed: int = 0) -> dict:
    splits = jax.random.split(jax.random.key(seed), 9)
    pixels = centred(splits[0], (IMAGES, H, W, C1), 1.0, 6.0, ((0, 4), (1, 4)))
    first_gain = jnp.clip(1.0 + 0.15 * jax.random.normal(splits[1], (C1,), jnp.float32), 0.25, 1.75)
    first_shift = centred(splits[2], (C1,), 0.5, 3.0, (), jnp.float32)
    first_kernel = centred(splits[3], (3, 3, C1, C1), (9 * C1) ** -0.5, 0.078125, ((2, 4),))
    projection = centred(splits[4], (C1, C2), C1 ** -0.5, 0.25, ((0, 4),))
    second_gain = jnp.clip(1.0 + 0.15 * jax.random.normal(splits[5], (C2,), jnp.float32), 0.25, 1.75)
    second_shift = centred(splits[6], (C2,), 0.5, 3.0, (), jnp.float32)
    second_kernel = centred(splits[7], (3, 3, C2, C2), (9 * C2) ** -0.5, 0.0390625, ((2, 16),))
    return {"pixels": pixels, "first_gain": first_gain, "first_shift": first_shift, "first_kernel": first_kernel, "projection": projection, "second_gain": second_gain, "second_shift": second_shift, "second_kernel": second_kernel}


LAYOUT = ("NHWC", "HWIO", "NHWC")


def convolve(inputs, kernel, padding):
    return lax.conv_general_dilated(inputs, kernel, (1, 1), padding, dimension_numbers=LAYOUT, preferred_element_type=jnp.float32)


def reduce_resolution(value_entries):
    count, height, breadth, depth = value_entries.shape
    blocks = value_entries.reshape(count, height // 2, 2, breadth // 2, 2, depth)
    return jnp.sum(blocks, axis=(2, 4)) * 0.25


def reference(pixels, first_gain, first_shift, first_kernel, projection, second_gain, second_shift, second_kernel):
    normalized_input = jax.nn.relu(pixels.astype(jnp.float32) * first_gain + first_shift).astype(jnp.bfloat16)
    blended_result = convolve(normalized_input, first_kernel, ((1, 1), (1, 1))) + pixels.astype(jnp.float32)
    averaged_pixels = reduce_resolution(blended_result).astype(jnp.bfloat16)
    flat = averaged_pixels.reshape(IMAGES * HO * WO, C1)
    projected = jnp.dot(flat, projection, preferred_element_type=jnp.float32).astype(jnp.bfloat16)
    projected = projected.reshape(IMAGES, HO, WO, C2)
    second_in = jax.nn.relu(projected.astype(jnp.float32) * second_gain + second_shift).astype(jnp.bfloat16)
    block = convolve(second_in, second_kernel, ((1, 1), (1, 1))) + projected.astype(jnp.float32)
    return jnp.stack([projected, block.astype(jnp.bfloat16)])
```

```python
import jax
import jax.numpy as jnp
from jax import lax
from jax.sharding import PartitionSpec as P

LAYOUT = ("NHWC", "HWIO", "NHWC")
BF16 = jnp.bfloat16
F32 = jnp.float32


def conv(inputs, kernel, stride, padding):
    return lax.conv_general_dilated(
        inputs, kernel, (stride, stride), padding, dimension_numbers=LAYOUT, preferred_element_type=F32
    )


def swap(array, axis, k, unit=1):
    count = lax.axis_size(axis)
    return lax.ppermute(array, axis, [(i, i ^ (k * unit)) for i in range(count)])


def pick(stack, index):
    return lax.dynamic_index_in_dim(stack, index, 0, keepdims=False)


def body(pixels, first_gain, first_shift, first_kernel, projection, second_gain, second_shift, second_kernel):
    sec = lax.axis_index("section")
    z = lax.axis_index("img")
    ch = lax.axis_index("ch")
    sections = lax.axis_size("section")
    groups = lax.axis_size("img")
    shards = lax.axis_size("ch")
    pairs = shards // 2
    y, core = ch // 2, ch % 2
    per = pixels.shape[0] // sections
    _, rows, cols, depth = pixels.shape
    orows, ocols = rows // 2, cols // 2
    wide = second_gain.shape[0]
    slab = wide // groups
    kc = slab // pairs
    kd = kc // 2
    c1 = depth // groups

    other_kernel = swap(second_kernel, "ch", 1)
    proj_parts = projection.reshape(c1, groups, slab).transpose(1, 0, 2)
    proj_rel = [pick(proj_parts, z)] + [
        swap(pick(proj_parts, z ^ k), "img", k) for k in range(1, groups)
    ]
    proj_rel = jnp.stack(proj_rel)
    proj_slab = jnp.concatenate([pick(proj_rel, z ^ i) for i in range(groups)], axis=0)

    own = lax.dynamic_slice_in_dim(pixels, sec * per, per, 0)
    above = lax.ppermute(own[:, -1:], "ch", [(i, i + 1) for i in range(shards - 1)])
    below = lax.ppermute(own[:, :1], "ch", [(i + 1, i) for i in range(shards - 1)])
    ext = jnp.concatenate([above, own, below], axis=1)
    normed = jax.nn.relu(ext.astype(F32) * first_gain + first_shift).astype(BF16)
    row = lax.broadcasted_iota(jnp.int32, (1, rows + 2, 1, 1), 1)
    dead = ((row == 0) & (ch == 0)) | ((row == rows + 1) & (ch == shards - 1))
    normed = jnp.where(dead, jnp.zeros((), BF16), normed)
    blocks = normed.reshape(per, rows + 2, cols, groups, c1).transpose(3, 0, 1, 2, 4)
    shape = blocks.shape[1:]
    size = per * (rows + 2) * cols * c1
    flat = blocks.reshape(groups, size // 128, 128) if size % 128 == 0 else blocks
    mine = [pick(flat, z)] + [swap(pick(flat, z ^ k), "img", k) for k in range(1, groups)]
    acts = jnp.stack(mine).reshape((groups * per,) + shape[1:])
    wide_acts = jnp.pad(acts.astype(F32), ((0, 0), (0, 0), (1, 1), (0, 0)))
    tall = wide_acts[:, 1:] + wide_acts[:, :-1]
    box = ((tall[:, :, 1:] + tall[:, :, :-1]) * 0.25).astype(BF16)
    part = conv(box, first_kernel, 2, ((0, 0), (0, 0)))
    part = part.reshape(groups, per * orows * ocols, depth)
    sent = part.astype(BF16)
    total = part[0]
    for k in range(1, groups):
        total = total + swap(sent[k], "img", k).astype(F32)
    mean = jnp.sum(
        own.astype(F32).reshape(per, orows, 2, ocols, 2, depth), axis=(2, 4)
    ) * 0.25
    pooled = (total + mean.reshape(total.shape)).astype(BF16)
    pooled_all = jnp.stack([pooled] + [swap(pooled, "img", k) for k in range(1, groups)])
    px = per * orows * ocols
    projected = jnp.dot(
        pooled_all.reshape(groups * px, depth), proj_slab, preferred_element_type=F32
    ).astype(BF16)

    back = projected.reshape(groups, px, slab)
    back_rel = jnp.stack([back[0]] + [swap(back[k], "img", k) for k in range(1, groups)])
    mine_projected = jnp.concatenate([pick(back_rel, z ^ i) for i in range(groups)], axis=1)
    far_projected = lax.ppermute(mine_projected, "section", [(1, 0)])

    by_pair = projected.reshape(groups * px, pairs, kc).transpose(1, 0, 2)
    chip_rel = jnp.stack(
        [pick(by_pair, y)] + [swap(pick(by_pair, y ^ k), "ch", k, 2) for k in range(1, pairs)]
    )
    chip = jnp.stack([pick(chip_rel, y ^ i) for i in range(pairs)])
    chip = chip.reshape(pairs, groups * per, orows, ocols, kc)
    edges = swap(jnp.stack([chip[:, :, 0], chip[:, :, -1]]), "ch", 1)
    first_rows, last_rows = edges[0], edges[1]
    none = jnp.zeros_like(first_rows[:1])
    top = jnp.where(core == 0, jnp.concatenate([none, last_rows[:-1]]), last_rows)
    bottom = jnp.where(core == 0, first_rows, jnp.concatenate([first_rows[1:], none]))
    tall_in = jnp.concatenate([top[:, :, None], chip, bottom[:, :, None]], axis=2)
    start = (z * pairs + y) * kc
    gain = lax.dynamic_slice_in_dim(second_gain, start, kc)
    shift = lax.dynamic_slice_in_dim(second_shift, start, kc)
    second_in = jax.nn.relu(tall_in.astype(F32) * gain + shift).astype(BF16)
    pair_id = lax.broadcasted_iota(jnp.int32, (pairs, 1, orows + 2, 1, 1), 0)
    row_id = lax.broadcasted_iota(jnp.int32, (pairs, 1, orows + 2, 1, 1), 2)
    edge = ((pair_id == 0) & (row_id == 0) & (core == 0)) | (
        (pair_id == pairs - 1) & (row_id == orows + 1) & (core == 1)
    )
    second_in = jnp.where(edge, jnp.zeros((), BF16), second_in)
    second_in = second_in.reshape(pairs * groups * per, orows + 2, ocols, kc)
    low, high = second_in[..., :kd], second_in[..., kd:]
    in_own = jnp.where(core == 0, low, high)
    in_other = jnp.where(core == 0, high, low)

    chunks = 4 if wide % 512 == 0 else 1
    n = wide // chunks
    padded = jnp.pad(chip.reshape(-1, kc), ((0, 0), (n, n)))
    outs, fars = [], []
    for j in range(chunks):
        cut = slice(j * n, (j + 1) * n)
        value = conv(in_own, second_kernel[..., cut], 1, ((0, 0), (1, 1)))
        value = value + conv(in_other, other_kernel[..., cut], 1, ((0, 0), (1, 1)))
        at = jnp.clip(j * n - start + n, 0, n + kc)
        value = value.reshape(-1, n) + lax.dynamic_slice_in_dim(padded, at, n, 1).astype(F32)
        value = value.reshape(pairs, groups, px, n)
        sent = value.astype(BF16)
        kept = pick(value, y)
        for k in range(1, pairs):
            kept = kept + swap(pick(sent, y ^ k), "ch", k, 2).astype(F32)
        sent = kept.astype(BF16)
        total = kept[0]
        for k in range(1, groups):
            total = total + swap(sent[k], "img", k).astype(F32)
        done = total.astype(BF16)
        outs.append(done)
        fars.append(lax.ppermute(done, "section", [(0, 1)]))
    block = jnp.concatenate(outs, axis=-1)
    far_block = jnp.concatenate(fars, axis=-1)
    first = jnp.stack([mine_projected, far_projected])
    second = jnp.stack([far_block, block])
    final = jnp.where(sec == 0, first, second)
    return final.reshape(1, sections * per, orows, ocols, wide)


def solution(mesh):
    placed = (
        P("img", "ch", None, None),
        P(),
        P(),
        P(None, None, "img", None),
        P("img", None),
        P(),
        P(),
        P(None, None, ("img", "ch"), None),
    )
    return jax.shard_map(
        body,
        mesh=mesh,
        in_specs=placed,
        out_specs=P("section", "img", "ch", None, None),
        check_vma=False,
    )
```

```python
import functools

import jax
import jax.numpy as jnp
from jax import lax
from jax.experimental import pallas as pl
from jax.experimental.pallas import tpu as pltpu
from jax.sharding import PartitionSpec as P

LAYOUT = ("NHWC", "HWIO", "NHWC")
BF16 = jnp.bfloat16
F32 = jnp.float32


def conv(inputs, kernel, stride, padding):
    return lax.conv_general_dilated(
        inputs, kernel, (stride, stride), padding, dimension_numbers=LAYOUT, preferred_element_type=F32
    )


def swap(array, axis, k, unit=1):
    count = lax.axis_size(axis)
    return lax.ppermute(array, axis, [(i, i ^ (k * unit)) for i in range(count)])


def pick(stack, index):
    return lax.dynamic_index_in_dim(stack, index, 0, keepdims=False)


def whole(memory_space=pltpu.VMEM):
    return pl.BlockSpec(memory_space=memory_space)


def unfold_kernel(pairs, imgs, ocols, kd, ids, gain, shift, *refs):
    own, other = refs[:pairs], refs[pairs : 2 * pairs]
    out_own, out_other, centre, border, strip = refs[2 * pairs :]
    y, core = ids[0], ids[1]
    px = own[0].shape[1]
    first = core == 0
    base = 24

    def halves(value):
        normed = jax.nn.relu(value.astype(F32) * gain[...] + shift[...]).astype(BF16).astype(F32)
        low, high = normed[:, :kd], normed[:, kd:]
        return jnp.where(first, low, high), jnp.where(first, high, low)

    border[0] = jnp.zeros(border.shape[1:], F32)
    border[pairs + 1] = jnp.zeros(border.shape[1:], F32)
    for k in range(pairs):
        place = jnp.bitwise_xor(y, k)
        for i in range(imgs):
            for half, value in enumerate(halves(own[k][i])):
                centre[place, i, half] = value
            for half, value in enumerate(halves(other[k][i])):
                border[place + 1, i, half, 0] = value[:ocols]
                border[place + 1, i, half, 1] = value[px - ocols :]
    at = lax.broadcasted_iota(jnp.int32, (px, kd), 0) % ocols
    left, right = at == 0, at == ocols - 1
    shift_up = jnp.where(first, 0, 1)
    strip[...] = jnp.zeros(strip.shape, F32)
    for k in range(pairs):
        place = jnp.bitwise_xor(y, k)
        for half, out in enumerate((out_own, out_other)):
            for i in range(0, imgs, 2):
                for m in range(2):
                    strip[m, base : base + px] = centre[place, i + m, half]
                    strip[m, base - ocols : base] = border[place + shift_up, i + m, half, 1]
                    strip[m, base + px : base + px + ocols] = border[place + 1 + shift_up, i + m, half, 0]
                for tap in range(9):
                    dy, dx = tap // 3 - 1, tap % 3 - 1
                    off = base + dy * ocols + dx
                    values = [strip[m, off : off + px] for m in range(2)]
                    if dx == -1:
                        values = [jnp.where(left, 0.0, v) for v in values]
                    if dx == 1:
                        values = [jnp.where(right, 0.0, v) for v in values]
                    row = (k * imgs + i) * px
                    out[row : row + 2 * px, tap * kd : (tap + 1) * kd] = jnp.concatenate(values).astype(BF16)


def unfold(ids, gain, shift, own, other, ocols):
    pairs = len(own)
    imgs, px, kc = own[0].shape
    kd = kc // 2
    rows = pairs * imgs * px
    return pl.pallas_call(
        functools.partial(unfold_kernel, pairs, imgs, ocols, kd),
        out_shape=[jax.ShapeDtypeStruct((rows, 9 * kd), BF16)] * 2,
        in_specs=[whole(pltpu.SMEM)] + [whole()] * (2 + 2 * pairs),
        out_specs=[whole()] * 2,
        scratch_shapes=[
            pltpu.VMEM((pairs, imgs, 2, px, kd), F32),
            pltpu.VMEM((pairs + 2, imgs, 2, 2, ocols, kd), F32),
            pltpu.VMEM((2, 24 + px + 24, kd), F32),
        ],
        name="unfold",
        cost_estimate=pl.CostEstimate(flops=20 * rows * 9 * kd, bytes_accessed=8 * rows * 9 * kd, transcendentals=0),
    )(ids, gain, shift, *own, *other)


def mix_kernel(a_own, a_other, w_own, w_other, out):
    value = jnp.dot(a_own[...], w_own[...], preferred_element_type=F32)
    value = value + jnp.dot(a_other[...], w_other[...], preferred_element_type=F32)
    out[...] = value.astype(BF16)


def mix(a_own, a_other, w_own, w_other, first, count, step):
    rows, deep = a_own.shape
    weight = pl.BlockSpec((deep, step), lambda i: (0, first // step + i))
    return pl.pallas_call(
        mix_kernel,
        grid=(count // step,),
        out_shape=jax.ShapeDtypeStruct((rows, count), BF16),
        in_specs=[pl.BlockSpec((rows, deep), lambda i: (0, 0))] * 2 + [weight] * 2,
        out_specs=pl.BlockSpec((rows, step), lambda i: (0, i)),
        name="mix",
        cost_estimate=pl.CostEstimate(
            flops=4 * rows * deep * count,
            bytes_accessed=4 * (rows * deep + deep * count) + 2 * rows * count,
            transcendentals=0,
        ),
    )(a_own, a_other, w_own, w_other)


def sum_images(value, groups):
    k = 1
    while k < groups:
        sent = value.astype(BF16)
        value = value[0::2].astype(F32) + swap(sent[1::2], "img", k).astype(F32)
        k *= 2
    return value[0]


def sum_pairs(value, pairs):
    k = 1
    while k < pairs:
        sent = value.astype(BF16)
        value = value[0::2].astype(F32) + swap(sent[1::2], "ch", k, 2).astype(F32)
        k *= 2
    return value[0]


def cross(stack_of, index, count):
    return [pick(stack_of, index ^ i) for i in range(count)]


def body(pixels, first_gain, first_shift, first_kernel, projection, second_gain, second_shift, second_kernel):
    sec = lax.axis_index("section")
    z = lax.axis_index("img")
    ch = lax.axis_index("ch")
    sections = lax.axis_size("section")
    groups = lax.axis_size("img")
    shards = lax.axis_size("ch")
    pairs = shards // 2
    y, core = ch // 2, ch % 2
    per = pixels.shape[0] // sections
    _, rows, cols, depth = pixels.shape
    orows, ocols = rows // 2, cols // 2
    wide = second_gain.shape[0]
    slab = wide // groups
    kc = slab // pairs
    kd = kc // 2
    c1 = depth // groups

    other_kernel = swap(second_kernel, "ch", 1)
    part_rows = c1 // shards
    mine_rows = lax.dynamic_slice_in_dim(projection, ch * part_rows, part_rows, 0)
    proj_parts = mine_rows.reshape(part_rows, groups, slab).transpose(1, 0, 2)
    proj_rel = jnp.stack(
        [pick(proj_parts, z)] + [swap(pick(proj_parts, z ^ k), "img", k) for k in range(1, groups)]
    )
    proj_abs = jnp.stack(cross(proj_rel, z, groups))
    proj_pairs = jnp.stack([proj_abs] + [swap(proj_abs, "ch", k, 2) for k in range(1, pairs)])
    proj_pairs = jnp.stack(cross(proj_pairs, y, pairs), axis=1)
    proj_twin = swap(proj_pairs, "ch", 1)
    proj_cores = jnp.where(core == 0, jnp.stack([proj_pairs, proj_twin], 2), jnp.stack([proj_twin, proj_pairs], 2))
    proj_slab = proj_cores.reshape(depth, slab)

    own = lax.dynamic_slice_in_dim(pixels, sec * per, per, 0)
    above = lax.ppermute(own[:, -1:], "ch", [(i, i + 1) for i in range(shards - 1)])
    below = lax.ppermute(own[:, :1], "ch", [(i + 1, i) for i in range(shards - 1)])
    ext = jnp.concatenate([above, own, below], axis=1)
    normed = jax.nn.relu(ext.astype(F32) * first_gain + first_shift).astype(BF16)
    row = lax.broadcasted_iota(jnp.int32, (1, rows + 2, 1, 1), 1)
    dead = ((row == 0) & (ch == 0)) | ((row == rows + 1) & (ch == shards - 1))
    normed = jnp.where(dead, jnp.zeros((), BF16), normed)
    blocks = normed.reshape(per, rows + 2, cols, groups, c1).transpose(3, 0, 1, 2, 4)
    shape = blocks.shape[1:]
    size = per * (rows + 2) * cols * c1
    flat = blocks.reshape(groups, size // 128, 128) if size % 128 == 0 else blocks
    mine = [pick(flat, z)] + [swap(pick(flat, z ^ k), "img", k) for k in range(1, groups)]
    acts = jnp.stack(mine).reshape((groups * per,) + shape[1:])
    wide_acts = jnp.pad(acts.astype(F32), ((0, 0), (0, 0), (1, 1), (0, 0)))
    tall = wide_acts[:, 1:] + wide_acts[:, :-1]
    box = ((tall[:, :, 1:] + tall[:, :, :-1]) * 0.25).astype(BF16)
    part = conv(box, first_kernel, 2, ((0, 0), (0, 0)))
    part = part.reshape(groups, per * orows * ocols, depth)
    sent = part.astype(BF16)
    total = part[0]
    for k in range(1, groups):
        total = total + swap(sent[k], "img", k).astype(F32)
    mean = jnp.sum(
        own.astype(F32).reshape(per, orows, 2, ocols, 2, depth), axis=(2, 4)
    ) * 0.25
    pooled = (total + mean.reshape(total.shape)).astype(BF16)
    pooled_all = jnp.stack([pooled] + [swap(pooled, "img", k) for k in range(1, groups)])
    px = per * orows * ocols
    projected = jnp.dot(
        pooled_all.reshape(groups * px, depth), proj_slab, preferred_element_type=F32
    ).astype(BF16)

    back = projected.reshape(groups, px, slab)
    back_rel = jnp.stack([back[0]] + [swap(back[k], "img", k) for k in range(1, groups)])
    mine_projected = jnp.concatenate([pick(back_rel, z ^ i) for i in range(groups)], axis=1)
    far_projected = lax.ppermute(mine_projected, "section", [(1, 0)])

    imgs = groups * per
    out_px = orows * ocols
    by_pair = projected.reshape(groups * px, pairs, kc).transpose(1, 0, 2)
    chip = [pick(by_pair, y)]
    twin = [swap(chip[0], "ch", 1)]
    for k in range(1, pairs):
        chip.append(swap(pick(by_pair, y ^ k), "ch", k, 2))
        twin.append(swap(chip[k], "ch", 1))
    start = (z * pairs + y) * kc
    gain = lax.dynamic_slice_in_dim(second_gain, start, kc).reshape(1, kc)
    shift = lax.dynamic_slice_in_dim(second_shift, start, kc).reshape(1, kc)
    ids = jnp.stack([y, core]).astype(jnp.int32)
    a_own, a_other = unfold(
        ids,
        gain,
        shift,
        [c.reshape(imgs, out_px, kc) for c in chip],
        [c.reshape(imgs, out_px, kc) for c in twin],
        ocols,
    )
    w_own = second_kernel.reshape(9 * kd, wide)
    w_other = other_kernel.reshape(9 * kd, wide)

    chunks = 4 if wide % 1024 == 0 or wide % 512 == 0 else 2
    n = wide // chunks
    outs, fars = [], []
    for j in range(chunks):
        value = mix(a_own, a_other, w_own, w_other, j * n, n, n)
        value = value.reshape(pairs, groups, px, n)
        if j % 2 == 0:
            total = sum_images(sum_pairs(value, pairs), groups)
        else:
            total = sum_pairs(sum_images(value.swapaxes(0, 1), groups), pairs)
        done = (total + mine_projected[:, j * n : (j + 1) * n].astype(F32)).astype(BF16)
        outs.append(done)
        fars.append(lax.ppermute(done, "section", [(0, 1)]))
    block = jnp.concatenate(outs, axis=-1)
    far_block = jnp.concatenate(fars, axis=-1)
    first = jnp.stack([mine_projected, far_projected])
    second = jnp.stack([far_block, block])
    final = jnp.where(sec == 0, first, second)
    return final.reshape(1, sections * per, orows, ocols, wide)


def solution(mesh):
    placed = (
        P("img", "ch", None, None),
        P(),
        P(),
        P(None, None, "img", None),
        P("img", None),
        P(),
        P(),
        P(None, None, ("img", "ch"), None),
    )
    return jax.shard_map(
        body,
        mesh=mesh,
        in_specs=placed,
        out_specs=P("section", "img", "ch", None, None),
        check_vma=False,
    )
```

```python
import functools

import jax
import jax.numpy as jnp
from jax import lax
from jax.experimental import pallas as pl
from jax.experimental.pallas import tpu as pltpu
from jax.sharding import PartitionSpec as P

LAYOUT = ("NHWC", "HWIO", "NHWC")
BF16 = jnp.bfloat16
F32 = jnp.float32


def conv(inputs, kernel, stride, padding):
    return lax.conv_general_dilated(
        inputs, kernel, (stride, stride), padding, dimension_numbers=LAYOUT, preferred_element_type=F32
    )


def swap(array, axis, k, unit=1):
    count = lax.axis_size(axis)
    return lax.ppermute(array, axis, [(i, i ^ (k * unit)) for i in range(count)])


def pick(stack, index):
    return lax.dynamic_index_in_dim(stack, index, 0, keepdims=False)


def whole(memory_space=pltpu.VMEM):
    return pl.BlockSpec(memory_space=memory_space)


def unfold_kernel(pairs, imgs, ocols, kd, ids, gain, shift, *refs):
    own, other = refs[:pairs], refs[pairs : 2 * pairs]
    out_own, out_other, centre, border, strip = refs[2 * pairs :]
    y, core = ids[4], ids[5]
    px = own[0].shape[1]
    first = core == 0
    base = 24

    def halves(value):
        normed = jax.nn.relu(value.astype(F32) * gain[...] + shift[...]).astype(BF16).astype(F32)
        low, high = normed[:, :kd], normed[:, kd:]
        return jnp.where(first, low, high), jnp.where(first, high, low)

    border[0] = jnp.zeros(border.shape[1:], F32)
    border[pairs + 1] = jnp.zeros(border.shape[1:], F32)
    for k in range(pairs):
        place = jnp.bitwise_xor(y, k)
        for i in range(imgs):
            for half, value in enumerate(halves(own[k][i])):
                centre[place, i, half] = value
            for half, value in enumerate(halves(other[k][i])):
                border[place + 1, i, half, 0] = value[:ocols]
                border[place + 1, i, half, 1] = value[px - ocols :]
    at = lax.broadcasted_iota(jnp.int32, (px, kd), 0) % ocols
    left, right = at == 0, at == ocols - 1
    shift_up = jnp.where(first, 0, 1)
    strip[...] = jnp.zeros(strip.shape, F32)
    for k in range(pairs):
        place = jnp.bitwise_xor(y, k)
        for half, out in enumerate((out_own, out_other)):
            for i in range(0, imgs, 2):
                for m in range(2):
                    strip[m, base : base + px] = centre[place, i + m, half]
                    strip[m, base - ocols : base] = border[place + shift_up, i + m, half, 1]
                    strip[m, base + px : base + px + ocols] = border[place + 1 + shift_up, i + m, half, 0]
                for tap in range(9):
                    dy, dx = tap // 3 - 1, tap % 3 - 1
                    off = base + dy * ocols + dx
                    values = [strip[m, off : off + px] for m in range(2)]
                    if dx == -1:
                        values = [jnp.where(left, 0.0, v) for v in values]
                    if dx == 1:
                        values = [jnp.where(right, 0.0, v) for v in values]
                    row = (k * imgs + i) * px
                    out[row : row + 2 * px, tap * kd : (tap + 1) * kd] = jnp.concatenate(values).astype(BF16)


def unfold(ids, gain, shift, own, other, ocols):
    pairs = len(own)
    imgs, px, kc = own[0].shape
    kd = kc // 2
    rows = pairs * imgs * px
    lanes = -(-kd // 128) * 128
    need = 8 * pairs * imgs * px * lanes + 256 * (pairs + 2) * imgs * lanes
    need += 36 * rows * kd + 8 * pairs * imgs * px * lanes
    return pl.pallas_call(
        functools.partial(unfold_kernel, pairs, imgs, ocols, kd),
        out_shape=[jax.ShapeDtypeStruct((rows, 9 * kd), BF16)] * 2,
        in_specs=[whole(pltpu.SMEM)] + [whole()] * (2 + 2 * pairs),
        out_specs=[whole()] * 2,
        scratch_shapes=[
            pltpu.VMEM((pairs, imgs, 2, px, kd), F32),
            pltpu.VMEM((pairs + 2, imgs, 2, 2, ocols, kd), F32),
            pltpu.VMEM((2, 24 + px + 24, kd), F32),
        ],
        name="unfold",
        compiler_params=pltpu.CompilerParams(vmem_limit_bytes=min(60 << 20, (2 << 20) + 2 * need)),
        cost_estimate=pl.CostEstimate(flops=20 * rows * 9 * kd, bytes_accessed=8 * rows * 9 * kd, transcendentals=0),
    )(ids, gain, shift, *own, *other)


def mix_kernel(first, step, a_own, a_other, w_own, w_other, out):
    count = out.shape[1]
    for at in range(0, count, step):
        cut = slice(first + at, first + at + step)
        value = jnp.dot(a_own[...], w_own[:, cut], preferred_element_type=F32)
        value = value + jnp.dot(a_other[...], w_other[:, cut], preferred_element_type=F32)
        out[:, at : at + step] = value.astype(BF16)


def mix(a_own, a_other, w_own, w_other, first, count):
    rows, deep = a_own.shape
    return pl.pallas_call(
        functools.partial(mix_kernel, first, count),
        out_shape=jax.ShapeDtypeStruct((rows, count), BF16),
        in_specs=[whole()] * 4,
        out_specs=whole(),
        name="mix",
        compiler_params=pltpu.CompilerParams(vmem_limit_bytes=8 << 20),
        cost_estimate=pl.CostEstimate(
            flops=4 * rows * deep * count, bytes_accessed=2 * rows * count, transcendentals=0
        ),
    )(a_own, a_other, w_own, w_other)


def packing(rows, colp, c1):
    main = c1 // 128
    rest = c1 - main * 128
    fit = 128 // rest if rest else 1
    deep = -(-rows // fit) if rest else 0
    return main, rest, deep, main * rows * colp + deep * colp


def pack_kernel(groups, per, c1, colp, ids, pixels, above, below, gain, shift, *refs):
    outs, mean, held, pair = refs[:groups], refs[groups], refs[groups + 1], refs[groups + 2]
    sec, z, ch, last = ids[0], ids[1], ids[2], ids[3]
    _, rows, cols, depth = pixels.shape
    main, rest, deep, size = packing(rows + 2, colp, c1)
    scale, offset = gain[...], shift[...]
    filler = jnp.zeros((colp - cols, depth), F32)
    for p in range(per):
        for r in range(rows + 2):
            if r == 0:
                value = above[p, 0].astype(F32)
            elif r == rows + 1:
                value = below[p, 0].astype(F32)
            else:
                value = pixels[sec * per + p, r - 1].astype(F32)
            if 1 <= r <= rows:
                i, half = (r - 1) // 2, cols // 2
                for t in range(depth // 128):
                    lanes = slice(t * 128, (t + 1) * 128)
                    if r % 2 == 1:
                        pair[t] = value[:, lanes]
                    else:
                        pair[t] = pair[t] + value[:, lanes]
                        both = pair.at[t]
                        total = both[pl.ds(0, half, stride=2), :] + both[pl.ds(1, half, stride=2), :]
                        mean[p, i * half : (i + 1) * half, lanes] = total * 0.25
            value = jax.nn.relu(value * scale + offset)
            if r == 0:
                value = jnp.where(ch == 0, 0.0, value)
            if r == rows + 1:
                value = jnp.where(ch == last, 0.0, value)
            value = jnp.concatenate([value, filler]).astype(BF16)
            for g in range(groups):
                for m in range(main):
                    at = p * size + (m * (rows + 2) + r) * colp
                    lane = g * c1 + m * 128
                    held[g, at : at + colp, :] = value[:, lane : lane + 128]
                if rest:
                    at = p * size + main * (rows + 2) * colp + (r % deep) * colp
                    lane = g * c1 + main * 128
                    into = (r // deep) * rest
                    held[g, at : at + colp, into : into + rest] = value[:, lane : lane + rest]
    for k in range(groups):
        outs[k][...] = held[jnp.bitwise_xor(z, k)]


def pack(ids, pixels, above, below, gain, shift, groups, per, colp):
    _, rows, cols, depth = pixels.shape
    c1 = depth // groups
    size = packing(rows + 2, colp, c1)[3]
    block = jax.ShapeDtypeStruct((per * size, 128), BF16)
    half = jax.ShapeDtypeStruct((per, rows * cols // 4, depth), F32)
    return pl.pallas_call(
        functools.partial(pack_kernel, groups, per, c1, colp),
        out_shape=[block] * groups + [half],
        in_specs=[whole(pltpu.SMEM)] + [whole()] * 5,
        out_specs=[whole()] * (groups + 1),
        scratch_shapes=[pltpu.VMEM((groups, per * size, 128), BF16), pltpu.VMEM((depth // 128, cols, 128), F32)],
        name="pack",
        compiler_params=pltpu.CompilerParams(vmem_limit_bytes=8 << 20),
        cost_estimate=pl.CostEstimate(
            flops=4 * rows * cols * depth, bytes_accessed=6 * rows * cols * depth, transcendentals=0
        ),
    )(ids, pixels, above, below, gain, shift)


def stage_kernel(groups, per, rows, cols, colp, c1, *refs):
    blocks, kernel = refs[:groups], refs[groups]
    outs = refs[groups + 1 : 2 * groups + 1]
    flat, taps, squeezed = refs[2 * groups + 1 :]
    main, rest, deep, size = packing(rows + 2, colp, c1)
    tiles = main + (1 if rest else 0)
    orows, ocols = rows // 2, cols // 2
    base, wide = 8, (rows + 2) * colp
    half = colp // 2
    flat[...] = jnp.zeros(flat.shape, F32)
    for k in range(groups):
        for p in range(per):
            for t in range(tiles):
                lanes = 128 if t < main else rest
                if t < main:
                    at = p * size + t * wide
                    flat[t, base : base + wide, :] = blocks[k][at : at + wide, :].astype(F32)
                else:
                    for r in range(rows + 2):
                        at = p * size + main * wide + (r % deep) * colp
                        lane = (r // deep) * rest
                        flat[t, base + r * colp : base + (r + 1) * colp, 0:rest] = blocks[k][
                            at : at + colp, lane : lane + rest
                        ].astype(F32)
                span = (rows + 1) * colp + base + 8
                tall = flat[t, 0:span, :] + flat[t, colp : colp + span, :]
                flat[tiles, 0:span, :] = tall
                both = flat[tiles, 0 : span - 8, :] + flat[tiles, 1 : span - 7, :]
                flat[tiles + 1, 0 : span - 8, :] = both * 0.25
                plane = flat.at[tiles + 1]
                for tap in range(9):
                    ty, tx = tap // 3, tap % 3
                    for i in range(orows):
                        q = base + (2 * i + ty) * colp + tx - 1
                        value = plane[pl.ds(q, half, stride=2), :].astype(BF16)
                        row = ((k * per + p) * orows + i) * half
                        taps[tap, row : row + half, t * 128 : t * 128 + lanes] = value[:, :lanes]
    total = jnp.dot(taps[0], kernel[0], preferred_element_type=F32)
    for tap in range(1, 9):
        total = total + jnp.dot(taps[tap], kernel[tap], preferred_element_type=F32)
    for k in range(groups):
        for p in range(per):
            for i in range(orows):
                row = ((k * per + p) * orows + i) * half
                at = (p * orows + i) * ocols
                squeezed[at : at + ocols, :] = total[row : row + ocols]
        outs[k][...] = squeezed[...].astype(outs[k].dtype)


def stage(blocks, kernel, per, rows, cols, colp):
    groups = len(blocks)
    taps, c1, depth = kernel.shape
    tiles = -(-c1 // 128)
    px = per * rows * cols // 4
    count = groups * per * (rows // 2) * (colp // 2)
    return pl.pallas_call(
        functools.partial(stage_kernel, groups, per, rows, cols, colp, c1),
        out_shape=[jax.ShapeDtypeStruct((px, depth), F32)]
        + [jax.ShapeDtypeStruct((px, depth), BF16)] * (groups - 1),
        in_specs=[whole()] * (groups + 1),
        out_specs=[whole()] * groups,
        scratch_shapes=[
            pltpu.VMEM((tiles + 2, (rows + 3) * colp + 32, 128), F32),
            pltpu.VMEM((taps, count, c1), BF16),
            pltpu.VMEM((px, depth), F32),
        ],
        name="stage",
        compiler_params=pltpu.CompilerParams(vmem_limit_bytes=12 << 20),
        cost_estimate=pl.CostEstimate(
            flops=2 * count * taps * c1 * depth, bytes_accessed=4 * groups * px * depth, transcendentals=0
        ),
    )(*blocks, kernel)


def sum_images(value, groups):
    k = 1
    while k < groups:
        sent = value.astype(BF16)
        value = value[0::2].astype(F32) + swap(sent[1::2], "img", k).astype(F32)
        k *= 2
    return value[0]


def sum_pairs(value, pairs):
    k = 1
    while k < pairs:
        sent = value.astype(BF16)
        value = value[0::2].astype(F32) + swap(sent[1::2], "ch", k, 2).astype(F32)
        k *= 2
    return value[0]


def cross(stack_of, index, count):
    return [pick(stack_of, index ^ i) for i in range(count)]


def body(pixels, first_gain, first_shift, first_kernel, projection, second_gain, second_shift, second_kernel):
    sec = lax.axis_index("section")
    z = lax.axis_index("img")
    ch = lax.axis_index("ch")
    sections = lax.axis_size("section")
    groups = lax.axis_size("img")
    shards = lax.axis_size("ch")
    pairs = shards // 2
    y, core = ch // 2, ch % 2
    per = pixels.shape[0] // sections
    _, rows, cols, depth = pixels.shape
    orows, ocols = rows // 2, cols // 2
    wide = second_gain.shape[0]
    slab = wide // groups
    kc = slab // pairs
    kd = kc // 2
    c1 = depth // groups

    other_kernel = swap(second_kernel, "ch", 1)
    part_rows = c1 // shards
    mine_rows = lax.dynamic_slice_in_dim(projection, ch * part_rows, part_rows, 0)
    proj_parts = mine_rows.reshape(part_rows, groups, slab).transpose(1, 0, 2)
    proj_rel = jnp.stack(
        [pick(proj_parts, z)] + [swap(pick(proj_parts, z ^ k), "img", k) for k in range(1, groups)]
    )
    proj_abs = jnp.stack(cross(proj_rel, z, groups))
    proj_pairs = jnp.stack([proj_abs] + [swap(proj_abs, "ch", k, 2) for k in range(1, pairs)])
    proj_pairs = jnp.stack(cross(proj_pairs, y, pairs), axis=1)
    proj_twin = swap(proj_pairs, "ch", 1)
    proj_cores = jnp.where(core == 0, jnp.stack([proj_pairs, proj_twin], 2), jnp.stack([proj_twin, proj_pairs], 2))
    proj_slab = proj_cores.reshape(depth, slab)

    colp = -(-(cols + 2) // 16) * 16
    tails = lax.dynamic_slice_in_dim(pixels[:, -1:], sec * per, per, 0)
    heads = lax.dynamic_slice_in_dim(pixels[:, :1], sec * per, per, 0)
    above = lax.ppermute(tails, "ch", [(i, i + 1) for i in range(shards - 1)])
    below = lax.ppermute(heads, "ch", [(i + 1, i) for i in range(shards - 1)])
    ids = jnp.stack([sec, z, ch, jnp.int32(shards - 1), y, core]).astype(jnp.int32)
    *blocks, mean = pack(
        ids, pixels, above, below, first_gain.reshape(1, -1), first_shift.reshape(1, -1), groups, per, colp
    )
    got = [blocks[0]] + [swap(blocks[k], "img", k) for k in range(1, groups)]
    total, *sent = stage(got, first_kernel.reshape(9, c1, depth), per, rows, cols, colp)
    for k in range(1, groups):
        total = total + swap(sent[k - 1], "img", k).astype(F32)
    pooled = (total + mean.reshape(total.shape)).astype(BF16)
    pooled_all = jnp.stack([pooled] + [swap(pooled, "img", k) for k in range(1, groups)])
    px = per * orows * ocols
    projected = jnp.dot(
        pooled_all.reshape(groups * px, depth), proj_slab, preferred_element_type=F32
    ).astype(BF16)

    back = projected.reshape(groups, px, slab)
    back_rel = jnp.stack([back[0]] + [swap(back[k], "img", k) for k in range(1, groups)])
    mine_projected = jnp.concatenate([pick(back_rel, z ^ i) for i in range(groups)], axis=1)
    far_projected = lax.ppermute(mine_projected, "section", [(1, 0)])

    imgs = groups * per
    out_px = orows * ocols
    by_pair = projected.reshape(groups * px, pairs, kc).transpose(1, 0, 2)
    chip = [pick(by_pair, y)]
    twin = [swap(chip[0], "ch", 1)]
    for k in range(1, pairs):
        chip.append(swap(pick(by_pair, y ^ k), "ch", k, 2))
        twin.append(swap(chip[k], "ch", 1))
    start = (z * pairs + y) * kc
    gain = lax.dynamic_slice_in_dim(second_gain, start, kc).reshape(1, kc)
    shift = lax.dynamic_slice_in_dim(second_shift, start, kc).reshape(1, kc)
    a_own, a_other = unfold(
        ids,
        gain,
        shift,
        [c.reshape(imgs, out_px, kc) for c in chip],
        [c.reshape(imgs, out_px, kc) for c in twin],
        ocols,
    )
    w_own = second_kernel.reshape(9 * kd, wide)
    w_other = other_kernel.reshape(9 * kd, wide)

    unit = wide // 10
    outs, fars = [], []
    first = 0
    for j, n in enumerate((2 * unit, 3 * unit, 3 * unit, 2 * unit)):
        value = mix(a_own, a_other, w_own, w_other, first, n)
        value = value.reshape(pairs, groups, px, n)
        if j % 2 == 0:
            total = sum_images(sum_pairs(value, pairs), groups)
        else:
            total = sum_pairs(sum_images(value.swapaxes(0, 1), groups), pairs)
        done = (total + mine_projected[:, first : first + n].astype(F32)).astype(BF16)
        first += n
        outs.append(done)
        fars.append(lax.ppermute(done, "section", [(0, 1)]))
    block = jnp.concatenate(outs, axis=-1)
    far_block = jnp.concatenate(fars, axis=-1)
    first = jnp.stack([mine_projected, far_projected])
    second = jnp.stack([far_block, block])
    final = jnp.where(sec == 0, first, second)
    return final.reshape(1, sections * per, orows, ocols, wide)


def solution(mesh):
    placed = (
        P("img", "ch", None, None),
        P(),
        P(),
        P(None, None, "img", None),
        P("img", None),
        P(),
        P(),
        P(None, None, ("img", "ch"), None),
    )
    return jax.shard_map(
        body,
        mesh=mesh,
        in_specs=placed,
        out_specs=P("section", "img", "ch", None, None),
        check_vma=False,
    )
```

```python
import functools

import jax
import jax.numpy as jnp
from jax import lax
from jax.experimental import pallas as pl
from jax.experimental.pallas import tpu as pltpu
from jax.sharding import PartitionSpec as P


BF16 = jnp.bfloat16
F32 = jnp.float32


def swap(array, axis, k, unit=1):
    count = lax.axis_size(axis)
    return lax.ppermute(array, axis, [(i, i ^ (k * unit)) for i in range(count)])


def resident(array):
    return pltpu.with_memory_space_constraint(array, pltpu.VMEM)


def pick(stack, index):
    return lax.dynamic_index_in_dim(stack, index, 0, keepdims=False)


def whole(memory_space=pltpu.VMEM):
    return pl.BlockSpec(memory_space=memory_space)


def unfold_kernel(pairs, imgs, ocols, kd, ids, gains, shifts, *refs):
    own, other = refs[:pairs], refs[pairs : 2 * pairs]
    out_own, out_other, centre, border, strip = refs[2 * pairs :]
    y, core, group = ids[4], ids[5], ids[6]
    gain, shift = gains[pl.ds(group, 1), :], shifts[pl.ds(group, 1), :]
    px = own[0].shape[1]
    first = core == 0
    base = 24

    def halves(value):
        normed = jax.nn.relu(value.astype(F32) * gain + shift).astype(BF16).astype(F32)
        low, high = normed[:, :kd], normed[:, kd:]
        return jnp.where(first, low, high), jnp.where(first, high, low)

    border[0] = jnp.zeros(border.shape[1:], F32)
    border[pairs + 1] = jnp.zeros(border.shape[1:], F32)
    for k in range(pairs):
        place = jnp.bitwise_xor(y, k)
        for i in range(imgs):
            for half, value in enumerate(halves(own[k][i])):
                centre[place, i, half] = value
            for half, value in enumerate(halves(other[k][i])):
                border[place + 1, i, half, 0] = value[:ocols]
                border[place + 1, i, half, 1] = value[px - ocols :]
    at = lax.broadcasted_iota(jnp.int32, (px, kd), 0) % ocols
    left, right = at == 0, at == ocols - 1
    shift_up = jnp.where(first, 0, 1)
    strip[...] = jnp.zeros(strip.shape, F32)
    for k in range(pairs):
        place = jnp.bitwise_xor(y, k)
        for half, out in enumerate((out_own, out_other)):
            for i in range(0, imgs, 2):
                for m in range(2):
                    strip[m, base : base + px] = centre[place, i + m, half]
                    strip[m, base - ocols : base] = border[place + shift_up, i + m, half, 1]
                    strip[m, base + px : base + px + ocols] = border[place + 1 + shift_up, i + m, half, 0]
                for tap in range(9):
                    dy, dx = tap // 3 - 1, tap % 3 - 1
                    off = base + dy * ocols + dx
                    values = [strip[m, off : off + px] for m in range(2)]
                    if dx == -1:
                        values = [jnp.where(left, 0.0, v) for v in values]
                    if dx == 1:
                        values = [jnp.where(right, 0.0, v) for v in values]
                    row = (k * imgs + i) * px
                    out[row : row + 2 * px, tap * kd : (tap + 1) * kd] = jnp.concatenate(values).astype(BF16)


def unfold(ids, gain, shift, own, other, ocols):
    pairs = len(own)
    imgs, px, kc = own[0].shape
    kd = kc // 2
    rows = pairs * imgs * px
    lanes = -(-kd // 128) * 128
    need = 8 * pairs * imgs * px * lanes + 256 * (pairs + 2) * imgs * lanes
    need += 36 * rows * kd + 8 * pairs * imgs * px * lanes
    return pl.pallas_call(
        functools.partial(unfold_kernel, pairs, imgs, ocols, kd),
        out_shape=[pltpu.VMEM((rows, 9 * kd), BF16)] * 2,
        in_specs=[whole(pltpu.SMEM)] + [whole()] * (2 + 2 * pairs),
        out_specs=[whole()] * 2,
        scratch_shapes=[
            pltpu.VMEM((pairs, imgs, 2, px, kd), F32),
            pltpu.VMEM((pairs + 2, imgs, 2, 2, ocols, kd), F32),
            pltpu.VMEM((2, 24 + px + 24, kd), F32),
        ],
        name="unfold",
        compiler_params=pltpu.CompilerParams(vmem_limit_bytes=min(60 << 20, (2 << 20) + 2 * need)),
        cost_estimate=pl.CostEstimate(flops=20 * rows * 9 * kd, bytes_accessed=8 * rows * 9 * kd, transcendentals=0),
    )(ids, gain, shift, *own, *other)


def mix_kernel(first, step, a_own, a_other, w_own, w_other, out):
    count = out.shape[1]
    for at in range(0, count, step):
        cut = slice(first + at, first + at + step)
        value = jnp.dot(a_own[...], w_own[:, cut], preferred_element_type=F32)
        value = value + jnp.dot(a_other[...], w_other[:, cut], preferred_element_type=F32)
        out[:, at : at + step] = value.astype(BF16)


def mix(a_own, a_other, w_own, w_other, first, count):
    rows, deep = a_own.shape
    return pl.pallas_call(
        functools.partial(mix_kernel, first, count),
        out_shape=jax.ShapeDtypeStruct((rows, count), BF16),
        in_specs=[whole()] * 4,
        out_specs=whole(),
        name="mix",
        compiler_params=pltpu.CompilerParams(vmem_limit_bytes=8 << 20),
        cost_estimate=pl.CostEstimate(
            flops=4 * rows * deep * count, bytes_accessed=2 * rows * count, transcendentals=0
        ),
    )(a_own, a_other, w_own, w_other)


def packing(rows, colp, c1):
    main = c1 // 128
    rest = c1 - main * 128
    fit = 128 // rest if rest else 1
    deep = -(-rows // fit) if rest else 0
    return main, rest, deep, main * rows * colp + deep * colp


def pack_kernel(groups, per, c1, colp, ids, pixels, above, below, gain, shift, *refs):
    outs, mean, held, pair = refs[:groups], refs[groups], refs[groups + 1], refs[groups + 2]
    sec, z, ch, last = ids[0], ids[1], ids[2], ids[3]
    _, rows, cols, depth = pixels.shape
    main, rest, deep, size = packing(rows + 2, colp, c1)
    scale, offset = gain[...], shift[...]
    filler = jnp.zeros((colp - cols, depth), F32)
    for p in range(per):
        for r in range(rows + 2):
            if r == 0:
                value = above[p, 0].astype(F32)
            elif r == rows + 1:
                value = below[p, 0].astype(F32)
            else:
                value = pixels[sec * per + p, r - 1].astype(F32)
            if 1 <= r <= rows:
                i, half = (r - 1) // 2, cols // 2
                for t in range(depth // 128):
                    lanes = slice(t * 128, (t + 1) * 128)
                    if r % 2 == 1:
                        pair[t] = value[:, lanes]
                    else:
                        pair[t] = pair[t] + value[:, lanes]
                        both = pair.at[t]
                        total = both[pl.ds(0, half, stride=2), :] + both[pl.ds(1, half, stride=2), :]
                        mean[p, i * half : (i + 1) * half, lanes] = total * 0.25
            value = jax.nn.relu(value * scale + offset)
            if r == 0:
                value = jnp.where(ch == 0, 0.0, value)
            if r == rows + 1:
                value = jnp.where(ch == last, 0.0, value)
            value = jnp.concatenate([value, filler]).astype(BF16)
            for g in range(groups):
                for m in range(main):
                    at = p * size + (m * (rows + 2) + r) * colp
                    lane = g * c1 + m * 128
                    held[g, at : at + colp, :] = value[:, lane : lane + 128]
                if rest:
                    at = p * size + main * (rows + 2) * colp + (r % deep) * colp
                    lane = g * c1 + main * 128
                    into = (r // deep) * rest
                    held[g, at : at + colp, into : into + rest] = value[:, lane : lane + rest]
    for k in range(groups):
        outs[k][...] = held[jnp.bitwise_xor(z, k)]


def pack(ids, pixels, above, below, gain, shift, groups, per, colp):
    _, rows, cols, depth = pixels.shape
    c1 = depth // groups
    size = packing(rows + 2, colp, c1)[3]
    block = jax.ShapeDtypeStruct((per * size, 128), BF16)
    half = jax.ShapeDtypeStruct((per, rows * cols // 4, depth), F32)
    return pl.pallas_call(
        functools.partial(pack_kernel, groups, per, c1, colp),
        out_shape=[block] * groups + [half],
        in_specs=[whole(pltpu.SMEM)] + [whole()] * 5,
        out_specs=[whole()] * (groups + 1),
        scratch_shapes=[pltpu.VMEM((groups, per * size, 128), BF16), pltpu.VMEM((depth // 128, cols, 128), F32)],
        name="pack",
        compiler_params=pltpu.CompilerParams(vmem_limit_bytes=8 << 20),
        cost_estimate=pl.CostEstimate(
            flops=4 * rows * cols * depth, bytes_accessed=6 * rows * cols * depth, transcendentals=0
        ),
    )(ids, pixels, above, below, gain, shift)


def stage_kernel(groups, per, rows, cols, colp, c1, *refs):
    blocks, kernel = refs[:groups], refs[groups]
    outs = refs[groups + 1 : 2 * groups + 1]
    flat, taps, squeezed = refs[2 * groups + 1 :]
    main, rest, deep, size = packing(rows + 2, colp, c1)
    tiles = main + (1 if rest else 0)
    orows, ocols = rows // 2, cols // 2
    base, wide = 8, (rows + 2) * colp
    half = colp // 2
    flat[...] = jnp.zeros(flat.shape, F32)
    for k in range(groups):
        for p in range(per):
            for t in range(tiles):
                lanes = 128 if t < main else rest
                if t < main:
                    at = p * size + t * wide
                    flat[t, base : base + wide, :] = blocks[k][at : at + wide, :].astype(F32)
                else:
                    for r in range(rows + 2):
                        at = p * size + main * wide + (r % deep) * colp
                        lane = (r // deep) * rest
                        flat[t, base + r * colp : base + (r + 1) * colp, 0:rest] = blocks[k][
                            at : at + colp, lane : lane + rest
                        ].astype(F32)
                span = (rows + 1) * colp + base + 8
                tall = flat[t, 0:span, :] + flat[t, colp : colp + span, :]
                flat[tiles, 0:span, :] = tall
                both = flat[tiles, 0 : span - 8, :] + flat[tiles, 1 : span - 7, :]
                flat[tiles + 1, 0 : span - 8, :] = both * 0.25
                plane = flat.at[tiles + 1]
                for tap in range(9):
                    ty, tx = tap // 3, tap % 3
                    for i in range(orows):
                        q = base + (2 * i + ty) * colp + tx - 1
                        value = plane[pl.ds(q, half, stride=2), :].astype(BF16)
                        row = ((k * per + p) * orows + i) * half
                        taps[tap, row : row + half, t * 128 : t * 128 + lanes] = value[:, :lanes]
    total = jnp.dot(taps[0], kernel[0], preferred_element_type=F32)
    for tap in range(1, 9):
        total = total + jnp.dot(taps[tap], kernel[tap], preferred_element_type=F32)
    for k in range(groups):
        for p in range(per):
            for i in range(orows):
                row = ((k * per + p) * orows + i) * half
                at = (p * orows + i) * ocols
                squeezed[at : at + ocols, :] = total[row : row + ocols]
        outs[k][...] = squeezed[...].astype(outs[k].dtype)


def stage(blocks, kernel, per, rows, cols, colp):
    groups = len(blocks)
    taps, c1, depth = kernel.shape
    tiles = -(-c1 // 128)
    px = per * rows * cols // 4
    count = groups * per * (rows // 2) * (colp // 2)
    return pl.pallas_call(
        functools.partial(stage_kernel, groups, per, rows, cols, colp, c1),
        out_shape=[jax.ShapeDtypeStruct((px, depth), F32)]
        + [jax.ShapeDtypeStruct((px, depth), BF16)] * (groups - 1),
        in_specs=[whole()] * (groups + 1),
        out_specs=[whole()] * groups,
        scratch_shapes=[
            pltpu.VMEM((tiles + 2, (rows + 3) * colp + 32, 128), F32),
            pltpu.VMEM((taps, count, c1), BF16),
            pltpu.VMEM((px, depth), F32),
        ],
        name="stage",
        compiler_params=pltpu.CompilerParams(vmem_limit_bytes=12 << 20),
        cost_estimate=pl.CostEstimate(
            flops=2 * count * taps * c1 * depth, bytes_accessed=4 * groups * px * depth, transcendentals=0
        ),
    )(*blocks, kernel)


def sum_images(value, groups):
    k = 1
    while k < groups:
        sent = value.astype(BF16)
        value = value[0::2].astype(F32) + swap(sent[1::2], "img", k).astype(F32)
        k *= 2
    return value[0]


def sum_pairs(value, pairs):
    k = 1
    while k < pairs:
        sent = value.astype(BF16)
        value = value[0::2].astype(F32) + swap(sent[1::2], "ch", k, 2).astype(F32)
        k *= 2
    return value[0]


def cross(stack_of, index, count):
    return [pick(stack_of, index ^ i) for i in range(count)]


def body(pixels, first_gain, first_shift, first_kernel, projection, second_gain, second_shift, second_kernel):
    sec = lax.axis_index("section")
    z = lax.axis_index("img")
    ch = lax.axis_index("ch")
    sections = lax.axis_size("section")
    groups = lax.axis_size("img")
    shards = lax.axis_size("ch")
    pairs = shards // 2
    y, core = ch // 2, ch % 2
    per = pixels.shape[0] // sections
    _, rows, cols, depth = pixels.shape
    orows, ocols = rows // 2, cols // 2
    wide = second_gain.shape[0]
    slab = wide // groups
    kc = slab // pairs
    kd = kc // 2
    c1 = depth // groups

    other_kernel = swap(second_kernel, "ch", 1)

    colp = -(-(cols + 2) // 16) * 16
    tails = lax.dynamic_slice_in_dim(pixels[:, -1:], sec * per, per, 0)
    heads = lax.dynamic_slice_in_dim(pixels[:, :1], sec * per, per, 0)
    above = lax.ppermute(tails, "ch", [(i, i + 1) for i in range(shards - 1)])
    below = lax.ppermute(heads, "ch", [(i + 1, i) for i in range(shards - 1)])
    ids = jnp.stack([sec, z, ch, jnp.int32(shards - 1), y, core, z * pairs + y]).astype(jnp.int32)
    *blocks, mean = pack(
        ids, pixels, above, below, first_gain.reshape(1, -1), first_shift.reshape(1, -1), groups, per, colp
    )
    got = [blocks[0]] + [swap(blocks[k], "img", k) for k in range(1, groups)]

    part_rows = c1 // shards
    projection, mean = lax.optimization_barrier((projection, mean))
    mine_rows = lax.dynamic_slice_in_dim(projection, ch * part_rows, part_rows, 0)
    proj_parts = mine_rows.reshape(part_rows, groups, slab).transpose(1, 0, 2)
    proj_rel = [pick(proj_parts, z)] + [swap(pick(proj_parts, z ^ k), "img", k) for k in range(1, groups)]
    proj_abs = jnp.stack(cross(jnp.stack(proj_rel), z, groups))
    proj_pairs = [proj_abs] + [swap(proj_abs, "ch", k, 2) for k in range(1, pairs)]
    proj_pairs = jnp.stack(cross(jnp.stack(proj_pairs), y, pairs), axis=1)
    proj_twin = swap(proj_pairs, "ch", 1)
    proj_cores = jnp.where(core == 0, jnp.stack([proj_pairs, proj_twin], 2), jnp.stack([proj_twin, proj_pairs], 2))
    proj_slab = proj_cores.reshape(depth, slab)

    total, *sent = stage(got, first_kernel.reshape(9, c1, depth), per, rows, cols, colp)
    for k in range(1, groups):
        total = total + swap(sent[k - 1], "img", k).astype(F32)
    pooled = (total + mean.reshape(total.shape)).astype(BF16)
    pooled_all = jnp.stack([pooled] + [swap(pooled, "img", k) for k in range(1, groups)])
    px = per * orows * ocols
    projected = jnp.dot(
        pooled_all.reshape(groups * px, depth), proj_slab, preferred_element_type=F32
    ).astype(BF16)

    back = projected.reshape(groups, px, slab)
    back_rel = jnp.stack([back[0]] + [swap(back[k], "img", k) for k in range(1, groups)])
    mine_projected = jnp.concatenate([pick(back_rel, z ^ i) for i in range(groups)], axis=1)
    far_projected = lax.ppermute(mine_projected, "section", [(1, 0)])

    imgs = groups * per
    out_px = orows * ocols
    by_pair = projected.reshape(groups * px, pairs, kc).transpose(1, 0, 2)
    chip = [pick(by_pair, y)]
    chip += [swap(pick(by_pair, y ^ k), "ch", k, 2) for k in range(1, pairs)]
    twin = [swap(part, "ch", 1) for part in chip]
    a_own, a_other = unfold(
        ids,
        second_gain.reshape(groups * pairs, kc),
        second_shift.reshape(groups * pairs, kc),
        [c.reshape(imgs, out_px, kc) for c in chip],
        [c.reshape(imgs, out_px, kc) for c in twin],
        ocols,
    )
    w_own = resident(second_kernel.reshape(9 * kd, wide))
    w_other = resident(other_kernel.reshape(9 * kd, wide))

    unit = wide // 10
    outs, fars = [], []
    first = 0
    for j, n in enumerate((2 * unit, 3 * unit, 3 * unit, 2 * unit)):
        value = mix(a_own, a_other, w_own, w_other, first, n)
        value = value.reshape(pairs, groups, px, n)
        if j % 2 == 0:
            total = sum_pairs(value, pairs)
            total = sum_images(total, groups)
        else:
            total = sum_images(value.swapaxes(0, 1), groups)
            total = sum_pairs(total, pairs)
        done = (total + mine_projected[:, first : first + n].astype(F32)).astype(BF16)
        first += n
        outs.append(done)
        fars.append(lax.ppermute(done, "section", [(0, 1)]))
    block = jnp.concatenate(outs, axis=-1)
    far_block = jnp.concatenate(fars, axis=-1)
    first = jnp.stack([mine_projected, far_projected])
    second = jnp.stack([far_block, block])
    final = jnp.where(sec == 0, first, second)
    return final.reshape(1, sections * per, orows, ocols, wide)


def solution(mesh):
    placed = (
        P("img", "ch", None, None),
        P(),
        P(),
        P(None, None, "img", None),
        P("img", None),
        P(),
        P(),
        P(None, None, ("img", "ch"), None),
    )

    return jax.shard_map(
        body,
        mesh=mesh,
        in_specs=placed,
        out_specs=P("section", "img", "ch", None, None),
        check_vma=False,
    )
```

```python
import functools

import jax
import jax.numpy as jnp
from jax import lax
from jax.experimental import pallas as pl
from jax.experimental.pallas import tpu as pltpu
from jax.sharding import PartitionSpec as P


BF16 = jnp.bfloat16
F32 = jnp.float32


def swap(array, axis, k, unit=1):
    count = lax.axis_size(axis)
    return lax.ppermute(array, axis, [(i, i ^ (k * unit)) for i in range(count)])


def pick(stack, index):
    return lax.dynamic_index_in_dim(stack, index, 0, keepdims=False)


def whole(memory_space=pltpu.VMEM):
    return pl.BlockSpec(memory_space=memory_space)


def unfold_kernel(pairs, imgs, ocols, kd, ids, gains, shifts, *refs):
    own, other = refs[:pairs], refs[pairs : 2 * pairs]
    out_own, out_other, centre, border, strip = refs[2 * pairs :]
    y, core, group = ids[4], ids[5], ids[6]
    gain, shift = gains[pl.ds(group, 1), :], shifts[pl.ds(group, 1), :]
    px = own[0].shape[1]
    first = core == 0
    base = 24

    def halves(value):
        normed = jax.nn.relu(value.astype(F32) * gain + shift).astype(BF16).astype(F32)
        low, high = normed[:, :kd], normed[:, kd:]
        return jnp.where(first, low, high), jnp.where(first, high, low)

    border[0] = jnp.zeros(border.shape[1:], F32)
    border[pairs + 1] = jnp.zeros(border.shape[1:], F32)
    for k in range(pairs):
        place = jnp.bitwise_xor(y, k)
        for i in range(imgs):
            for half, value in enumerate(halves(own[k][i])):
                centre[place, i, half] = value
            for half, value in enumerate(halves(other[k][i])):
                border[place + 1, i, half, 0] = value[:ocols]
                border[place + 1, i, half, 1] = value[px - ocols :]
    at = lax.broadcasted_iota(jnp.int32, (px, kd), 0) % ocols
    left, right = at == 0, at == ocols - 1
    shift_up = jnp.where(first, 0, 1)
    strip[...] = jnp.zeros(strip.shape, F32)
    for k in range(pairs):
        place = jnp.bitwise_xor(y, k)
        for half, out in enumerate((out_own, out_other)):
            for i in range(0, imgs, 2):
                for m in range(2):
                    strip[m, base : base + px] = centre[place, i + m, half]
                    strip[m, base - ocols : base] = border[place + shift_up, i + m, half, 1]
                    strip[m, base + px : base + px + ocols] = border[place + 1 + shift_up, i + m, half, 0]
                for tap in range(9):
                    dy, dx = tap // 3 - 1, tap % 3 - 1
                    off = base + dy * ocols + dx
                    values = [strip[m, off : off + px] for m in range(2)]
                    if dx == -1:
                        values = [jnp.where(left, 0.0, v) for v in values]
                    if dx == 1:
                        values = [jnp.where(right, 0.0, v) for v in values]
                    row = (k * imgs + i) * px
                    out[row : row + 2 * px, tap * kd : (tap + 1) * kd] = jnp.concatenate(values).astype(BF16)


def unfold(ids, gain, shift, own, other, ocols):
    pairs = len(own)
    imgs, px, kc = own[0].shape
    kd = kc // 2
    rows = pairs * imgs * px
    lanes = -(-kd // 128) * 128
    need = 8 * pairs * imgs * px * lanes + 256 * (pairs + 2) * imgs * lanes
    need += 36 * rows * kd + 8 * pairs * imgs * px * lanes
    return pl.pallas_call(
        functools.partial(unfold_kernel, pairs, imgs, ocols, kd),
        out_shape=[pltpu.VMEM((rows, 9 * kd), BF16)] * 2,
        in_specs=[whole(pltpu.SMEM)] + [whole()] * (2 + 2 * pairs),
        out_specs=[whole()] * 2,
        scratch_shapes=[
            pltpu.VMEM((pairs, imgs, 2, px, kd), F32),
            pltpu.VMEM((pairs + 2, imgs, 2, 2, ocols, kd), F32),
            pltpu.VMEM((2, 24 + px + 24, kd), F32),
        ],
        name="unfold",
        compiler_params=pltpu.CompilerParams(vmem_limit_bytes=min(60 << 20, (2 << 20) + 2 * need)),
        cost_estimate=pl.CostEstimate(flops=20 * rows * 9 * kd, bytes_accessed=8 * rows * 9 * kd, transcendentals=0),
    )(ids, gain, shift, *own, *other)


def copy_rows(out, value, rows, px):
    for i, row in enumerate(rows):
        out[i * px : (i + 1) * px, :] = value[row * px : (row + 1) * px].astype(out.dtype)


def mix_kernel(rows, px, a_own, a_other, w_own, w_other, sent, kept):
    value = jnp.dot(a_own[...], w_own[...], preferred_element_type=F32)
    value = value + jnp.dot(a_other[...], w_other[...], preferred_element_type=F32)
    copy_rows(sent, value, rows[0], px)
    copy_rows(kept, value, rows[1], px)


def mix(a_own, a_other, w_own, w_other, first, count, step, rows, px):
    total, deep = a_own.shape
    weight = pl.BlockSpec((deep, step), lambda i: (0, first // step + i))
    sizes = [len(r) * px for r in rows]
    return pl.pallas_call(
        functools.partial(mix_kernel, rows, px),
        grid=(count // step,),
        out_shape=[
            jax.ShapeDtypeStruct((sizes[0], count), BF16),
            jax.ShapeDtypeStruct((sizes[1], count), F32),
        ],
        in_specs=[whole()] * 2 + [weight] * 2,
        out_specs=[pl.BlockSpec((size, step), lambda i: (0, i)) for size in sizes],
        name="mix",
        compiler_params=pltpu.CompilerParams(vmem_limit_bytes=16 << 20),
        cost_estimate=pl.CostEstimate(
            flops=4 * total * deep * count,
            bytes_accessed=4 * deep * count + 3 * total * count,
            transcendentals=0,
        ),
    )(a_own, a_other, w_own, w_other)


def merge_kernel(rows, px, kept, came, *outs):
    value = kept[...] + came[...].astype(F32)
    for out, some in zip(outs, rows):
        copy_rows(out, value, some, px)


def merge(kept, came, rows, px):
    count = kept.shape[1]
    return pl.pallas_call(
        functools.partial(merge_kernel, rows, px),
        out_shape=[jax.ShapeDtypeStruct((len(r) * px, count), t) for r, t in zip(rows, (BF16, F32))],
        in_specs=[whole()] * 2,
        out_specs=[whole()] * 2,
        name="merge",
        compiler_params=pltpu.CompilerParams(vmem_limit_bytes=10 << 20),
        cost_estimate=pl.CostEstimate(flops=kept.size, bytes_accessed=10 * kept.size, transcendentals=0),
    )(kept, came)


def finish_kernel(first, kept, came, extra, out):
    count = kept.shape[1]
    value = kept[...] + came[...].astype(F32) + extra[:, first : first + count].astype(F32)
    out[...] = value.astype(BF16)


def finish(kept, came, extra, first):
    return pl.pallas_call(
        functools.partial(finish_kernel, first),
        out_shape=jax.ShapeDtypeStruct(kept.shape, BF16),
        in_specs=[whole()] * 3,
        out_specs=whole(),
        name="finish",
        compiler_params=pltpu.CompilerParams(vmem_limit_bytes=6 << 20),
        cost_estimate=pl.CostEstimate(flops=2 * kept.size, bytes_accessed=10 * kept.size, transcendentals=0),
    )(kept, came, extra)


def join_kernel(*refs):
    for i, ref in enumerate(refs[:-1]):
        refs[-1][i] = ref[...]


def join(parts):
    return pl.pallas_call(
        join_kernel,
        out_shape=jax.ShapeDtypeStruct((len(parts),) + parts[0].shape, parts[0].dtype),
        in_specs=[whole()] * len(parts),
        out_specs=whole(),
        name="join",
        compiler_params=pltpu.CompilerParams(vmem_limit_bytes=6 << 20),
    )(*parts)


def project_kernel(groups, pairs, ids, *refs):
    pooled = refs[:groups]
    own, twin = refs[groups : groups + pairs], refs[groups + pairs : groups + 2 * pairs]
    backs = refs[groups + 2 * pairs : 2 * groups + 2 * pairs]
    parts = refs[2 * groups + 2 * pairs : 2 * groups + 3 * pairs]
    weight, held = refs[2 * groups + 3 * pairs :]
    z, y, core = ids[1], ids[4], ids[5]
    px, depth = pooled[0].shape
    for k in range(groups):
        for j in range(pairs):
            for half, source in enumerate((own, twin)):
                place = (jnp.bitwise_xor(z, k) * pairs + jnp.bitwise_xor(y, j)) * 2 + jnp.bitwise_xor(core, half)
                weight[place] = source[j][k].astype(F32)
    slab = weight[...].reshape(depth, weight.shape[2]).astype(BF16)
    kc = weight.shape[2] // pairs
    rows = jnp.concatenate([ref[...].astype(F32) for ref in pooled]).astype(BF16)
    value = jnp.dot(rows, slab, preferred_element_type=F32)
    for k in range(groups):
        backs[k][...] = value[k * px : (k + 1) * px].astype(BF16)
    for j in range(pairs):
        held[j] = value[:, j * kc : (j + 1) * kc].astype(BF16)
    for j in range(pairs):
        parts[j][...] = held[jnp.bitwise_xor(y, j)]


def project(ids, pooled, own, twin):
    groups, pairs = len(pooled), len(own)
    px, depth = pooled[0].shape
    _, deep, slab = own[0].shape
    kc = slab // pairs
    back = jax.ShapeDtypeStruct((px, slab), BF16)
    part = jax.ShapeDtypeStruct((groups * px, kc), BF16)
    return pl.pallas_call(
        functools.partial(project_kernel, groups, pairs),
        out_shape=[back] * groups + [part] * pairs,
        in_specs=[whole(pltpu.SMEM)] + [whole()] * (groups + 2 * pairs),
        out_specs=[whole()] * (groups + pairs),
        scratch_shapes=[
            pltpu.VMEM((groups * pairs * 2, deep, slab), F32),
            pltpu.VMEM((pairs, groups * px, kc), BF16),
        ],
        name="project",
        compiler_params=pltpu.CompilerParams(vmem_limit_bytes=14 << 20),
        cost_estimate=pl.CostEstimate(
            flops=2 * groups * px * depth * slab, bytes_accessed=4 * depth * slab, transcendentals=0
        ),
    )(ids, *pooled, *own, *twin)


def packing(rows, colp, c1):
    main = c1 // 128
    rest = c1 - main * 128
    fit = 128 // rest if rest else 1
    deep = -(-rows // fit) if rest else 0
    return main, rest, deep, main * rows * colp + deep * colp


def pack_kernel(groups, per, c1, colp, ids, pixels, above, below, gain, shift, projection, *refs):
    outs, mean = refs[:groups], refs[groups]
    cuts = refs[groups + 1 : 2 * groups + 1]
    held, pair, strip = refs[2 * groups + 1 :]
    sec, z, ch, last = ids[0], ids[1], ids[2], ids[3]
    _, rows, cols, depth = pixels.shape
    main, rest, deep, size = packing(rows + 2, colp, c1)
    scale, offset = gain[...], shift[...]
    filler = jnp.zeros((colp - cols, depth), F32)
    for p in range(per):
        for r in range(rows + 2):
            if r == 0:
                value = above[p, 0].astype(F32)
            elif r == rows + 1:
                value = below[p, 0].astype(F32)
            else:
                value = pixels[sec * per + p, r - 1].astype(F32)
            if 1 <= r <= rows:
                i, half = (r - 1) // 2, cols // 2
                for t in range(depth // 128):
                    lanes = slice(t * 128, (t + 1) * 128)
                    if r % 2 == 1:
                        pair[t] = value[:, lanes]
                    else:
                        pair[t] = pair[t] + value[:, lanes]
                        both = pair.at[t]
                        total = both[pl.ds(0, half, stride=2), :] + both[pl.ds(1, half, stride=2), :]
                        mean[p, i * half : (i + 1) * half, lanes] = total * 0.25
            value = jax.nn.relu(value * scale + offset)
            if r == 0:
                value = jnp.where(ch == 0, 0.0, value)
            if r == rows + 1:
                value = jnp.where(ch == last, 0.0, value)
            value = jnp.concatenate([value, filler]).astype(BF16)
            for g in range(groups):
                for m in range(main):
                    at = p * size + (m * (rows + 2) + r) * colp
                    lane = g * c1 + m * 128
                    held[g, at : at + colp, :] = value[:, lane : lane + 128]
                if rest:
                    at = p * size + main * (rows + 2) * colp + (r % deep) * colp
                    lane = g * c1 + main * 128
                    into = (r // deep) * rest
                    held[g, at : at + colp, into : into + rest] = value[:, lane : lane + rest]
    for k in range(groups):
        outs[k][...] = held[jnp.bitwise_xor(z, k)]
    deep, slab = cuts[0].shape
    for i in range(c1 // deep):
        for g in range(groups):
            strip[i, g] = projection[i * deep : (i + 1) * deep, g * slab : (g + 1) * slab].astype(F32)
    for k in range(groups):
        cuts[k][...] = strip[ch, jnp.bitwise_xor(z, k)].astype(BF16)


def pack(ids, pixels, above, below, gain, shift, projection, groups, shards, per, colp):
    _, rows, cols, depth = pixels.shape
    c1 = depth // groups
    size = packing(rows + 2, colp, c1)[3]
    block = jax.ShapeDtypeStruct((per * size, 128), BF16)
    half = jax.ShapeDtypeStruct((per, rows * cols // 4, depth), F32)
    deep, slab = c1 // shards, projection.shape[1] // groups
    cut = jax.ShapeDtypeStruct((deep, slab), BF16)
    return pl.pallas_call(
        functools.partial(pack_kernel, groups, per, c1, colp),
        out_shape=[block] * groups + [half] + [cut] * groups,
        in_specs=[whole(pltpu.SMEM)] + [whole()] * 6,
        out_specs=[whole()] * (2 * groups + 1),
        scratch_shapes=[
            pltpu.VMEM((groups, per * size, 128), BF16),
            pltpu.VMEM((depth // 128, cols, 128), F32),
            pltpu.VMEM((shards, groups, deep, slab), F32),
        ],
        name="pack",
        compiler_params=pltpu.CompilerParams(vmem_limit_bytes=14 << 20),
        cost_estimate=pl.CostEstimate(
            flops=4 * rows * cols * depth, bytes_accessed=6 * rows * cols * depth, transcendentals=0
        ),
    )(ids, pixels, above, below, gain, shift, projection)


def stage_kernel(groups, per, rows, cols, colp, c1, *refs):
    blocks, kernel = refs[:groups], refs[groups]
    outs = refs[groups + 1 : 2 * groups + 1]
    flat, taps, squeezed = refs[2 * groups + 1 :]
    main, rest, deep, size = packing(rows + 2, colp, c1)
    tiles = main + (1 if rest else 0)
    orows, ocols = rows // 2, cols // 2
    base, wide = 8, (rows + 2) * colp
    half = colp // 2
    flat[...] = jnp.zeros(flat.shape, F32)
    for k in range(groups):
        for p in range(per):
            for t in range(tiles):
                lanes = 128 if t < main else rest
                if t < main:
                    at = p * size + t * wide
                    flat[t, base : base + wide, :] = blocks[k][at : at + wide, :].astype(F32)
                else:
                    for r in range(rows + 2):
                        at = p * size + main * wide + (r % deep) * colp
                        lane = (r // deep) * rest
                        flat[t, base + r * colp : base + (r + 1) * colp, 0:rest] = blocks[k][
                            at : at + colp, lane : lane + rest
                        ].astype(F32)
                span = (rows + 1) * colp + base + 8
                tall = flat[t, 0:span, :] + flat[t, colp : colp + span, :]
                flat[tiles, 0:span, :] = tall
                both = flat[tiles, 0 : span - 8, :] + flat[tiles, 1 : span - 7, :]
                flat[tiles + 1, 0 : span - 8, :] = both * 0.25
                plane = flat.at[tiles + 1]
                for tap in range(9):
                    ty, tx = tap // 3, tap % 3
                    for i in range(orows):
                        q = base + (2 * i + ty) * colp + tx - 1
                        value = plane[pl.ds(q, half, stride=2), :].astype(BF16)
                        row = ((k * per + p) * orows + i) * half
                        taps[tap, row : row + half, t * 128 : t * 128 + lanes] = value[:, :lanes]
    total = jnp.dot(taps[0], kernel[0], preferred_element_type=F32)
    for tap in range(1, 9):
        total = total + jnp.dot(taps[tap], kernel[tap], preferred_element_type=F32)
    for k in range(groups):
        for p in range(per):
            for i in range(orows):
                row = ((k * per + p) * orows + i) * half
                at = (p * orows + i) * ocols
                squeezed[at : at + ocols, :] = total[row : row + ocols]
        outs[k][...] = squeezed[...].astype(outs[k].dtype)


def stage(blocks, kernel, per, rows, cols, colp):
    groups = len(blocks)
    taps, c1, depth = kernel.shape
    tiles = -(-c1 // 128)
    px = per * rows * cols // 4
    count = groups * per * (rows // 2) * (colp // 2)
    return pl.pallas_call(
        functools.partial(stage_kernel, groups, per, rows, cols, colp, c1),
        out_shape=[jax.ShapeDtypeStruct((px, depth), F32)]
        + [jax.ShapeDtypeStruct((px, depth), BF16)] * (groups - 1),
        in_specs=[whole()] * (groups + 1),
        out_specs=[whole()] * groups,
        scratch_shapes=[
            pltpu.VMEM((tiles + 2, (rows + 3) * colp + 32, 128), F32),
            pltpu.VMEM((taps, count, c1), BF16),
            pltpu.VMEM((px, depth), F32),
        ],
        name="stage",
        compiler_params=pltpu.CompilerParams(vmem_limit_bytes=12 << 20),
        cost_estimate=pl.CostEstimate(
            flops=2 * count * taps * c1 * depth, bytes_accessed=4 * groups * px * depth, transcendentals=0
        ),
    )(*blocks, kernel)


def body(pixels, first_gain, first_shift, first_kernel, projection, second_gain, second_shift, second_kernel):
    sec = lax.axis_index("section")
    z = lax.axis_index("img")
    ch = lax.axis_index("ch")
    sections = lax.axis_size("section")
    groups = lax.axis_size("img")
    shards = lax.axis_size("ch")
    pairs = shards // 2
    y, core = ch // 2, ch % 2
    per = pixels.shape[0] // sections
    _, rows, cols, depth = pixels.shape
    orows, ocols = rows // 2, cols // 2
    wide = second_gain.shape[0]
    slab = wide // groups
    kc = slab // pairs
    kd = kc // 2
    c1 = depth // groups

    other_kernel = swap(second_kernel, "ch", 1)

    colp = -(-(cols + 2) // 16) * 16
    tails = lax.dynamic_slice_in_dim(pixels[:, -1:], sec * per, per, 0)
    heads = lax.dynamic_slice_in_dim(pixels[:, :1], sec * per, per, 0)
    above = lax.ppermute(tails, "ch", [(i, i + 1) for i in range(shards - 1)])
    below = lax.ppermute(heads, "ch", [(i + 1, i) for i in range(shards - 1)])
    ids = jnp.stack([sec, z, ch, jnp.int32(shards - 1), y, core, z * pairs + y]).astype(jnp.int32)
    packed = pack(
        ids,
        pixels,
        above,
        below,
        first_gain.reshape(1, -1),
        first_shift.reshape(1, -1),
        projection,
        groups,
        shards,
        per,
        colp,
    )
    blocks, mean, cuts = packed[:groups], packed[groups], packed[groups + 1 :]
    got = [blocks[0]] + [swap(blocks[k], "img", k) for k in range(1, groups)]

    proj_z = join([cuts[0]] + [swap(cuts[k], "img", k) for k in range(1, groups)])
    proj_own = [proj_z] + [swap(proj_z, "ch", k, 2) for k in range(1, pairs)]
    proj_twin = [swap(part, "ch", 1) for part in proj_own]

    total, *sent = stage(got, first_kernel.reshape(9, c1, depth), per, rows, cols, colp)
    for k in range(1, groups):
        total = total + swap(sent[k - 1], "img", k).astype(F32)
    pooled = (total + mean.reshape(total.shape)).astype(BF16)
    pooled_all = [pooled] + [swap(pooled, "img", k) for k in range(1, groups)]
    px = per * orows * ocols
    imgs = groups * per
    out_px = orows * ocols
    made = project(ids, pooled_all, proj_own, proj_twin)
    back, chip = made[:groups], made[groups:]

    chip = [chip[0]] + [swap(chip[k], "ch", k, 2) for k in range(1, pairs)]
    twin = [swap(part, "ch", 1) for part in chip]
    back = [back[0]] + [swap(back[k], "img", k) for k in range(1, groups)]
    a_own, a_other = unfold(
        ids,
        second_gain.reshape(groups * pairs, kc),
        second_shift.reshape(groups * pairs, kc),
        [c.reshape(imgs, out_px, kc) for c in chip],
        [c.reshape(imgs, out_px, kc) for c in twin],
        ocols,
    )
    w_own = second_kernel.reshape(9 * kd, wide)
    w_other = other_kernel.reshape(9 * kd, wide)

    unit = wide // 10
    plan = ((0, 2), (1, 3), (0, 3), (1, 2))
    names = [("ch", 1 << i, 2) for i in range(pairs.bit_length() - 1)]
    names_z = [("img", 1 << i, 1) for i in range(groups.bit_length() - 1)]
    values, first = [], 0
    for kind, n in plan:
        hops = names_z + names if kind else names + names_z
        keys = [(a, b) for a in range(pairs) for b in range(groups)]

        def split(keys, hop):
            axis, k, _ = hop
            bit = [key[0] & k if axis == "ch" else key[1] & k for key in keys]
            rows = ([i for i, x in enumerate(bit) if x], [i for i, x in enumerate(bit) if not x])
            return rows, [key for key, x in zip(keys, bit) if not x]

        rows, keys = split(keys, hops[0])
        sent, kept = mix(a_own, a_other, w_own, w_other, first, n * unit, unit, rows, px)
        for h, hop in enumerate(hops):
            axis, k, size = hop
            came = swap(sent, axis, k, size)
            if h + 1 < len(hops):
                rows, keys = split(keys, hops[h + 1])
                sent, kept = merge(kept, came, rows, px)
        values.append((kept, came, first, n * unit))
        first += n * unit

    back_rel = join(back)
    mine_projected = jnp.concatenate([pick(back_rel, z ^ i) for i in range(groups)], axis=1)
    far_projected = lax.ppermute(mine_projected, "section", [(1, 0)])
    outs, fars = [], []
    for j, (kept, came, first, n) in enumerate(values):
        outs.append(finish(kept, came, mine_projected, first))
        fars.append(lax.ppermute(outs[j], "section", [(0, 1)]))
    block = jnp.concatenate(outs, axis=-1)
    far_block = jnp.concatenate(fars, axis=-1)
    first = jnp.stack([mine_projected, far_projected])
    second = jnp.stack([far_block, block])
    final = jnp.where(sec == 0, first, second)
    return final.reshape(1, sections * per, orows, ocols, wide)


def solution(mesh):
    placed = (
        P("img", "ch", None, None),
        P(),
        P(),
        P(None, None, "img", None),
        P("img", None),
        P(),
        P(),
        P(None, None, ("img", "ch"), None),
    )

    return jax.shard_map(
        body,
        mesh=mesh,
        in_specs=placed,
        out_specs=P("section", "img", "ch", None, None),
        check_vma=False,
    )
```

```python
import functools

import jax
import jax.numpy as jnp
from jax import lax
from jax.experimental import pallas as pl
from jax.experimental.pallas import tpu as pltpu
from jax.sharding import PartitionSpec as P


BF16 = jnp.bfloat16
F32 = jnp.float32


def swap(array, axis, k, unit=1):
    count = lax.axis_size(axis)
    return lax.ppermute(array, axis, [(i, i ^ (k * unit)) for i in range(count)])


def streamed(array):
    return pltpu.with_memory_space_constraint(array, pltpu.HBM)


def whole(memory_space=pltpu.VMEM):
    return pl.BlockSpec(memory_space=memory_space)


def unfold_kernel(pairs, imgs, ocols, kd, ids, gains, shifts, *refs):
    own, other = refs[:pairs], refs[pairs : 2 * pairs]
    out_own, out_other, centre, border, strip = refs[2 * pairs :]
    y, core, group = ids[4], ids[5], ids[6]
    gain, shift = gains[pl.ds(group, 1), :], shifts[pl.ds(group, 1), :]
    px = own[0].shape[1]
    first = core == 0
    base = 24

    def halves(value):
        normed = jax.nn.relu(value.astype(F32) * gain + shift).astype(BF16).astype(F32)
        low, high = normed[:, :kd], normed[:, kd:]
        return jnp.where(first, low, high), jnp.where(first, high, low)

    border[0] = jnp.zeros(border.shape[1:], F32)
    border[pairs + 1] = jnp.zeros(border.shape[1:], F32)
    for k in range(pairs):
        place = jnp.bitwise_xor(y, k)
        for i in range(imgs):
            for half, value in enumerate(halves(own[k][i])):
                centre[place, i, half] = value
            for half, value in enumerate(halves(other[k][i])):
                border[place + 1, i, half, 0] = value[:ocols]
                border[place + 1, i, half, 1] = value[px - ocols :]
    at = lax.broadcasted_iota(jnp.int32, (px, kd), 0) % ocols
    left, right = at == 0, at == ocols - 1
    shift_up = jnp.where(first, 0, 1)
    strip[...] = jnp.zeros(strip.shape, F32)
    for k in range(pairs):
        place = jnp.bitwise_xor(y, k)
        for half, out in enumerate((out_own, out_other)):
            for i in range(0, imgs, 2):
                for m in range(2):
                    strip[m, base : base + px] = centre[place, i + m, half]
                    strip[m, base - ocols : base] = border[place + shift_up, i + m, half, 1]
                    strip[m, base + px : base + px + ocols] = border[place + 1 + shift_up, i + m, half, 0]
                for tap in range(9):
                    dy, dx = tap // 3 - 1, tap % 3 - 1
                    off = base + dy * ocols + dx
                    values = [strip[m, off : off + px] for m in range(2)]
                    if dx == -1:
                        values = [jnp.where(left, 0.0, v) for v in values]
                    if dx == 1:
                        values = [jnp.where(right, 0.0, v) for v in values]
                    row = (k * imgs + i) * px
                    out[row : row + 2 * px, tap * kd : (tap + 1) * kd] = jnp.concatenate(values).astype(BF16)


def unfold(ids, gain, shift, own, other, ocols):
    pairs = len(own)
    imgs, px, kc = own[0].shape
    kd = kc // 2
    rows = pairs * imgs * px
    lanes = -(-kd // 128) * 128
    need = 8 * pairs * imgs * px * lanes + 256 * (pairs + 2) * imgs * lanes
    need += 36 * rows * kd + 8 * pairs * imgs * px * lanes
    return pl.pallas_call(
        functools.partial(unfold_kernel, pairs, imgs, ocols, kd),
        out_shape=[pltpu.VMEM((rows, 9 * kd), BF16)] * 2,
        in_specs=[whole(pltpu.SMEM)] + [whole()] * (2 + 2 * pairs),
        out_specs=[whole()] * 2,
        scratch_shapes=[
            pltpu.VMEM((pairs, imgs, 2, px, kd), F32),
            pltpu.VMEM((pairs + 2, imgs, 2, 2, ocols, kd), F32),
            pltpu.VMEM((2, 24 + px + 24, kd), F32),
        ],
        name="unfold",
        compiler_params=pltpu.CompilerParams(vmem_limit_bytes=min(60 << 20, (2 << 20) + 2 * need)),
        cost_estimate=pl.CostEstimate(flops=20 * rows * 9 * kd, bytes_accessed=8 * rows * 9 * kd, transcendentals=0),
    )(ids, gain, shift, *own, *other)


def copy_rows(out, value, rows, px):
    for i, row in enumerate(rows):
        out[i * px : (i + 1) * px, :] = value[row * px : (row + 1) * px].astype(out.dtype)


def mix_kernel(rows, px, a_own, a_other, w_own, w_other, sent, kept):
    value = jnp.dot(a_own[...], w_own[...], preferred_element_type=F32)
    value = value + jnp.dot(a_other[...], w_other[...], preferred_element_type=F32)
    copy_rows(sent, value, rows[0], px)
    copy_rows(kept, value, rows[1], px)


def mix(a_own, a_other, w_own, w_other, first, count, step, rows, px):
    total, deep = a_own.shape
    weight = pl.BlockSpec((deep, step), lambda i: (0, first // step + i))
    sizes = [len(r) * px for r in rows]
    return pl.pallas_call(
        functools.partial(mix_kernel, rows, px),
        grid=(count // step,),
        out_shape=[
            jax.ShapeDtypeStruct((sizes[0], count), BF16),
            jax.ShapeDtypeStruct((sizes[1], count), F32),
        ],
        in_specs=[whole()] * 2 + [weight] * 2,
        out_specs=[pl.BlockSpec((size, step), lambda i: (0, i)) for size in sizes],
        name="mix",
        compiler_params=pltpu.CompilerParams(vmem_limit_bytes=16 << 20),
        cost_estimate=pl.CostEstimate(
            flops=4 * total * deep * count,
            bytes_accessed=4 * deep * count + 3 * total * count,
            transcendentals=0,
        ),
    )(a_own, a_other, w_own, w_other)


def merge_kernel(rows, px, kept, came, *outs):
    value = kept[...] + came[...].astype(F32)
    for out, some in zip(outs, rows):
        copy_rows(out, value, some, px)


def merge(kept, came, rows, px):
    count = kept.shape[1]
    return pl.pallas_call(
        functools.partial(merge_kernel, rows, px),
        out_shape=[jax.ShapeDtypeStruct((len(r) * px, count), t) for r, t in zip(rows, (BF16, F32))],
        in_specs=[whole()] * 2,
        out_specs=[whole()] * 2,
        name="merge",
        compiler_params=pltpu.CompilerParams(vmem_limit_bytes=10 << 20),
        cost_estimate=pl.CostEstimate(flops=kept.size, bytes_accessed=10 * kept.size, transcendentals=0),
    )(kept, came)


def finish_kernel(first, count, *refs):
    extra, out = refs[2 * count :]
    at = 0
    for i in range(count):
        kept, came = refs[2 * i : 2 * i + 2]
        n = kept.shape[1]
        value = kept[...] + came[...].astype(F32) + extra[:, first + at : first + at + n].astype(F32)
        out[:, at : at + n] = value.astype(BF16)
        at += n


def finish(parts, extra, first):
    flat = [array for part in parts for array in part]
    px = flat[0].shape[0]
    wide = sum(part[0].shape[1] for part in parts)
    return pl.pallas_call(
        functools.partial(finish_kernel, first, len(parts)),
        out_shape=jax.ShapeDtypeStruct((px, wide), BF16),
        in_specs=[whole()] * (2 * len(parts) + 1),
        out_specs=whole(),
        name="finish",
        compiler_params=pltpu.CompilerParams(vmem_limit_bytes=6 << 20),
        cost_estimate=pl.CostEstimate(flops=2 * px * wide, bytes_accessed=10 * px * wide, transcendentals=0),
    )(*flat, extra)


def join_kernel(*refs):
    for i, ref in enumerate(refs[:-1]):
        refs[-1][i] = ref[...]


def join(parts):
    return pl.pallas_call(
        join_kernel,
        out_shape=jax.ShapeDtypeStruct((len(parts),) + parts[0].shape, parts[0].dtype),
        in_specs=[whole()] * len(parts),
        out_specs=whole(),
        name="join",
        compiler_params=pltpu.CompilerParams(vmem_limit_bytes=6 << 20),
    )(*parts)


def project_kernel(groups, pairs, ids, *refs):
    pooled = refs[:groups]
    own, twin = refs[groups : groups + pairs], refs[groups + pairs : groups + 2 * pairs]
    backs = refs[groups + 2 * pairs : 2 * groups + 2 * pairs]
    parts = refs[2 * groups + 2 * pairs : 2 * groups + 3 * pairs]
    weight, held = refs[2 * groups + 3 * pairs :]
    z, y, core = ids[1], ids[4], ids[5]
    px, depth = pooled[0].shape
    for k in range(groups):
        for j in range(pairs):
            for half, source in enumerate((own, twin)):
                place = (jnp.bitwise_xor(z, k) * pairs + jnp.bitwise_xor(y, j)) * 2 + jnp.bitwise_xor(core, half)
                weight[place] = source[j][k].astype(F32)
    slab = weight[...].reshape(depth, weight.shape[2]).astype(BF16)
    kc = weight.shape[2] // pairs
    rows = jnp.concatenate([ref[...].astype(F32) for ref in pooled]).astype(BF16)
    value = jnp.dot(rows, slab, preferred_element_type=F32)
    for k in range(groups):
        backs[k][...] = value[k * px : (k + 1) * px].astype(BF16)
    for j in range(pairs):
        held[j] = value[:, j * kc : (j + 1) * kc].astype(BF16)
    for j in range(pairs):
        parts[j][...] = held[jnp.bitwise_xor(y, j)]


def project(ids, pooled, own, twin):
    groups, pairs = len(pooled), len(own)
    px, depth = pooled[0].shape
    _, deep, slab = own[0].shape
    kc = slab // pairs
    back = jax.ShapeDtypeStruct((px, slab), BF16)
    part = jax.ShapeDtypeStruct((groups * px, kc), BF16)
    return pl.pallas_call(
        functools.partial(project_kernel, groups, pairs),
        out_shape=[back] * groups + [part] * pairs,
        in_specs=[whole(pltpu.SMEM)] + [whole()] * (groups + 2 * pairs),
        out_specs=[whole()] * (groups + pairs),
        scratch_shapes=[
            pltpu.VMEM((groups * pairs * 2, deep, slab), F32),
            pltpu.VMEM((pairs, groups * px, kc), BF16),
        ],
        name="project",
        compiler_params=pltpu.CompilerParams(vmem_limit_bytes=14 << 20),
        cost_estimate=pl.CostEstimate(
            flops=2 * groups * px * depth * slab, bytes_accessed=4 * depth * slab, transcendentals=0
        ),
    )(ids, *pooled, *own, *twin)


def packing(rows, colp, c1):
    main = c1 // 128
    rest = c1 - main * 128
    fit = 128 // rest if rest else 1
    deep = -(-rows // fit) if rest else 0
    return main, rest, deep, main * rows * colp + deep * colp


def cut_kernel(ids, projection, *refs):
    cuts, strip = refs[:-1], refs[-1]
    z, ch = ids[1], ids[2]
    deep, slab = cuts[0].shape
    groups = len(cuts)
    for i in range(projection.shape[0] // deep):
        for g in range(groups):
            strip[i, g] = projection[i * deep : (i + 1) * deep, g * slab : (g + 1) * slab].astype(F32)
    for k in range(groups):
        cuts[k][...] = strip[ch, jnp.bitwise_xor(z, k)].astype(BF16)


def cut(ids, projection, groups, shards):
    deep, slab = projection.shape[0] // shards, projection.shape[1] // groups
    return pl.pallas_call(
        cut_kernel,
        out_shape=[jax.ShapeDtypeStruct((deep, slab), BF16)] * groups,
        in_specs=[whole(pltpu.SMEM), whole()],
        out_specs=[whole()] * groups,
        scratch_shapes=[pltpu.VMEM((shards, groups, deep, slab), F32)],
        name="cut",
        compiler_params=pltpu.CompilerParams(vmem_limit_bytes=8 << 20),
    )(ids, projection)


def spread_kernel(groups, ids, *refs):
    backs, out, held = refs[:groups], refs[groups], refs[groups + 1]
    slab = backs[0].shape[1]
    for k in range(groups):
        held[jnp.bitwise_xor(ids[1], k)] = backs[k][...]
    for g in range(groups):
        out[:, g * slab : (g + 1) * slab] = held[g]


def spread(ids, backs):
    px, slab = backs[0].shape
    groups = len(backs)
    return pl.pallas_call(
        functools.partial(spread_kernel, groups),
        out_shape=jax.ShapeDtypeStruct((px, groups * slab), BF16),
        in_specs=[whole(pltpu.SMEM)] + [whole()] * groups,
        out_specs=whole(),
        scratch_shapes=[pltpu.VMEM((groups, px, slab), BF16)],
        name="spread",
        compiler_params=pltpu.CompilerParams(vmem_limit_bytes=6 << 20),
    )(ids, *backs)


def final_kernel(parts, per, orows, ocols, ids, mine, far_mine, *refs):
    own, far = refs[:parts], refs[parts : 2 * parts]
    out, held = refs[2 * parts :]
    first = ids[0] == 0
    for half in range(2):
        at = 0
        for i in range(parts):
            count = own[i].shape[1]
            for lane in range(0, count, 128):
                here = slice(lane, lane + 128)
                there = slice(at + lane, at + lane + 128)
                a = mine[:, there] if half == 0 else far_mine[:, there]
                b = far[i][:, here] if half == 0 else own[i][:, here]
                held[...] = jnp.where(first, a.astype(F32), b.astype(F32))
                for p in range(per):
                    for c in range(ocols):
                        some = held[pl.ds(p * orows * ocols + c, orows, stride=ocols), :]
                        out[half * per + p, c, :, there] = some.astype(BF16)
            at += count


def final(ids, mine, far_mine, own, far, per, orows, ocols):
    wide = mine.shape[1]
    return pl.pallas_call(
        functools.partial(final_kernel, len(own), per, orows, ocols),
        out_shape=jax.ShapeDtypeStruct((2 * per, ocols, orows, wide), BF16),
        in_specs=[whole(pltpu.SMEM)] + [whole()] * (2 + 2 * len(own)),
        out_specs=whole(),
        scratch_shapes=[pltpu.VMEM((mine.shape[0], 128), F32)],
        name="final",
        compiler_params=pltpu.CompilerParams(vmem_limit_bytes=10 << 20),
    )(ids, mine, far_mine, *own, *far)


def pack_kernel(groups, per, c1, colp, ids, pixels, above, below, gain, shift, *refs):
    outs, mean = refs[:groups], refs[groups]
    held, pair = refs[groups + 1 :]
    sec, z, ch, last = ids[0], ids[1], ids[2], ids[3]
    _, rows, cols, depth = pixels.shape
    main, rest, deep, size = packing(rows + 2, colp, c1)
    scale, offset = gain[...], shift[...]
    filler = jnp.zeros((colp - cols, depth), F32)
    for p in range(per):
        for r in range(rows + 2):
            if r == 0:
                value = above[p, 0].astype(F32)
            elif r == rows + 1:
                value = below[p, 0].astype(F32)
            else:
                value = pixels[sec * per + p, r - 1].astype(F32)
            if 1 <= r <= rows:
                i, half = (r - 1) // 2, cols // 2
                for t in range(depth // 128):
                    lanes = slice(t * 128, (t + 1) * 128)
                    if r % 2 == 1:
                        pair[t] = value[:, lanes]
                    else:
                        pair[t] = pair[t] + value[:, lanes]
                        both = pair.at[t]
                        total = both[pl.ds(0, half, stride=2), :] + both[pl.ds(1, half, stride=2), :]
                        mean[p, i * half : (i + 1) * half, lanes] = total * 0.25
            value = jax.nn.relu(value * scale + offset)
            if r == 0:
                value = jnp.where(ch == 0, 0.0, value)
            if r == rows + 1:
                value = jnp.where(ch == last, 0.0, value)
            value = jnp.concatenate([value, filler]).astype(BF16)
            for g in range(groups):
                for m in range(main):
                    at = p * size + (m * (rows + 2) + r) * colp
                    lane = g * c1 + m * 128
                    held[g, at : at + colp, :] = value[:, lane : lane + 128]
                if rest:
                    at = p * size + main * (rows + 2) * colp + (r % deep) * colp
                    lane = g * c1 + main * 128
                    into = (r // deep) * rest
                    held[g, at : at + colp, into : into + rest] = value[:, lane : lane + rest]
    for k in range(groups):
        outs[k][...] = held[jnp.bitwise_xor(z, k)]


def pack(ids, pixels, above, below, gain, shift, groups, per, colp):
    _, rows, cols, depth = pixels.shape
    c1 = depth // groups
    size = packing(rows + 2, colp, c1)[3]
    block = jax.ShapeDtypeStruct((per * size, 128), BF16)
    half = jax.ShapeDtypeStruct((per, rows * cols // 4, depth), F32)
    return pl.pallas_call(
        functools.partial(pack_kernel, groups, per, c1, colp),
        out_shape=[block] * groups + [half],
        in_specs=[whole(pltpu.SMEM)] + [whole()] * 5,
        out_specs=[whole()] * (groups + 1),
        scratch_shapes=[
            pltpu.VMEM((groups, per * size, 128), BF16),
            pltpu.VMEM((depth // 128, cols, 128), F32),
        ],
        name="pack",
        compiler_params=pltpu.CompilerParams(vmem_limit_bytes=14 << 20),
        cost_estimate=pl.CostEstimate(
            flops=4 * rows * cols * depth, bytes_accessed=6 * rows * cols * depth, transcendentals=0
        ),
    )(ids, pixels, above, below, gain, shift)


def stage_kernel(groups, per, rows, cols, colp, c1, *refs):
    blocks, kernel = refs[:groups], refs[groups]
    outs = refs[groups + 1 : 2 * groups + 1]
    flat, taps, squeezed = refs[2 * groups + 1 :]
    main, rest, deep, size = packing(rows + 2, colp, c1)
    tiles = main + (1 if rest else 0)
    orows, ocols = rows // 2, cols // 2
    base, wide = 8, (rows + 2) * colp
    half = colp // 2
    flat[...] = jnp.zeros(flat.shape, F32)
    for k in range(groups):
        for p in range(per):
            for t in range(tiles):
                lanes = 128 if t < main else rest
                if t < main:
                    at = p * size + t * wide
                    flat[t, base : base + wide, :] = blocks[k][at : at + wide, :].astype(F32)
                else:
                    for r in range(rows + 2):
                        at = p * size + main * wide + (r % deep) * colp
                        lane = (r // deep) * rest
                        flat[t, base + r * colp : base + (r + 1) * colp, 0:rest] = blocks[k][
                            at : at + colp, lane : lane + rest
                        ].astype(F32)
                span = (rows + 1) * colp + base + 8
                tall = flat[t, 0:span, :] + flat[t, colp : colp + span, :]
                flat[tiles, 0:span, :] = tall
                both = flat[tiles, 0 : span - 8, :] + flat[tiles, 1 : span - 7, :]
                flat[tiles + 1, 0 : span - 8, :] = both * 0.25
                plane = flat.at[tiles + 1]
                for tap in range(9):
                    ty, tx = tap // 3, tap % 3
                    for i in range(orows):
                        q = base + (2 * i + ty) * colp + tx - 1
                        value = plane[pl.ds(q, half, stride=2), :].astype(BF16)
                        row = ((k * per + p) * orows + i) * half
                        taps[tap, row : row + half, t * 128 : t * 128 + lanes] = value[:, :lanes]
    total = jnp.dot(taps[0], kernel[0], preferred_element_type=F32)
    for tap in range(1, 9):
        total = total + jnp.dot(taps[tap], kernel[tap], preferred_element_type=F32)
    for k in range(groups):
        for p in range(per):
            for i in range(orows):
                row = ((k * per + p) * orows + i) * half
                at = (p * orows + i) * ocols
                squeezed[at : at + ocols, :] = total[row : row + ocols]
        outs[k][...] = squeezed[...].astype(outs[k].dtype)


def stage(blocks, kernel, per, rows, cols, colp):
    groups = len(blocks)
    taps, c1, depth = kernel.shape
    tiles = -(-c1 // 128)
    px = per * rows * cols // 4
    count = groups * per * (rows // 2) * (colp // 2)
    return pl.pallas_call(
        functools.partial(stage_kernel, groups, per, rows, cols, colp, c1),
        out_shape=[jax.ShapeDtypeStruct((px, depth), F32)]
        + [jax.ShapeDtypeStruct((px, depth), BF16)] * (groups - 1),
        in_specs=[whole()] * (groups + 1),
        out_specs=[whole()] * groups,
        scratch_shapes=[
            pltpu.VMEM((tiles + 2, (rows + 3) * colp + 32, 128), F32),
            pltpu.VMEM((taps, count, c1), BF16),
            pltpu.VMEM((px, depth), F32),
        ],
        name="stage",
        compiler_params=pltpu.CompilerParams(vmem_limit_bytes=12 << 20),
        cost_estimate=pl.CostEstimate(
            flops=2 * count * taps * c1 * depth, bytes_accessed=4 * groups * px * depth, transcendentals=0
        ),
    )(*blocks, kernel)


def body(pixels, first_gain, first_shift, first_kernel, projection, second_gain, second_shift, second_kernel):
    sec = lax.axis_index("section")
    z = lax.axis_index("img")
    ch = lax.axis_index("ch")
    sections = lax.axis_size("section")
    groups = lax.axis_size("img")
    shards = lax.axis_size("ch")
    pairs = shards // 2
    y, core = ch // 2, ch % 2
    per = pixels.shape[0] // sections
    _, rows, cols, depth = pixels.shape
    orows, ocols = rows // 2, cols // 2
    wide = second_gain.shape[0]
    slab = wide // groups
    kc = slab // pairs
    kd = kc // 2
    c1 = depth // groups

    other_kernel = swap(second_kernel, "ch", 1)

    ids = jnp.stack([sec, z, ch, jnp.int32(shards - 1), y, core, z * pairs + y]).astype(jnp.int32)
    cuts = cut(ids, projection, groups, shards)
    colp = -(-(cols + 2) // 16) * 16
    tails = lax.dynamic_slice_in_dim(pixels[:, -1:], sec * per, per, 0)
    heads = lax.dynamic_slice_in_dim(pixels[:, :1], sec * per, per, 0)
    pixels, tails, heads = lax.optimization_barrier((pixels, tails, heads))
    above = lax.ppermute(tails, "ch", [(i, i + 1) for i in range(shards - 1)])
    below = lax.ppermute(heads, "ch", [(i + 1, i) for i in range(shards - 1)])
    packed = pack(
        ids,
        pixels,
        above,
        below,
        first_gain.reshape(1, -1),
        first_shift.reshape(1, -1),
        groups,
        per,
        colp,
    )
    blocks, mean = packed[:groups], packed[groups]
    got = [blocks[0]] + [swap(blocks[k], "img", k) for k in range(1, groups)]

    proj_z = join([cuts[0]] + [swap(cuts[k], "img", k) for k in range(1, groups)])
    proj_own = [proj_z] + [swap(proj_z, "ch", k, 2) for k in range(1, pairs)]
    proj_twin = [swap(part, "ch", 1) for part in proj_own]

    total, *sent = stage(got, first_kernel.reshape(9, c1, depth), per, rows, cols, colp)
    for k in range(1, groups):
        total = total + swap(sent[k - 1], "img", k).astype(F32)
    pooled = (total + mean.reshape(total.shape)).astype(BF16)
    pooled_all = [pooled] + [swap(pooled, "img", k) for k in range(1, groups)]
    px = per * orows * ocols
    imgs = groups * per
    out_px = orows * ocols
    made = project(ids, pooled_all, proj_own, proj_twin)
    back, chip = made[:groups], made[groups:]

    chip = [chip[0]] + [swap(chip[k], "ch", k, 2) for k in range(1, pairs)]
    twin = [swap(chip[0], "ch", 1)]
    twin += [swap(part, "ch", 1) for part in chip[1:]]
    back = [back[0]] + [swap(back[k], "img", k) for k in range(1, groups)]
    a_own, a_other = unfold(
        ids,
        second_gain.reshape(groups * pairs, kc),
        second_shift.reshape(groups * pairs, kc),
        [c.reshape(imgs, out_px, kc) for c in chip],
        [c.reshape(imgs, out_px, kc) for c in twin],
        ocols,
    )
    w_own = streamed(second_kernel.reshape(9 * kd, wide))
    w_other = streamed(other_kernel.reshape(9 * kd, wide))

    unit = wide // 10
    plan = ((0, 2), (1, 3), (0, 3), (1, 2))
    names = [("ch", 1 << i, 2) for i in range(pairs.bit_length() - 1)]
    names_z = [("img", 1 << i, 1) for i in range(groups.bit_length() - 1)]
    values, first = [], 0
    for kind, n in plan:
        hops = names_z + names if kind else names + names_z
        keys = [(a, b) for a in range(pairs) for b in range(groups)]

        def split(keys, hop):
            axis, k, _ = hop
            bit = [key[0] & k if axis == "ch" else key[1] & k for key in keys]
            rows = ([i for i, x in enumerate(bit) if x], [i for i, x in enumerate(bit) if not x])
            return rows, [key for key, x in zip(keys, bit) if not x]

        rows, keys = split(keys, hops[0])
        sent, kept = mix(a_own, a_other, w_own, w_other, first, n * unit, unit, rows, px)
        for h, hop in enumerate(hops):
            axis, k, size = hop
            came = swap(sent, axis, k, size)
            if h + 1 < len(hops):
                rows, keys = split(keys, hops[h + 1])
                sent, kept = merge(kept, came, rows, px)
        values.append((kept, came, first, n * unit))
        first += n * unit

    mine_projected = spread(ids, back)
    far_projected = lax.ppermute(mine_projected, "section", [(1, 0)])
    outs, fars = [], []
    for j, some in enumerate((values[:2], values[2:])):
        outs.append(finish([v[:2] for v in some], mine_projected, some[0][2]))
        fars.append(lax.ppermute(outs[j], "section", [(0, 1)]))
    block = final(ids, mine_projected, far_projected, outs, fars, per, orows, ocols)
    return block.transpose(0, 2, 1, 3)[None]


def solution(mesh):
    placed = (
        P("img", "ch", None, None),
        P(),
        P(),
        P(None, None, "img", None),
        P("img", None),
        P(),
        P(),
        P(None, None, ("img", "ch"), None),
    )

    return jax.shard_map(
        body,
        mesh=mesh,
        in_specs=placed,
        out_specs=P("section", "img", "ch", None, None),
        check_vma=False,
    )
```

```python
import functools

import jax
import jax.numpy as jnp
from jax import lax
from jax.experimental import pallas as pl
from jax.experimental.pallas import tpu as pltpu
from jax.sharding import PartitionSpec as P


BF16 = jnp.bfloat16
F32 = jnp.float32


def swap(array, axis, k, unit=1):
    count = lax.axis_size(axis)
    return lax.ppermute(array, axis, [(i, i ^ (k * unit)) for i in range(count)])


def streamed(array):
    return pltpu.with_memory_space_constraint(array, pltpu.HBM)


def whole(memory_space=pltpu.VMEM):
    return pl.BlockSpec(memory_space=memory_space)


def unfold_kernel(pairs, imgs, ocols, kd, rows, px, first, step, ids, gains, shifts, *refs):
    w_own, w_other = refs[2 * pairs : 2 * pairs + 2]
    a_own, a_other, sent, kept = refs[2 * pairs + 2 : 2 * pairs + 6]
    held_own, held_other, sems = refs[2 * pairs + 9 :]
    count = held_own.shape[1]
    columns = pl.ds(first, count)
    copies = [
        pltpu.make_async_copy(w_own.at[:, columns], held_own, sems.at[0]),
        pltpu.make_async_copy(w_other.at[:, columns], held_other, sems.at[1]),
    ]
    for copy in copies:
        copy.start()
    unfold_rows(pairs, imgs, ocols, kd, ids, gains, shifts, *refs[: 2 * pairs], *refs[2 * pairs + 2 : 2 * pairs + 4],
                *refs[2 * pairs + 6 : 2 * pairs + 9])
    for copy in copies:
        copy.wait()
    for at in range(0, count, step):
        cut = slice(at, at + step)
        value = jnp.dot(a_own[...], held_own[:, cut], preferred_element_type=F32)
        value = value + jnp.dot(a_other[...], held_other[:, cut], preferred_element_type=F32)
        copy_rows(sent.at[:, cut], value, rows[0], px)
        copy_rows(kept.at[:, cut], value, rows[1], px)


def unfold_rows(pairs, imgs, ocols, kd, ids, gains, shifts, *refs):
    own, other = refs[:pairs], refs[pairs : 2 * pairs]
    out_own, out_other, centre, border, strip = refs[2 * pairs :]
    y, core, group = ids[4], ids[5], ids[6]
    gain, shift = gains[pl.ds(group, 1), :], shifts[pl.ds(group, 1), :]
    px = own[0].shape[1]
    first = core == 0
    base = 24

    def halves(value):
        normed = jax.nn.relu(value.astype(F32) * gain + shift).astype(BF16).astype(F32)
        low, high = normed[:, :kd], normed[:, kd:]
        return jnp.where(first, low, high), jnp.where(first, high, low)

    border[0] = jnp.zeros(border.shape[1:], F32)
    border[pairs + 1] = jnp.zeros(border.shape[1:], F32)
    for k in range(pairs):
        place = jnp.bitwise_xor(y, k)
        for i in range(imgs):
            for half, value in enumerate(halves(own[k][i])):
                centre[place, i, half] = value
            for half, value in enumerate(halves(other[k][i])):
                border[place + 1, i, half, 0] = value[:ocols]
                border[place + 1, i, half, 1] = value[px - ocols :]
    at = lax.broadcasted_iota(jnp.int32, (px, kd), 0) % ocols
    left, right = at == 0, at == ocols - 1
    shift_up = jnp.where(first, 0, 1)
    strip[...] = jnp.zeros(strip.shape, F32)
    for k in range(pairs):
        place = jnp.bitwise_xor(y, k)
        for half, out in enumerate((out_own, out_other)):
            for i in range(0, imgs, 2):
                for m in range(2):
                    strip[m, base : base + px] = centre[place, i + m, half]
                    strip[m, base - ocols : base] = border[place + shift_up, i + m, half, 1]
                    strip[m, base + px : base + px + ocols] = border[place + 1 + shift_up, i + m, half, 0]
                for tap in range(9):
                    dy, dx = tap // 3 - 1, tap % 3 - 1
                    off = base + dy * ocols + dx
                    values = [strip[m, off : off + px] for m in range(2)]
                    if dx == -1:
                        values = [jnp.where(left, 0.0, v) for v in values]
                    if dx == 1:
                        values = [jnp.where(right, 0.0, v) for v in values]
                    row = (k * imgs + i) * px
                    out[row : row + 2 * px, tap * kd : (tap + 1) * kd] = jnp.concatenate(values).astype(BF16)


def unfold(ids, gain, shift, own, other, ocols, w_own, w_other, first, count, step, split, block):
    pairs = len(own)
    imgs, px, kc = own[0].shape
    kd = kc // 2
    rows = pairs * imgs * px
    lanes = -(-kd // 128) * 128
    deep = 9 * kd
    need = 8 * pairs * imgs * px * lanes + 256 * (pairs + 2) * imgs * lanes
    need += 36 * rows * kd + 8 * pairs * imgs * px * lanes
    limit = (4 << 20) + 2 * need + 4 * deep * count + 8 * rows * count
    sizes = [len(r) * block for r in split]
    return pl.pallas_call(
        functools.partial(unfold_kernel, pairs, imgs, ocols, kd, split, block, first, step),
        out_shape=[pltpu.VMEM((rows, deep), BF16)] * 2
        + [
            jax.ShapeDtypeStruct((sizes[0], count), BF16),
            jax.ShapeDtypeStruct((sizes[1], count), F32),
        ],
        in_specs=[whole(pltpu.SMEM)]
        + [whole()] * (2 + 2 * pairs)
        + [pl.BlockSpec(memory_space=pltpu.HBM)] * 2,
        out_specs=[whole()] * 4,
        scratch_shapes=[
            pltpu.VMEM((pairs, imgs, 2, px, kd), F32),
            pltpu.VMEM((pairs + 2, imgs, 2, 2, ocols, kd), F32),
            pltpu.VMEM((2, 24 + px + 24, kd), F32),
            pltpu.VMEM((deep, count), BF16),
            pltpu.VMEM((deep, count), BF16),
            pltpu.SemaphoreType.DMA((2,)),
        ],
        name="unfold",
        compiler_params=pltpu.CompilerParams(vmem_limit_bytes=min(60 << 20, limit)),
        cost_estimate=pl.CostEstimate(
            flops=4 * rows * deep * count, bytes_accessed=4 * deep * count, transcendentals=0
        ),
    )(ids, gain, shift, *own, *other, w_own, w_other)


def copy_rows(out, value, rows, px):
    for i, row in enumerate(rows):
        out[i * px : (i + 1) * px, :] = value[row * px : (row + 1) * px].astype(out.dtype)


def mix_kernel(rows, px, a_own, a_other, w_own, w_other, sent, kept):
    value = jnp.dot(a_own[...], w_own[...], preferred_element_type=F32)
    value = value + jnp.dot(a_other[...], w_other[...], preferred_element_type=F32)
    copy_rows(sent, value, rows[0], px)
    copy_rows(kept, value, rows[1], px)


def mix(a_own, a_other, w_own, w_other, first, count, step, rows, px):
    total, deep = a_own.shape
    weight = pl.BlockSpec((deep, step), lambda i: (0, first // step + i))
    sizes = [len(r) * px for r in rows]
    return pl.pallas_call(
        functools.partial(mix_kernel, rows, px),
        grid=(count // step,),
        out_shape=[
            jax.ShapeDtypeStruct((sizes[0], count), BF16),
            jax.ShapeDtypeStruct((sizes[1], count), F32),
        ],
        in_specs=[whole()] * 2 + [weight] * 2,
        out_specs=[pl.BlockSpec((size, step), lambda i: (0, i)) for size in sizes],
        name="mix",
        compiler_params=pltpu.CompilerParams(vmem_limit_bytes=16 << 20),
        cost_estimate=pl.CostEstimate(
            flops=4 * total * deep * count,
            bytes_accessed=4 * deep * count + 3 * total * count,
            transcendentals=0,
        ),
    )(a_own, a_other, w_own, w_other)


def merge_kernel(rows, px, kept, came, *outs):
    value = kept[...] + came[...].astype(F32)
    for out, some in zip(outs, rows):
        copy_rows(out, value, some, px)


def merge(kept, came, rows, px):
    count = kept.shape[1]
    return pl.pallas_call(
        functools.partial(merge_kernel, rows, px),
        out_shape=[jax.ShapeDtypeStruct((len(r) * px, count), t) for r, t in zip(rows, (BF16, F32))],
        in_specs=[whole()] * 2,
        out_specs=[whole()] * 2,
        name="merge",
        compiler_params=pltpu.CompilerParams(vmem_limit_bytes=10 << 20),
        cost_estimate=pl.CostEstimate(flops=kept.size, bytes_accessed=10 * kept.size, transcendentals=0),
    )(kept, came)


def finish_kernel(first, count, *refs):
    extra, out = refs[2 * count :]
    at = 0
    for i in range(count):
        kept, came = refs[2 * i : 2 * i + 2]
        n = kept.shape[1]
        value = kept[...] + came[...].astype(F32) + extra[:, first + at : first + at + n].astype(F32)
        out[:, at : at + n] = value.astype(BF16)
        at += n


def finish(parts, extra, first):
    flat = [array for part in parts for array in part]
    px = flat[0].shape[0]
    wide = sum(part[0].shape[1] for part in parts)
    return pl.pallas_call(
        functools.partial(finish_kernel, first, len(parts)),
        out_shape=jax.ShapeDtypeStruct((px, wide), BF16),
        in_specs=[whole()] * (2 * len(parts) + 1),
        out_specs=whole(),
        name="finish",
        compiler_params=pltpu.CompilerParams(vmem_limit_bytes=6 << 20),
        cost_estimate=pl.CostEstimate(flops=2 * px * wide, bytes_accessed=10 * px * wide, transcendentals=0),
    )(*flat, extra)


def pool_kernel(total, mean, *refs):
    value = total[...] + mean[...].reshape(total.shape)
    for ref in refs[:-1]:
        value = value + ref[...].astype(F32)
    refs[-1][...] = value.astype(BF16)


def pool(total, mean, came):
    return pl.pallas_call(
        pool_kernel,
        out_shape=jax.ShapeDtypeStruct(total.shape, BF16),
        in_specs=[whole()] * (2 + len(came)),
        out_specs=whole(),
        name="pool",
        compiler_params=pltpu.CompilerParams(vmem_limit_bytes=4 << 20),
    )(total, mean, *came)


def join_kernel(*refs):
    for i, ref in enumerate(refs[:-1]):
        refs[-1][i] = ref[...]


def join(parts):
    return pl.pallas_call(
        join_kernel,
        out_shape=jax.ShapeDtypeStruct((len(parts),) + parts[0].shape, parts[0].dtype),
        in_specs=[whole()] * len(parts),
        out_specs=whole(),
        name="join",
        compiler_params=pltpu.CompilerParams(vmem_limit_bytes=6 << 20),
    )(*parts)


def project_kernel(groups, pairs, ids, *refs):
    pooled = refs[:groups]
    own, twin = refs[groups : groups + pairs], refs[groups + pairs : groups + 2 * pairs]
    backs = refs[groups + 2 * pairs : 2 * groups + 2 * pairs]
    parts = refs[2 * groups + 2 * pairs : 2 * groups + 3 * pairs]
    weight, held = refs[2 * groups + 3 * pairs :]
    z, y, core = ids[1], ids[4], ids[5]
    px, depth = pooled[0].shape
    for k in range(groups):
        for j in range(pairs):
            for half, source in enumerate((own, twin)):
                place = (jnp.bitwise_xor(z, k) * pairs + jnp.bitwise_xor(y, j)) * 2 + jnp.bitwise_xor(core, half)
                weight[place] = source[j][k].astype(F32)
    slab = weight[...].reshape(depth, weight.shape[2]).astype(BF16)
    kc = weight.shape[2] // pairs
    rows = jnp.concatenate([ref[...].astype(F32) for ref in pooled]).astype(BF16)
    value = jnp.dot(rows, slab, preferred_element_type=F32)
    for k in range(groups):
        backs[k][...] = value[k * px : (k + 1) * px].astype(BF16)
    for j in range(pairs):
        held[j] = value[:, j * kc : (j + 1) * kc].astype(BF16)
    for j in range(pairs):
        parts[j][...] = held[jnp.bitwise_xor(y, j)]


def project(ids, pooled, own, twin):
    groups, pairs = len(pooled), len(own)
    px, depth = pooled[0].shape
    _, deep, slab = own[0].shape
    kc = slab // pairs
    back = jax.ShapeDtypeStruct((px, slab), BF16)
    part = jax.ShapeDtypeStruct((groups * px, kc), BF16)
    return pl.pallas_call(
        functools.partial(project_kernel, groups, pairs),
        out_shape=[back] * groups + [part] * pairs,
        in_specs=[whole(pltpu.SMEM)] + [whole()] * (groups + 2 * pairs),
        out_specs=[whole()] * (groups + pairs),
        scratch_shapes=[
            pltpu.VMEM((groups * pairs * 2, deep, slab), F32),
            pltpu.VMEM((pairs, groups * px, kc), BF16),
        ],
        name="project",
        compiler_params=pltpu.CompilerParams(vmem_limit_bytes=14 << 20),
        cost_estimate=pl.CostEstimate(
            flops=2 * groups * px * depth * slab, bytes_accessed=4 * depth * slab, transcendentals=0
        ),
    )(ids, *pooled, *own, *twin)


def packing(rows, colp, c1):
    main = c1 // 128
    rest = c1 - main * 128
    fit = 128 // rest if rest else 1
    deep = -(-rows // fit) if rest else 0
    return main, rest, deep, main * rows * colp + deep * colp


def cut_kernel(ids, projection, *refs):
    cuts, strip = refs[:-1], refs[-1]
    z, ch = ids[1], ids[2]
    deep, slab = cuts[0].shape
    groups = len(cuts)
    for i in range(projection.shape[0] // deep):
        for g in range(groups):
            strip[i, g] = projection[i * deep : (i + 1) * deep, g * slab : (g + 1) * slab].astype(F32)
    for k in range(groups):
        cuts[k][...] = strip[ch, jnp.bitwise_xor(z, k)].astype(BF16)


def cut(ids, projection, groups, shards):
    deep, slab = projection.shape[0] // shards, projection.shape[1] // groups
    return pl.pallas_call(
        cut_kernel,
        out_shape=[jax.ShapeDtypeStruct((deep, slab), BF16)] * groups,
        in_specs=[whole(pltpu.SMEM), whole()],
        out_specs=[whole()] * groups,
        scratch_shapes=[pltpu.VMEM((shards, groups, deep, slab), F32)],
        name="cut",
        compiler_params=pltpu.CompilerParams(vmem_limit_bytes=8 << 20),
    )(ids, projection)


def spread_kernel(groups, ids, *refs):
    backs, out, held = refs[:groups], refs[groups], refs[groups + 1]
    slab = backs[0].shape[1]
    for k in range(groups):
        held[jnp.bitwise_xor(ids[1], k)] = backs[k][...]
    for g in range(groups):
        out[:, g * slab : (g + 1) * slab] = held[g]


def spread(ids, backs):
    px, slab = backs[0].shape
    groups = len(backs)
    return pl.pallas_call(
        functools.partial(spread_kernel, groups),
        out_shape=jax.ShapeDtypeStruct((px, groups * slab), BF16),
        in_specs=[whole(pltpu.SMEM)] + [whole()] * groups,
        out_specs=whole(),
        scratch_shapes=[pltpu.VMEM((groups, px, slab), BF16)],
        name="spread",
        compiler_params=pltpu.CompilerParams(vmem_limit_bytes=6 << 20),
    )(ids, *backs)


def final_kernel(per, orows, ocols, ids, mine, far_mine, own, far, *refs):
    out, held = refs[-2:]
    first = ids[0] == 0
    for half in range(2):
        for lane in range(0, own.shape[1], 128):
            lanes = slice(lane, lane + 128)
            a = mine if half == 0 else far_mine
            b = far if half == 0 else own
            held[...] = jnp.where(first, a[:, lanes].astype(F32), b[:, lanes].astype(F32))
            for p in range(per):
                for c in range(ocols):
                    some = held[pl.ds(p * orows * ocols + c, orows, stride=ocols), :]
                    out[half * per + p, c, :, lanes] = some.astype(BF16)


def final(ids, mine, far_mine, own, far, so_far, first, step, per, orows, ocols):
    px, wide = mine.shape
    at = first // step
    shared = pl.BlockSpec((px, step), lambda i: (0, at + i))
    local = pl.BlockSpec((px, step), lambda i: (0, i))
    more = [] if so_far is None else [so_far]
    return pl.pallas_call(
        functools.partial(final_kernel, per, orows, ocols),
        grid=(own.shape[1] // step,),
        out_shape=jax.ShapeDtypeStruct((2 * per, ocols, orows, wide), BF16),
        in_specs=[whole(pltpu.SMEM), shared, shared, local, local]
        + [pl.BlockSpec(memory_space=pl.ANY)] * len(more),
        out_specs=pl.BlockSpec((2 * per, ocols, orows, step), lambda i: (0, 0, 0, at + i)),
        scratch_shapes=[pltpu.VMEM((px, 128), F32)],
        input_output_aliases={5: 0} if more else {},
        name="final",
        compiler_params=pltpu.CompilerParams(vmem_limit_bytes=6 << 20),
    )(ids, mine, far_mine, own, far, *more)


def pack_kernel(groups, per, c1, colp, ids, pixels, above, below, gain, shift, *refs):
    outs, mean = refs[:groups], refs[groups]
    held, pair = refs[groups + 1 :]
    sec, z, ch, last = ids[0], ids[1], ids[2], ids[3]
    _, rows, cols, depth = pixels.shape
    main, rest, deep, size = packing(rows + 2, colp, c1)
    scale, offset = gain[...], shift[...]
    filler = jnp.zeros((colp - cols, depth), F32)
    for p in range(per):
        for r in range(rows + 2):
            if r == 0:
                value = above[p, 0].astype(F32)
            elif r == rows + 1:
                value = below[p, 0].astype(F32)
            else:
                value = pixels[sec * per + p, r - 1].astype(F32)
            if 1 <= r <= rows:
                i, half = (r - 1) // 2, cols // 2
                for t in range(depth // 128):
                    lanes = slice(t * 128, (t + 1) * 128)
                    if r % 2 == 1:
                        pair[t] = value[:, lanes]
                    else:
                        pair[t] = pair[t] + value[:, lanes]
                        both = pair.at[t]
                        total = both[pl.ds(0, half, stride=2), :] + both[pl.ds(1, half, stride=2), :]
                        mean[p, i * half : (i + 1) * half, lanes] = total * 0.25
            value = jax.nn.relu(value * scale + offset)
            if r == 0:
                value = jnp.where(ch == 0, 0.0, value)
            if r == rows + 1:
                value = jnp.where(ch == last, 0.0, value)
            value = jnp.concatenate([value, filler]).astype(BF16)
            for g in range(groups):
                for m in range(main):
                    at = p * size + (m * (rows + 2) + r) * colp
                    lane = g * c1 + m * 128
                    held[g, at : at + colp, :] = value[:, lane : lane + 128]
                if rest:
                    at = p * size + main * (rows + 2) * colp + (r % deep) * colp
                    lane = g * c1 + main * 128
                    into = (r // deep) * rest
                    held[g, at : at + colp, into : into + rest] = value[:, lane : lane + rest]
    for k in range(groups):
        outs[k][...] = held[jnp.bitwise_xor(z, k)]


def pack(ids, pixels, above, below, gain, shift, groups, per, colp):
    _, rows, cols, depth = pixels.shape
    c1 = depth // groups
    size = packing(rows + 2, colp, c1)[3]
    block = jax.ShapeDtypeStruct((per * size, 128), BF16)
    half = jax.ShapeDtypeStruct((per, rows * cols // 4, depth), F32)
    return pl.pallas_call(
        functools.partial(pack_kernel, groups, per, c1, colp),
        out_shape=[block] * groups + [half],
        in_specs=[whole(pltpu.SMEM)] + [whole()] * 5,
        out_specs=[whole()] * (groups + 1),
        scratch_shapes=[
            pltpu.VMEM((groups, per * size, 128), BF16),
            pltpu.VMEM((depth // 128, cols, 128), F32),
        ],
        name="pack",
        compiler_params=pltpu.CompilerParams(vmem_limit_bytes=14 << 20),
        cost_estimate=pl.CostEstimate(
            flops=4 * rows * cols * depth, bytes_accessed=6 * rows * cols * depth, transcendentals=0
        ),
    )(ids, pixels, above, below, gain, shift)


def stage_kernel(groups, per, rows, cols, colp, c1, *refs):
    blocks, kernel = refs[:groups], refs[groups]
    outs = refs[groups + 1 : 2 * groups + 1]
    flat, taps, squeezed = refs[2 * groups + 1 :]
    main, rest, deep, size = packing(rows + 2, colp, c1)
    tiles = main + (1 if rest else 0)
    orows, ocols = rows // 2, cols // 2
    base, wide = 8, (rows + 2) * colp
    half = colp // 2
    flat[...] = jnp.zeros(flat.shape, F32)
    for k in range(groups):
        for p in range(per):
            for t in range(tiles):
                lanes = 128 if t < main else rest
                if t < main:
                    at = p * size + t * wide
                    flat[t, base : base + wide, :] = blocks[k][at : at + wide, :].astype(F32)
                else:
                    for r in range(rows + 2):
                        at = p * size + main * wide + (r % deep) * colp
                        lane = (r // deep) * rest
                        flat[t, base + r * colp : base + (r + 1) * colp, 0:rest] = blocks[k][
                            at : at + colp, lane : lane + rest
                        ].astype(F32)
                span = (rows + 1) * colp + base + 8
                tall = flat[t, 0:span, :] + flat[t, colp : colp + span, :]
                flat[tiles, 0:span, :] = tall
                both = flat[tiles, 0 : span - 8, :] + flat[tiles, 1 : span - 7, :]
                flat[tiles + 1, 0 : span - 8, :] = both * 0.25
                plane = flat.at[tiles + 1]
                for tap in range(9):
                    ty, tx = tap // 3, tap % 3
                    for i in range(orows):
                        q = base + (2 * i + ty) * colp + tx - 1
                        value = plane[pl.ds(q, half, stride=2), :].astype(BF16)
                        row = ((k * per + p) * orows + i) * half
                        taps[tap, row : row + half, t * 128 : t * 128 + lanes] = value[:, :lanes]
    total = jnp.dot(taps[0], kernel[0], preferred_element_type=F32)
    for tap in range(1, 9):
        total = total + jnp.dot(taps[tap], kernel[tap], preferred_element_type=F32)
    for k in range(groups):
        for p in range(per):
            for i in range(orows):
                row = ((k * per + p) * orows + i) * half
                at = (p * orows + i) * ocols
                squeezed[at : at + ocols, :] = total[row : row + ocols]
        outs[k][...] = squeezed[...].astype(outs[k].dtype)


def stage(blocks, kernel, per, rows, cols, colp):
    groups = len(blocks)
    taps, c1, depth = kernel.shape
    tiles = -(-c1 // 128)
    px = per * rows * cols // 4
    count = groups * per * (rows // 2) * (colp // 2)
    return pl.pallas_call(
        functools.partial(stage_kernel, groups, per, rows, cols, colp, c1),
        out_shape=[jax.ShapeDtypeStruct((px, depth), F32)]
        + [jax.ShapeDtypeStruct((px, depth), BF16)] * (groups - 1),
        in_specs=[whole()] * (groups + 1),
        out_specs=[whole()] * groups,
        scratch_shapes=[
            pltpu.VMEM((tiles + 2, (rows + 3) * colp + 32, 128), F32),
            pltpu.VMEM((taps, count, c1), BF16),
            pltpu.VMEM((px, depth), F32),
        ],
        name="stage",
        compiler_params=pltpu.CompilerParams(vmem_limit_bytes=12 << 20),
        cost_estimate=pl.CostEstimate(
            flops=2 * count * taps * c1 * depth, bytes_accessed=4 * groups * px * depth, transcendentals=0
        ),
    )(*blocks, kernel)


def body(pixels, first_gain, first_shift, first_kernel, projection, second_gain, second_shift, second_kernel):
    sec = lax.axis_index("section")
    z = lax.axis_index("img")
    ch = lax.axis_index("ch")
    sections = lax.axis_size("section")
    groups = lax.axis_size("img")
    shards = lax.axis_size("ch")
    pairs = shards // 2
    y, core = ch // 2, ch % 2
    per = pixels.shape[0] // sections
    _, rows, cols, depth = pixels.shape
    orows, ocols = rows // 2, cols // 2
    wide = second_gain.shape[0]
    slab = wide // groups
    kc = slab // pairs
    kd = kc // 2
    c1 = depth // groups

    other_kernel = swap(second_kernel, "ch", 1)

    ids = jnp.stack([sec, z, ch, jnp.int32(shards - 1), y, core, z * pairs + y]).astype(jnp.int32)
    cuts = cut(ids, projection, groups, shards)
    colp = -(-(cols + 2) // 16) * 16
    tails = lax.dynamic_slice_in_dim(pixels[:, -1:], sec * per, per, 0)
    heads = lax.dynamic_slice_in_dim(pixels[:, :1], sec * per, per, 0)
    pixels, tails, heads = lax.optimization_barrier((pixels, tails, heads))
    above = lax.ppermute(tails, "ch", [(i, i + 1) for i in range(shards - 1)])
    below = lax.ppermute(heads, "ch", [(i + 1, i) for i in range(shards - 1)])
    packed = pack(
        ids,
        pixels,
        above,
        below,
        first_gain.reshape(1, -1),
        first_shift.reshape(1, -1),
        groups,
        per,
        colp,
    )
    blocks, mean = packed[:groups], packed[groups]
    got = [blocks[0]] + [swap(blocks[k], "img", k) for k in range(1, groups)]

    proj_z = join([cuts[0]] + [swap(cuts[k], "img", k) for k in range(1, groups)])
    proj_own = [proj_z] + [swap(proj_z, "ch", k, 2) for k in range(1, pairs)]
    proj_twin = [swap(part, "ch", 1) for part in proj_own]

    total, *sent = stage(got, first_kernel.reshape(9, c1, depth), per, rows, cols, colp)
    came = [swap(sent[k - 1], "img", k) for k in range(1, groups)]
    pooled = pool(total, mean, came)
    pooled_all = [pooled] + [swap(pooled, "img", k) for k in range(1, groups)]
    px = per * orows * ocols
    imgs = groups * per
    out_px = orows * ocols
    made = project(ids, pooled_all, proj_own, proj_twin)
    back, chip = made[:groups], made[groups:]

    chip = [chip[0]] + [swap(chip[k], "ch", k, 2) for k in range(1, pairs)]
    twin = [swap(chip[0], "ch", 1)]
    twin += [swap(part, "ch", 1) for part in chip[1:]]
    back = [back[0]] + [swap(back[k], "img", k) for k in range(1, groups)]
    w_own = streamed(second_kernel.reshape(9 * kd, wide))
    w_other = streamed(other_kernel.reshape(9 * kd, wide))

    unit = wide // 10
    plan = ((0, 4), (1, 3), (0, 3))
    names = [("ch", 1 << i, 2) for i in range(pairs.bit_length() - 1)]
    names_z = [("img", 1 << i, 1) for i in range(groups.bit_length() - 1)]
    values, first = [], 0
    for j, (kind, n) in enumerate(plan):
        hops = names_z + names if kind else names + names_z
        keys = [(a, b) for a in range(pairs) for b in range(groups)]

        def split(keys, hop):
            axis, k, _ = hop
            bit = [key[0] & k if axis == "ch" else key[1] & k for key in keys]
            rows = ([i for i, x in enumerate(bit) if x], [i for i, x in enumerate(bit) if not x])
            return rows, [key for key, x in zip(keys, bit) if not x]

        rows, keys = split(keys, hops[0])
        if j == 0:
            a_own, a_other, sent, kept = unfold(
                ids,
                second_gain.reshape(groups * pairs, kc),
                second_shift.reshape(groups * pairs, kc),
                [c.reshape(imgs, out_px, kc) for c in chip],
                [c.reshape(imgs, out_px, kc) for c in twin],
                ocols,
                w_own,
                w_other,
                first,
                n * unit,
                unit,
                rows,
                px,
            )
        else:
            sent, kept = mix(a_own, a_other, w_own, w_other, first, n * unit, unit, rows, px)
        for h, hop in enumerate(hops):
            axis, k, size = hop
            came = swap(sent, axis, k, size)
            if h + 1 < len(hops):
                rows, keys = split(keys, hops[h + 1])
                sent, kept = merge(kept, came, rows, px)
        values.append((kept, came, first, n * unit))
        first += n * unit

    mine_projected = spread(ids, back)
    far_projected = lax.ppermute(mine_projected, "section", [(1, 0)])
    block = None
    for some in (values[:2], values[2:]):
        at = some[0][2]
        done = finish([v[:2] for v in some], mine_projected, at)
        far = lax.ppermute(done, "section", [(0, 1)])
        block = final(ids, mine_projected, far_projected, done, far, block, at, unit, per, orows, ocols)
    return block.transpose(0, 2, 1, 3)[None]


def solution(mesh):
    placed = (
        P("img", "ch", None, None),
        P(),
        P(),
        P(None, None, "img", None),
        P("img", None),
        P(),
        P(),
        P(None, None, ("img", "ch"), None),
    )

    return jax.shard_map(
        body,
        mesh=mesh,
        in_specs=placed,
        out_specs=P("section", "img", "ch", None, None),
        check_vma=False,
    )
```

```python
import functools

import jax
import jax.numpy as jnp
from jax import lax
from jax.experimental import pallas as pl
from jax.experimental.pallas import tpu as pltpu
from jax.sharding import PartitionSpec as P


BF16 = jnp.bfloat16
F32 = jnp.float32


def swap(array, axis, k, unit=1):
    count = lax.axis_size(axis)
    return lax.ppermute(array, axis, [(i, i ^ (k * unit)) for i in range(count)])


def streamed(array):
    return pltpu.with_memory_space_constraint(array, pltpu.HBM)


def whole(memory_space=pltpu.VMEM):
    return pl.BlockSpec(memory_space=memory_space)


def unfold_kernel(pairs, imgs, ocols, kd, rows, px, first, step, ids, gains, shifts, *refs):
    w_own, w_other = refs[2 * pairs : 2 * pairs + 2]
    a_own, a_other, sent, kept = refs[2 * pairs + 2 : 2 * pairs + 6]
    held_own, held_other, sems = refs[2 * pairs + 9 :]
    count = held_own.shape[1]
    copies = []
    for i in range(count // step):
        here, there = pl.ds(i * step, step), pl.ds(first + i * step, step)
        copies.append(
            [
                pltpu.make_async_copy(w_own.at[:, there], held_own.at[:, here], sems.at[2 * i]),
                pltpu.make_async_copy(w_other.at[:, there], held_other.at[:, here], sems.at[2 * i + 1]),
            ]
        )
        for copy in copies[i]:
            copy.start()
    unfold_rows(pairs, imgs, ocols, kd, ids, gains, shifts, *refs[: 2 * pairs], *refs[2 * pairs + 2 : 2 * pairs + 4],
                *refs[2 * pairs + 6 : 2 * pairs + 9])
    for at in range(0, count, step):
        cut = slice(at, at + step)
        for copy in copies[at // step]:
            copy.wait()
        value = jnp.dot(a_own[...], held_own[:, cut], preferred_element_type=F32)
        value = value + jnp.dot(a_other[...], held_other[:, cut], preferred_element_type=F32)
        copy_rows(sent.at[:, cut], value, rows[0], px)
        copy_rows(kept.at[:, cut], value, rows[1], px)


def unfold_rows(pairs, imgs, ocols, kd, ids, gains, shifts, *refs):
    own, other = refs[:pairs], refs[pairs : 2 * pairs]
    out_own, out_other, centre, border, strip = refs[2 * pairs :]
    y, core, group = ids[4], ids[5], ids[6]
    gain, shift = gains[pl.ds(group, 1), :], shifts[pl.ds(group, 1), :]
    px = own[0].shape[1]
    first = core == 0
    base = 24

    def halves(value):
        normed = jax.nn.relu(value.astype(F32) * gain + shift).astype(BF16).astype(F32)
        low, high = normed[:, :kd], normed[:, kd:]
        return jnp.where(first, low, high), jnp.where(first, high, low)

    border[0] = jnp.zeros(border.shape[1:], F32)
    border[pairs + 1] = jnp.zeros(border.shape[1:], F32)
    for k in range(pairs):
        place = jnp.bitwise_xor(y, k)
        for i in range(imgs):
            for half, value in enumerate(halves(own[k][i])):
                centre[place, i, half] = value
            for half, value in enumerate(halves(other[k][i])):
                border[place + 1, i, half, 0] = value[:ocols]
                border[place + 1, i, half, 1] = value[px - ocols :]
    at = lax.broadcasted_iota(jnp.int32, (px, kd), 0) % ocols
    left, right = at == 0, at == ocols - 1
    shift_up = jnp.where(first, 0, 1)
    strip[...] = jnp.zeros(strip.shape, F32)
    for k in range(pairs):
        place = jnp.bitwise_xor(y, k)
        for half, out in enumerate((out_own, out_other)):
            for i in range(0, imgs, 2):
                for m in range(2):
                    strip[m, base : base + px] = centre[place, i + m, half]
                    strip[m, base - ocols : base] = border[place + shift_up, i + m, half, 1]
                    strip[m, base + px : base + px + ocols] = border[place + 1 + shift_up, i + m, half, 0]
                for tap in range(9):
                    dy, dx = tap // 3 - 1, tap % 3 - 1
                    off = base + dy * ocols + dx
                    values = [strip[m, off : off + px] for m in range(2)]
                    if dx == -1:
                        values = [jnp.where(left, 0.0, v) for v in values]
                    if dx == 1:
                        values = [jnp.where(right, 0.0, v) for v in values]
                    row = (k * imgs + i) * px
                    out[row : row + 2 * px, tap * kd : (tap + 1) * kd] = jnp.concatenate(values).astype(BF16)


def unfold(ids, gain, shift, own, other, ocols, w_own, w_other, first, count, step, split, block):
    pairs = len(own)
    imgs, px, kc = own[0].shape
    kd = kc // 2
    rows = pairs * imgs * px
    lanes = -(-kd // 128) * 128
    deep = 9 * kd
    need = 8 * pairs * imgs * px * lanes + 256 * (pairs + 2) * imgs * lanes
    need += 36 * rows * kd + 8 * pairs * imgs * px * lanes
    limit = (4 << 20) + 2 * need + 4 * deep * count + 8 * rows * count
    sizes = [len(r) * block for r in split]
    return pl.pallas_call(
        functools.partial(unfold_kernel, pairs, imgs, ocols, kd, split, block, first, step),
        out_shape=[pltpu.VMEM((rows, deep), BF16)] * 2
        + [
            jax.ShapeDtypeStruct((sizes[0], count), BF16),
            jax.ShapeDtypeStruct((sizes[1], count), F32),
        ],
        in_specs=[whole(pltpu.SMEM)]
        + [whole()] * (2 + 2 * pairs)
        + [pl.BlockSpec(memory_space=pltpu.HBM)] * 2,
        out_specs=[whole()] * 4,
        scratch_shapes=[
            pltpu.VMEM((pairs, imgs, 2, px, kd), F32),
            pltpu.VMEM((pairs + 2, imgs, 2, 2, ocols, kd), F32),
            pltpu.VMEM((2, 24 + px + 24, kd), F32),
            pltpu.VMEM((deep, count), BF16),
            pltpu.VMEM((deep, count), BF16),
            pltpu.SemaphoreType.DMA((2 * (count // step),)),
        ],
        name="unfold",
        compiler_params=pltpu.CompilerParams(vmem_limit_bytes=min(60 << 20, limit)),
        cost_estimate=pl.CostEstimate(
            flops=4 * rows * deep * count, bytes_accessed=4 * deep * count, transcendentals=0
        ),
    )(ids, gain, shift, *own, *other, w_own, w_other)


def copy_rows(out, value, rows, px):
    for i, row in enumerate(rows):
        out[i * px : (i + 1) * px, :] = value[row * px : (row + 1) * px].astype(out.dtype)


def mix_kernel(rows, px, a_own, a_other, w_own, w_other, sent, kept):
    value = jnp.dot(a_own[...], w_own[...], preferred_element_type=F32)
    value = value + jnp.dot(a_other[...], w_other[...], preferred_element_type=F32)
    copy_rows(sent, value, rows[0], px)
    copy_rows(kept, value, rows[1], px)


def mix(a_own, a_other, w_own, w_other, first, count, step, rows, px):
    total, deep = a_own.shape
    weight = pl.BlockSpec((deep, step), lambda i: (0, first // step + i))
    sizes = [len(r) * px for r in rows]
    return pl.pallas_call(
        functools.partial(mix_kernel, rows, px),
        grid=(count // step,),
        out_shape=[
            jax.ShapeDtypeStruct((sizes[0], count), BF16),
            jax.ShapeDtypeStruct((sizes[1], count), F32),
        ],
        in_specs=[whole()] * 2 + [weight] * 2,
        out_specs=[pl.BlockSpec((size, step), lambda i: (0, i)) for size in sizes],
        name="mix",
        compiler_params=pltpu.CompilerParams(vmem_limit_bytes=16 << 20),
        cost_estimate=pl.CostEstimate(
            flops=4 * total * deep * count,
            bytes_accessed=4 * deep * count + 3 * total * count,
            transcendentals=0,
        ),
    )(a_own, a_other, w_own, w_other)


def merge_kernel(rows, px, kept, came, *outs):
    value = kept[...] + came[...].astype(F32)
    for out, some in zip(outs, rows):
        copy_rows(out, value, some, px)


def merge(kept, came, rows, px):
    count = kept.shape[1]
    return pl.pallas_call(
        functools.partial(merge_kernel, rows, px),
        out_shape=[jax.ShapeDtypeStruct((len(r) * px, count), t) for r, t in zip(rows, (BF16, F32))],
        in_specs=[whole()] * 2,
        out_specs=[whole()] * 2,
        name="merge",
        compiler_params=pltpu.CompilerParams(vmem_limit_bytes=10 << 20),
        cost_estimate=pl.CostEstimate(flops=kept.size, bytes_accessed=10 * kept.size, transcendentals=0),
    )(kept, came)


def finish_kernel(first, count, *refs):
    extra, out = refs[2 * count :]
    at = 0
    for i in range(count):
        kept, came = refs[2 * i : 2 * i + 2]
        n = kept.shape[1]
        value = kept[...] + came[...].astype(F32) + extra[:, first + at : first + at + n].astype(F32)
        out[:, at : at + n] = value.astype(BF16)
        at += n


def finish(parts, extra, first):
    flat = [array for part in parts for array in part]
    px = flat[0].shape[0]
    wide = sum(part[0].shape[1] for part in parts)
    return pl.pallas_call(
        functools.partial(finish_kernel, first, len(parts)),
        out_shape=jax.ShapeDtypeStruct((px, wide), BF16),
        in_specs=[whole()] * (2 * len(parts) + 1),
        out_specs=whole(),
        name="finish",
        compiler_params=pltpu.CompilerParams(vmem_limit_bytes=6 << 20),
        cost_estimate=pl.CostEstimate(flops=2 * px * wide, bytes_accessed=10 * px * wide, transcendentals=0),
    )(*flat, extra)


def pool_kernel(total, mean, *refs):
    value = total[...] + mean[...].reshape(total.shape)
    for ref in refs[:-1]:
        value = value + ref[...].astype(F32)
    refs[-1][...] = value.astype(BF16)


def pool(total, mean, came):
    return pl.pallas_call(
        pool_kernel,
        out_shape=jax.ShapeDtypeStruct(total.shape, BF16),
        in_specs=[whole()] * (2 + len(came)),
        out_specs=whole(),
        name="pool",
        compiler_params=pltpu.CompilerParams(vmem_limit_bytes=4 << 20),
    )(total, mean, *came)


def join_kernel(*refs):
    for i, ref in enumerate(refs[:-1]):
        refs[-1][i] = ref[...]


def join(parts):
    return pl.pallas_call(
        join_kernel,
        out_shape=jax.ShapeDtypeStruct((len(parts),) + parts[0].shape, parts[0].dtype),
        in_specs=[whole()] * len(parts),
        out_specs=whole(),
        name="join",
        compiler_params=pltpu.CompilerParams(vmem_limit_bytes=6 << 20),
    )(*parts)


def project_kernel(groups, pairs, ids, *refs):
    pooled = refs[:groups]
    own, twin = refs[groups : groups + pairs], refs[groups + pairs : groups + 2 * pairs]
    backs = refs[groups + 2 * pairs : 2 * groups + 2 * pairs]
    parts = refs[2 * groups + 2 * pairs : 2 * groups + 3 * pairs]
    weight, held = refs[2 * groups + 3 * pairs :]
    z, y, core = ids[1], ids[4], ids[5]
    px, depth = pooled[0].shape
    for k in range(groups):
        for j in range(pairs):
            for half, source in enumerate((own, twin)):
                place = (jnp.bitwise_xor(z, k) * pairs + jnp.bitwise_xor(y, j)) * 2 + jnp.bitwise_xor(core, half)
                weight[place] = source[j][k].astype(F32)
    slab = weight[...].reshape(depth, weight.shape[2]).astype(BF16)
    kc = weight.shape[2] // pairs
    rows = jnp.concatenate([ref[...].astype(F32) for ref in pooled]).astype(BF16)
    value = jnp.dot(rows, slab, preferred_element_type=F32)
    for k in range(groups):
        backs[k][...] = value[k * px : (k + 1) * px].astype(BF16)
    for j in range(pairs):
        held[j] = value[:, j * kc : (j + 1) * kc].astype(BF16)
    for j in range(pairs):
        parts[j][...] = held[jnp.bitwise_xor(y, j)]


def project(ids, pooled, own, twin):
    groups, pairs = len(pooled), len(own)
    px, depth = pooled[0].shape
    _, deep, slab = own[0].shape
    kc = slab // pairs
    back = jax.ShapeDtypeStruct((px, slab), BF16)
    part = jax.ShapeDtypeStruct((groups * px, kc), BF16)
    return pl.pallas_call(
        functools.partial(project_kernel, groups, pairs),
        out_shape=[back] * groups + [part] * pairs,
        in_specs=[whole(pltpu.SMEM)] + [whole()] * (groups + 2 * pairs),
        out_specs=[whole()] * (groups + pairs),
        scratch_shapes=[
            pltpu.VMEM((groups * pairs * 2, deep, slab), F32),
            pltpu.VMEM((pairs, groups * px, kc), BF16),
        ],
        name="project",
        compiler_params=pltpu.CompilerParams(vmem_limit_bytes=14 << 20),
        cost_estimate=pl.CostEstimate(
            flops=2 * groups * px * depth * slab, bytes_accessed=4 * depth * slab, transcendentals=0
        ),
    )(ids, *pooled, *own, *twin)


def packing(rows, colp, c1):
    main = c1 // 128
    rest = c1 - main * 128
    fit = 128 // rest if rest else 1
    deep = -(-rows // fit) if rest else 0
    return main, rest, deep, main * rows * colp + deep * colp


def cut_kernel(ids, projection, *refs):
    cuts, strip = refs[:-1], refs[-1]
    z, ch = ids[1], ids[2]
    deep, slab = cuts[0].shape
    groups = len(cuts)
    for i in range(projection.shape[0] // deep):
        for g in range(groups):
            strip[i, g] = projection[i * deep : (i + 1) * deep, g * slab : (g + 1) * slab].astype(F32)
    for k in range(groups):
        cuts[k][...] = strip[ch, jnp.bitwise_xor(z, k)].astype(BF16)


def cut(ids, projection, groups, shards):
    deep, slab = projection.shape[0] // shards, projection.shape[1] // groups
    return pl.pallas_call(
        cut_kernel,
        out_shape=[jax.ShapeDtypeStruct((deep, slab), BF16)] * groups,
        in_specs=[whole(pltpu.SMEM), whole()],
        out_specs=[whole()] * groups,
        scratch_shapes=[pltpu.VMEM((shards, groups, deep, slab), F32)],
        name="cut",
        compiler_params=pltpu.CompilerParams(vmem_limit_bytes=8 << 20),
    )(ids, projection)


def spread_kernel(groups, ids, *refs):
    backs, out, held = refs[:groups], refs[groups], refs[groups + 1]
    slab = backs[0].shape[1]
    for k in range(groups):
        held[jnp.bitwise_xor(ids[1], k)] = backs[k][...]
    for g in range(groups):
        out[:, g * slab : (g + 1) * slab] = held[g]


def spread(ids, backs):
    px, slab = backs[0].shape
    groups = len(backs)
    return pl.pallas_call(
        functools.partial(spread_kernel, groups),
        out_shape=jax.ShapeDtypeStruct((px, groups * slab), BF16),
        in_specs=[whole(pltpu.SMEM)] + [whole()] * groups,
        out_specs=whole(),
        scratch_shapes=[pltpu.VMEM((groups, px, slab), BF16)],
        name="spread",
        compiler_params=pltpu.CompilerParams(vmem_limit_bytes=6 << 20),
    )(ids, *backs)


def final_kernel(parts, per, orows, ocols, ids, mine, far_mine, *refs):
    own, far = refs[:parts], refs[parts : 2 * parts]
    out, held = refs[2 * parts :]
    first = ids[0] == 0
    for half in range(2):
        at = 0
        for i in range(parts):
            count = own[i].shape[1]
            for lane in range(0, count, 128):
                here = slice(lane, lane + 128)
                there = slice(at + lane, at + lane + 128)
                a = mine[:, there] if half == 0 else far_mine[:, there]
                b = far[i][:, here] if half == 0 else own[i][:, here]
                held[...] = jnp.where(first, a.astype(F32), b.astype(F32))
                for p in range(per):
                    for c in range(ocols):
                        some = held[pl.ds(p * orows * ocols + c, orows, stride=ocols), :]
                        out[half * per + p, c, :, there] = some.astype(BF16)
            at += count


def final(ids, mine, far_mine, own, far, per, orows, ocols):
    wide = mine.shape[1]
    return pl.pallas_call(
        functools.partial(final_kernel, len(own), per, orows, ocols),
        out_shape=jax.ShapeDtypeStruct((2 * per, ocols, orows, wide), BF16),
        in_specs=[whole(pltpu.SMEM)] + [whole()] * (2 + 2 * len(own)),
        out_specs=whole(),
        scratch_shapes=[pltpu.VMEM((mine.shape[0], 128), F32)],
        name="final",
        compiler_params=pltpu.CompilerParams(vmem_limit_bytes=10 << 20),
    )(ids, mine, far_mine, *own, *far)


def pack_kernel(groups, per, c1, colp, ids, pixels, above, below, gain, shift, *refs):
    outs, mean = refs[:groups], refs[groups]
    held, pair = refs[groups + 1 :]
    sec, z, ch, last = ids[0], ids[1], ids[2], ids[3]
    _, rows, cols, depth = pixels.shape
    main, rest, deep, size = packing(rows + 2, colp, c1)
    scale, offset = gain[...], shift[...]
    filler = jnp.zeros((colp - cols, depth), F32)
    for p in range(per):
        for r in range(rows + 2):
            if r == 0:
                value = above[p, 0].astype(F32)
            elif r == rows + 1:
                value = below[p, 0].astype(F32)
            else:
                value = pixels[sec * per + p, r - 1].astype(F32)
            if 1 <= r <= rows:
                i, half = (r - 1) // 2, cols // 2
                for t in range(depth // 128):
                    lanes = slice(t * 128, (t + 1) * 128)
                    if r % 2 == 1:
                        pair[t] = value[:, lanes]
                    else:
                        pair[t] = pair[t] + value[:, lanes]
                        both = pair.at[t]
                        total = both[pl.ds(0, half, stride=2), :] + both[pl.ds(1, half, stride=2), :]
                        mean[p, i * half : (i + 1) * half, lanes] = total * 0.25
            value = jax.nn.relu(value * scale + offset)
            if r == 0:
                value = jnp.where(ch == 0, 0.0, value)
            if r == rows + 1:
                value = jnp.where(ch == last, 0.0, value)
            value = jnp.concatenate([value, filler]).astype(BF16)
            for g in range(groups):
                for m in range(main):
                    at = p * size + (m * (rows + 2) + r) * colp
                    lane = g * c1 + m * 128
                    held[g, at : at + colp, :] = value[:, lane : lane + 128]
                if rest:
                    at = p * size + main * (rows + 2) * colp + (r % deep) * colp
                    lane = g * c1 + main * 128
                    into = (r // deep) * rest
                    held[g, at : at + colp, into : into + rest] = value[:, lane : lane + rest]
    for k in range(groups):
        outs[k][...] = held[jnp.bitwise_xor(z, k)]


def pack(ids, pixels, above, below, gain, shift, groups, per, colp):
    _, rows, cols, depth = pixels.shape
    c1 = depth // groups
    size = packing(rows + 2, colp, c1)[3]
    block = jax.ShapeDtypeStruct((per * size, 128), BF16)
    half = jax.ShapeDtypeStruct((per, rows * cols // 4, depth), F32)
    return pl.pallas_call(
        functools.partial(pack_kernel, groups, per, c1, colp),
        out_shape=[block] * groups + [half],
        in_specs=[whole(pltpu.SMEM)] + [whole()] * 5,
        out_specs=[whole()] * (groups + 1),
        scratch_shapes=[
            pltpu.VMEM((groups, per * size, 128), BF16),
            pltpu.VMEM((depth // 128, cols, 128), F32),
        ],
        name="pack",
        compiler_params=pltpu.CompilerParams(vmem_limit_bytes=14 << 20),
        cost_estimate=pl.CostEstimate(
            flops=4 * rows * cols * depth, bytes_accessed=6 * rows * cols * depth, transcendentals=0
        ),
    )(ids, pixels, above, below, gain, shift)


def stage_kernel(groups, per, rows, cols, colp, c1, *refs):
    blocks, kernel = refs[:groups], refs[groups]
    outs = refs[groups + 1 : 2 * groups + 1]
    flat, taps, squeezed = refs[2 * groups + 1 :]
    main, rest, deep, size = packing(rows + 2, colp, c1)
    tiles = main + (1 if rest else 0)
    orows, ocols = rows // 2, cols // 2
    base, wide = 8, (rows + 2) * colp
    half = colp // 2
    flat[...] = jnp.zeros(flat.shape, F32)
    for k in range(groups):
        for p in range(per):
            for t in range(tiles):
                lanes = 128 if t < main else rest
                if t < main:
                    at = p * size + t * wide
                    flat[t, base : base + wide, :] = blocks[k][at : at + wide, :].astype(F32)
                else:
                    for r in range(rows + 2):
                        at = p * size + main * wide + (r % deep) * colp
                        lane = (r // deep) * rest
                        flat[t, base + r * colp : base + (r + 1) * colp, 0:rest] = blocks[k][
                            at : at + colp, lane : lane + rest
                        ].astype(F32)
                span = (rows + 1) * colp + base + 8
                tall = flat[t, 0:span, :] + flat[t, colp : colp + span, :]
                flat[tiles, 0:span, :] = tall
                both = flat[tiles, 0 : span - 8, :] + flat[tiles, 1 : span - 7, :]
                flat[tiles + 1, 0 : span - 8, :] = both * 0.25
                plane = flat.at[tiles + 1]
                for tap in range(9):
                    ty, tx = tap // 3, tap % 3
                    for i in range(orows):
                        q = base + (2 * i + ty) * colp + tx - 1
                        value = plane[pl.ds(q, half, stride=2), :].astype(BF16)
                        row = ((k * per + p) * orows + i) * half
                        taps[tap, row : row + half, t * 128 : t * 128 + lanes] = value[:, :lanes]
    total = jnp.dot(taps[0], kernel[0], preferred_element_type=F32)
    for tap in range(1, 9):
        total = total + jnp.dot(taps[tap], kernel[tap], preferred_element_type=F32)
    for k in range(groups):
        for p in range(per):
            for i in range(orows):
                row = ((k * per + p) * orows + i) * half
                at = (p * orows + i) * ocols
                squeezed[at : at + ocols, :] = total[row : row + ocols]
        outs[k][...] = squeezed[...].astype(outs[k].dtype)


def stage(blocks, kernel, per, rows, cols, colp):
    groups = len(blocks)
    taps, c1, depth = kernel.shape
    tiles = -(-c1 // 128)
    px = per * rows * cols // 4
    count = groups * per * (rows // 2) * (colp // 2)
    return pl.pallas_call(
        functools.partial(stage_kernel, groups, per, rows, cols, colp, c1),
        out_shape=[jax.ShapeDtypeStruct((px, depth), F32)]
        + [jax.ShapeDtypeStruct((px, depth), BF16)] * (groups - 1),
        in_specs=[whole()] * (groups + 1),
        out_specs=[whole()] * groups,
        scratch_shapes=[
            pltpu.VMEM((tiles + 2, (rows + 3) * colp + 32, 128), F32),
            pltpu.VMEM((taps, count, c1), BF16),
            pltpu.VMEM((px, depth), F32),
        ],
        name="stage",
        compiler_params=pltpu.CompilerParams(vmem_limit_bytes=12 << 20),
        cost_estimate=pl.CostEstimate(
            flops=2 * count * taps * c1 * depth, bytes_accessed=4 * groups * px * depth, transcendentals=0
        ),
    )(*blocks, kernel)


def body(pixels, first_gain, first_shift, first_kernel, projection, second_gain, second_shift, second_kernel):
    sec = lax.axis_index("section")
    z = lax.axis_index("img")
    ch = lax.axis_index("ch")
    sections = lax.axis_size("section")
    groups = lax.axis_size("img")
    shards = lax.axis_size("ch")
    pairs = shards // 2
    y, core = ch // 2, ch % 2
    per = pixels.shape[0] // sections
    _, rows, cols, depth = pixels.shape
    orows, ocols = rows // 2, cols // 2
    wide = second_gain.shape[0]
    slab = wide // groups
    kc = slab // pairs
    kd = kc // 2
    c1 = depth // groups

    other_kernel = swap(second_kernel, "ch", 1)

    ids = jnp.stack([sec, z, ch, jnp.int32(shards - 1), y, core, z * pairs + y]).astype(jnp.int32)
    colp = -(-(cols + 2) // 16) * 16
    tails = lax.dynamic_slice_in_dim(pixels[:, -1:], sec * per, per, 0)
    heads = lax.dynamic_slice_in_dim(pixels[:, :1], sec * per, per, 0)
    pixels, tails, heads = lax.optimization_barrier((pixels, tails, heads))
    above = lax.ppermute(tails, "ch", [(i, i + 1) for i in range(shards - 1)])
    below = lax.ppermute(heads, "ch", [(i + 1, i) for i in range(shards - 1)])
    packed = pack(
        ids,
        pixels,
        above,
        below,
        first_gain.reshape(1, -1),
        first_shift.reshape(1, -1),
        groups,
        per,
        colp,
    )
    blocks, mean = packed[:groups], packed[groups]
    got = [blocks[0]] + [swap(blocks[k], "img", k) for k in range(1, groups)]

    cuts = cut(ids, projection, groups, shards)
    proj_z = join([cuts[0]] + [swap(cuts[k], "img", k) for k in range(1, groups)])
    proj_own = [proj_z] + [swap(proj_z, "ch", k, 2) for k in range(1, pairs)]
    proj_twin = [swap(part, "ch", 1) for part in proj_own]

    total, *sent = stage(got, first_kernel.reshape(9, c1, depth), per, rows, cols, colp)
    came = [swap(sent[k - 1], "img", k) for k in range(1, groups)]
    pooled = pool(total, mean, came)
    pooled_all = [pooled] + [swap(pooled, "img", k) for k in range(1, groups)]
    px = per * orows * ocols
    imgs = groups * per
    out_px = orows * ocols
    made = project(ids, pooled_all, proj_own, proj_twin)
    back, chip = made[:groups], made[groups:]

    chip = [chip[0]] + [swap(chip[k], "ch", k, 2) for k in range(1, pairs)]
    twin = [swap(chip[0], "ch", 1)]
    twin += [swap(part, "ch", 1) for part in chip[1:]]
    back = [back[0]] + [swap(back[k], "img", k) for k in range(1, groups)]
    w_own = streamed(second_kernel.reshape(9 * kd, wide))
    w_other = streamed(other_kernel.reshape(9 * kd, wide))

    unit = wide // 10
    plan = ((0, 4), (1, 3), (0, 3))
    names = [("ch", 1 << i, 2) for i in range(pairs.bit_length() - 1)]
    names_z = [("img", 1 << i, 1) for i in range(groups.bit_length() - 1)]
    values, first = [], 0
    for j, (kind, n) in enumerate(plan):
        hops = names_z + names if kind else names + names_z
        keys = [(a, b) for a in range(pairs) for b in range(groups)]

        def split(keys, hop):
            axis, k, _ = hop
            bit = [key[0] & k if axis == "ch" else key[1] & k for key in keys]
            rows = ([i for i, x in enumerate(bit) if x], [i for i, x in enumerate(bit) if not x])
            return rows, [key for key, x in zip(keys, bit) if not x]

        rows, keys = split(keys, hops[0])
        if j == 0:
            a_own, a_other, sent, kept = unfold(
                ids,
                second_gain.reshape(groups * pairs, kc),
                second_shift.reshape(groups * pairs, kc),
                [c.reshape(imgs, out_px, kc) for c in chip],
                [c.reshape(imgs, out_px, kc) for c in twin],
                ocols,
                w_own,
                w_other,
                first,
                n * unit,
                unit,
                rows,
                px,
            )
        else:
            sent, kept = mix(a_own, a_other, w_own, w_other, first, n * unit, unit, rows, px)
        for h, hop in enumerate(hops):
            axis, k, size = hop
            came = swap(sent, axis, k, size)
            if h + 1 < len(hops):
                rows, keys = split(keys, hops[h + 1])
                sent, kept = merge(kept, came, rows, px)
        values.append((kept, came, first, n * unit))
        first += n * unit

    mine_projected = spread(ids, back)
    far_projected = lax.ppermute(mine_projected, "section", [(1, 0)])
    outs, fars = [], []
    for j, some in enumerate((values[:2], values[2:])):
        outs.append(finish([v[:2] for v in some], mine_projected, some[0][2]))
        fars.append(lax.ppermute(outs[j], "section", [(0, 1)]))
    block = final(ids, mine_projected, far_projected, outs, fars, per, orows, ocols)
    return block.transpose(0, 2, 1, 3)[None]


def solution(mesh):
    placed = (
        P("img", "ch", None, None),
        P(),
        P(),
        P(None, None, "img", None),
        P("img", None),
        P(),
        P(),
        P(None, None, ("img", "ch"), None),
    )

    return jax.shard_map(
        body,
        mesh=mesh,
        in_specs=placed,
        out_specs=P("section", "img", "ch", None, None),
        check_vma=False,
    )
```

```python
import functools

import jax
import jax.numpy as jnp
from jax import lax
from jax.experimental import pallas as pl
from jax.experimental.pallas import tpu as pltpu
from jax.sharding import PartitionSpec as P


BF16 = jnp.bfloat16
F32 = jnp.float32


def swap(array, axis, k, unit=1):
    count = lax.axis_size(axis)
    return lax.ppermute(array, axis, [(i, i ^ (k * unit)) for i in range(count)])


def streamed(array):
    return pltpu.with_memory_space_constraint(array, pltpu.HBM)


def whole(memory_space=pltpu.VMEM):
    return pl.BlockSpec(memory_space=memory_space)


def unfold_kernel(pairs, imgs, ocols, kd, rows, px, first, step, ids, gains, shifts, *refs):
    w_own, w_other = refs[2 * pairs : 2 * pairs + 2]
    a_own, a_other, held_own, held_other, sent, kept = refs[2 * pairs + 2 : 2 * pairs + 8]
    scratch, partial, sems = refs[2 * pairs + 8 : -2], refs[-2], refs[-1]
    pieces = sems.shape[0] // 2
    deep = w_own.shape[0] // pieces
    copies = []
    for i in range(2 * pieces):
        source, target = ((w_own, held_own), (w_other, held_other))[i // pieces]
        if pieces > 1:
            some = pl.ds((i % pieces) * deep, deep)
            source, target = source.at[some], target.at[some]
        copies.append(pltpu.make_async_copy(source, target, sems.at[i]))
        copies[i].start()
    unfold_rows(pairs, imgs, ocols, kd, ids, gains, shifts, *refs[: 2 * pairs], a_own, a_other, *scratch)
    for copy in copies[:pieces]:
        copy.wait()
    count = sent.shape[1]
    cuts = [slice(first + at, first + at + step) for at in range(0, count, step)]
    for i, cut in enumerate(cuts):
        partial[:, i * step : (i + 1) * step] = jnp.dot(a_own[...], held_own[:, cut], preferred_element_type=F32)
    for copy in copies[pieces:]:
        copy.wait()
    for i, cut in enumerate(cuts):
        here = slice(i * step, (i + 1) * step)
        value = partial[:, here] + jnp.dot(a_other[...], held_other[:, cut], preferred_element_type=F32)
        copy_rows(sent.at[:, here], value, rows[0], px)
        copy_rows(kept.at[:, here], value, rows[1], px)


def unfold_rows(pairs, imgs, ocols, kd, ids, gains, shifts, *refs):
    own, other = refs[:pairs], refs[pairs : 2 * pairs]
    out_own, out_other, centre, border, strip = refs[2 * pairs :]
    y, core, group = ids[4], ids[5], ids[6]
    gain, shift = gains[pl.ds(group, 1), :], shifts[pl.ds(group, 1), :]
    px = own[0].shape[1]
    first = core == 0
    base = 24

    def halves(value):
        normed = jax.nn.relu(value.astype(F32) * gain + shift).astype(BF16).astype(F32)
        low, high = normed[:, :kd], normed[:, kd:]
        return jnp.where(first, low, high), jnp.where(first, high, low)

    border[0] = jnp.zeros(border.shape[1:], F32)
    border[pairs + 1] = jnp.zeros(border.shape[1:], F32)
    for k in range(pairs):
        place = jnp.bitwise_xor(y, k)
        for i in range(imgs):
            for half, value in enumerate(halves(own[k][i])):
                centre[place, i, half] = value
            for half, value in enumerate(halves(other[k][i])):
                border[place + 1, i, half, 0] = value[:ocols]
                border[place + 1, i, half, 1] = value[px - ocols :]
    at = lax.broadcasted_iota(jnp.int32, (px, kd), 0) % ocols
    left, right = at == 0, at == ocols - 1
    shift_up = jnp.where(first, 0, 1)
    strip[...] = jnp.zeros(strip.shape, F32)
    for k in range(pairs):
        place = jnp.bitwise_xor(y, k)
        for half, out in enumerate((out_own, out_other)):
            for i in range(0, imgs, 2):
                for m in range(2):
                    strip[m, base : base + px] = centre[place, i + m, half]
                    strip[m, base - ocols : base] = border[place + shift_up, i + m, half, 1]
                    strip[m, base + px : base + px + ocols] = border[place + 1 + shift_up, i + m, half, 0]
                for tap in range(9):
                    dy, dx = tap // 3 - 1, tap % 3 - 1
                    off = base + dy * ocols + dx
                    values = [strip[m, off : off + px] for m in range(2)]
                    if dx == -1:
                        values = [jnp.where(left, 0.0, v) for v in values]
                    if dx == 1:
                        values = [jnp.where(right, 0.0, v) for v in values]
                    row = (k * imgs + i) * px
                    out[row : row + 2 * px, tap * kd : (tap + 1) * kd] = jnp.concatenate(values).astype(BF16)


def unfold(ids, gain, shift, own, other, ocols, w_own, w_other, first, count, step, split, block):
    pairs = len(own)
    imgs, px, kc = own[0].shape
    kd = kc // 2
    rows = pairs * imgs * px
    lanes = -(-kd // 128) * 128
    deep = 9 * kd
    need = 8 * pairs * imgs * px * lanes + 256 * (pairs + 2) * imgs * lanes
    need += 36 * rows * kd + 8 * pairs * imgs * px * lanes
    limit = (4 << 20) + need + need // 4 + 8 * rows * count
    pieces = 3 if deep % 24 == 0 else 1
    sizes = [len(r) * block for r in split]
    return pl.pallas_call(
        functools.partial(unfold_kernel, pairs, imgs, ocols, kd, split, block, first, step),
        out_shape=[pltpu.VMEM((rows, deep), BF16)] * 2
        + [pltpu.VMEM(w_own.shape, BF16)] * 2
        + [
            jax.ShapeDtypeStruct((sizes[0], count), BF16),
            jax.ShapeDtypeStruct((sizes[1], count), F32),
        ],
        in_specs=[whole(pltpu.SMEM)]
        + [whole()] * (2 + 2 * pairs)
        + [pl.BlockSpec(memory_space=pltpu.HBM)] * 2,
        out_specs=[whole()] * 6,
        scratch_shapes=[
            pltpu.VMEM((pairs, imgs, 2, px, kd), F32),
            pltpu.VMEM((pairs + 2, imgs, 2, 2, ocols, kd), F32),
            pltpu.VMEM((2, 24 + px + 24, kd), F32),
            pltpu.VMEM((rows, count), F32),
            pltpu.SemaphoreType.DMA((2 * pieces,)),
        ],
        name="unfold",
        compiler_params=pltpu.CompilerParams(vmem_limit_bytes=min(60 << 20, limit)),
        cost_estimate=pl.CostEstimate(
            flops=4 * rows * deep * count, bytes_accessed=8 * deep * w_own.shape[1], transcendentals=0
        ),
    )(ids, gain, shift, *own, *other, w_own, w_other)


def copy_rows(out, value, rows, px):
    for i, row in enumerate(rows):
        out[i * px : (i + 1) * px, :] = value[row * px : (row + 1) * px].astype(out.dtype)


def mix_kernel(rows, px, first, step, a_own, a_other, w_own, w_other, sent, kept):
    for at in range(0, sent.shape[1], step):
        cut = slice(first + at, first + at + step)
        value = jnp.dot(a_own[...], w_own[:, cut], preferred_element_type=F32)
        value = value + jnp.dot(a_other[...], w_other[:, cut], preferred_element_type=F32)
        here = slice(at, at + step)
        copy_rows(sent.at[:, here], value, rows[0], px)
        copy_rows(kept.at[:, here], value, rows[1], px)


def mix(a_own, a_other, w_own, w_other, first, count, step, rows, px):
    total, deep = a_own.shape
    sizes = [len(r) * px for r in rows]
    return pl.pallas_call(
        functools.partial(mix_kernel, rows, px, first, step),
        out_shape=[
            jax.ShapeDtypeStruct((sizes[0], count), BF16),
            jax.ShapeDtypeStruct((sizes[1], count), F32),
        ],
        in_specs=[whole()] * 4,
        out_specs=[whole()] * 2,
        name="mix",
        compiler_params=pltpu.CompilerParams(vmem_limit_bytes=12 << 20),
        cost_estimate=pl.CostEstimate(
            flops=4 * total * deep * count, bytes_accessed=3 * total * count, transcendentals=0
        ),
    )(a_own, a_other, w_own, w_other)


def merge_kernel(rows, px, kept, came, *outs):
    value = kept[...] + came[...].astype(F32)
    for out, some in zip(outs, rows):
        copy_rows(out, value, some, px)


def merge(kept, came, rows, px):
    count = kept.shape[1]
    return pl.pallas_call(
        functools.partial(merge_kernel, rows, px),
        out_shape=[jax.ShapeDtypeStruct((len(r) * px, count), t) for r, t in zip(rows, (BF16, F32))],
        in_specs=[whole()] * 2,
        out_specs=[whole()] * 2,
        name="merge",
        compiler_params=pltpu.CompilerParams(vmem_limit_bytes=10 << 20),
        cost_estimate=pl.CostEstimate(flops=kept.size, bytes_accessed=10 * kept.size, transcendentals=0),
    )(kept, came)


def finish_kernel(first, count, *refs):
    extra, out = refs[2 * count :]
    at = 0
    for i in range(count):
        kept, came = refs[2 * i : 2 * i + 2]
        n = kept.shape[1]
        value = kept[...] + came[...].astype(F32) + extra[:, first + at : first + at + n].astype(F32)
        out[:, at : at + n] = value.astype(BF16)
        at += n


def finish(parts, extra, first):
    flat = [array for part in parts for array in part]
    px = flat[0].shape[0]
    wide = sum(part[0].shape[1] for part in parts)
    return pl.pallas_call(
        functools.partial(finish_kernel, first, len(parts)),
        out_shape=jax.ShapeDtypeStruct((px, wide), BF16),
        in_specs=[whole()] * (2 * len(parts) + 1),
        out_specs=whole(),
        name="finish",
        compiler_params=pltpu.CompilerParams(vmem_limit_bytes=6 << 20),
        cost_estimate=pl.CostEstimate(flops=2 * px * wide, bytes_accessed=10 * px * wide, transcendentals=0),
    )(*flat, extra)


def pool_kernel(total, mean, *refs):
    value = total[...] + mean[...].reshape(total.shape)
    for ref in refs[:-1]:
        value = value + ref[...].astype(F32)
    refs[-1][...] = value.astype(BF16)


def pool(total, mean, came):
    return pl.pallas_call(
        pool_kernel,
        out_shape=jax.ShapeDtypeStruct(total.shape, BF16),
        in_specs=[whole()] * (2 + len(came)),
        out_specs=whole(),
        name="pool",
        compiler_params=pltpu.CompilerParams(vmem_limit_bytes=4 << 20),
    )(total, mean, *came)


def join_kernel(*refs):
    for i, ref in enumerate(refs[:-1]):
        refs[-1][i] = ref[...]


def join(parts):
    return pl.pallas_call(
        join_kernel,
        out_shape=jax.ShapeDtypeStruct((len(parts),) + parts[0].shape, parts[0].dtype),
        in_specs=[whole()] * len(parts),
        out_specs=whole(),
        name="join",
        compiler_params=pltpu.CompilerParams(vmem_limit_bytes=6 << 20),
    )(*parts)


def project_kernel(groups, pairs, ids, *refs):
    pooled = refs[:groups]
    own, twin = refs[groups : groups + pairs], refs[groups + pairs : groups + 2 * pairs]
    backs = refs[groups + 2 * pairs : 2 * groups + 2 * pairs]
    parts = refs[2 * groups + 2 * pairs : 2 * groups + 3 * pairs]
    weight, held = refs[2 * groups + 3 * pairs :]
    z, y, core = ids[1], ids[4], ids[5]
    px, depth = pooled[0].shape
    for k in range(groups):
        for j in range(pairs):
            for half, source in enumerate((own, twin)):
                place = (jnp.bitwise_xor(z, k) * pairs + jnp.bitwise_xor(y, j)) * 2 + jnp.bitwise_xor(core, half)
                weight[place] = source[j][k].astype(F32)
    slab = weight[...].reshape(depth, weight.shape[2]).astype(BF16)
    kc = weight.shape[2] // pairs
    rows = jnp.concatenate([ref[...].astype(F32) for ref in pooled]).astype(BF16)
    value = jnp.dot(rows, slab, preferred_element_type=F32)
    for k in range(groups):
        backs[k][...] = value[k * px : (k + 1) * px].astype(BF16)
    for j in range(pairs):
        held[j] = value[:, j * kc : (j + 1) * kc].astype(BF16)
    for j in range(pairs):
        parts[j][...] = held[jnp.bitwise_xor(y, j)]


def project(ids, pooled, own, twin):
    groups, pairs = len(pooled), len(own)
    px, depth = pooled[0].shape
    _, deep, slab = own[0].shape
    kc = slab // pairs
    back = jax.ShapeDtypeStruct((px, slab), BF16)
    part = jax.ShapeDtypeStruct((groups * px, kc), BF16)
    return pl.pallas_call(
        functools.partial(project_kernel, groups, pairs),
        out_shape=[back] * groups + [part] * pairs,
        in_specs=[whole(pltpu.SMEM)] + [whole()] * (groups + 2 * pairs),
        out_specs=[whole()] * (groups + pairs),
        scratch_shapes=[
            pltpu.VMEM((groups * pairs * 2, deep, slab), F32),
            pltpu.VMEM((pairs, groups * px, kc), BF16),
        ],
        name="project",
        compiler_params=pltpu.CompilerParams(vmem_limit_bytes=14 << 20),
        cost_estimate=pl.CostEstimate(
            flops=2 * groups * px * depth * slab, bytes_accessed=4 * depth * slab, transcendentals=0
        ),
    )(ids, *pooled, *own, *twin)


def packing(rows, colp, c1):
    main = c1 // 128
    rest = c1 - main * 128
    fit = 128 // rest if rest else 1
    deep = -(-rows // fit) if rest else 0
    return main, rest, deep, main * rows * colp + deep * colp


def cut_kernel(ids, projection, *refs):
    cuts, strip = refs[:-1], refs[-1]
    z, ch = ids[1], ids[2]
    deep, slab = cuts[0].shape
    groups = len(cuts)
    for i in range(projection.shape[0] // deep):
        for g in range(groups):
            strip[i, g] = projection[i * deep : (i + 1) * deep, g * slab : (g + 1) * slab].astype(F32)
    for k in range(groups):
        cuts[k][...] = strip[ch, jnp.bitwise_xor(z, k)].astype(BF16)


def cut(ids, projection, groups, shards):
    deep, slab = projection.shape[0] // shards, projection.shape[1] // groups
    return pl.pallas_call(
        cut_kernel,
        out_shape=[jax.ShapeDtypeStruct((deep, slab), BF16)] * groups,
        in_specs=[whole(pltpu.SMEM), whole()],
        out_specs=[whole()] * groups,
        scratch_shapes=[pltpu.VMEM((shards, groups, deep, slab), F32)],
        name="cut",
        compiler_params=pltpu.CompilerParams(vmem_limit_bytes=8 << 20),
    )(ids, projection)


def spread_kernel(groups, ids, *refs):
    backs, out, held = refs[:groups], refs[groups], refs[groups + 1]
    slab = backs[0].shape[1]
    for k in range(groups):
        held[jnp.bitwise_xor(ids[1], k)] = backs[k][...]
    for g in range(groups):
        out[:, g * slab : (g + 1) * slab] = held[g]


def spread(ids, backs):
    px, slab = backs[0].shape
    groups = len(backs)
    return pl.pallas_call(
        functools.partial(spread_kernel, groups),
        out_shape=jax.ShapeDtypeStruct((px, groups * slab), BF16),
        in_specs=[whole(pltpu.SMEM)] + [whole()] * groups,
        out_specs=whole(),
        scratch_shapes=[pltpu.VMEM((groups, px, slab), BF16)],
        name="spread",
        compiler_params=pltpu.CompilerParams(vmem_limit_bytes=6 << 20),
    )(ids, *backs)


def final_kernel(parts, per, orows, ocols, ids, mine, far_mine, *refs):
    own, far = refs[:parts], refs[parts : 2 * parts]
    out, held = refs[2 * parts :]
    first = ids[0] == 0
    for half in range(2):
        at = 0
        for i in range(parts):
            count = own[i].shape[1]
            for lane in range(0, count, 128):
                here = slice(lane, lane + 128)
                there = slice(at + lane, at + lane + 128)
                a = mine[:, there] if half == 0 else far_mine[:, there]
                b = far[i][:, here] if half == 0 else own[i][:, here]
                held[...] = jnp.where(first, a.astype(F32), b.astype(F32))
                for p in range(per):
                    for c in range(ocols):
                        some = held[pl.ds(p * orows * ocols + c, orows, stride=ocols), :]
                        out[half * per + p, c, :, there] = some.astype(BF16)
            at += count


def final(ids, mine, far_mine, own, far, per, orows, ocols):
    wide = mine.shape[1]
    return pl.pallas_call(
        functools.partial(final_kernel, len(own), per, orows, ocols),
        out_shape=jax.ShapeDtypeStruct((2 * per, ocols, orows, wide), BF16),
        in_specs=[whole(pltpu.SMEM)] + [whole()] * (2 + 2 * len(own)),
        out_specs=whole(),
        scratch_shapes=[pltpu.VMEM((mine.shape[0], 128), F32)],
        name="final",
        compiler_params=pltpu.CompilerParams(vmem_limit_bytes=10 << 20),
    )(ids, mine, far_mine, *own, *far)


def pack_kernel(groups, per, c1, colp, ids, pixels, above, below, gain, shift, *refs):
    outs, mean = refs[:groups], refs[groups]
    held, pair = refs[groups + 1 :]
    sec, z, ch, last = ids[0], ids[1], ids[2], ids[3]
    _, rows, cols, depth = pixels.shape
    main, rest, deep, size = packing(rows + 2, colp, c1)
    scale, offset = gain[...], shift[...]
    filler = jnp.zeros((colp - cols, depth), F32)
    for p in range(per):
        for r in range(rows + 2):
            if r == 0:
                value = above[p, 0].astype(F32)
            elif r == rows + 1:
                value = below[p, 0].astype(F32)
            else:
                value = pixels[sec * per + p, r - 1].astype(F32)
            if 1 <= r <= rows:
                i, half = (r - 1) // 2, cols // 2
                for t in range(depth // 128):
                    lanes = slice(t * 128, (t + 1) * 128)
                    if r % 2 == 1:
                        pair[t] = value[:, lanes]
                    else:
                        pair[t] = pair[t] + value[:, lanes]
                        both = pair.at[t]
                        total = both[pl.ds(0, half, stride=2), :] + both[pl.ds(1, half, stride=2), :]
                        mean[p, i * half : (i + 1) * half, lanes] = total * 0.25
            value = jax.nn.relu(value * scale + offset)
            if r == 0:
                value = jnp.where(ch == 0, 0.0, value)
            if r == rows + 1:
                value = jnp.where(ch == last, 0.0, value)
            value = jnp.concatenate([value, filler]).astype(BF16)
            for g in range(groups):
                for m in range(main):
                    at = p * size + (m * (rows + 2) + r) * colp
                    lane = g * c1 + m * 128
                    held[g, at : at + colp, :] = value[:, lane : lane + 128]
                if rest:
                    at = p * size + main * (rows + 2) * colp + (r % deep) * colp
                    lane = g * c1 + main * 128
                    into = (r // deep) * rest
                    held[g, at : at + colp, into : into + rest] = value[:, lane : lane + rest]
    for k in range(groups):
        outs[k][...] = held[jnp.bitwise_xor(z, k)]


def pack(ids, pixels, above, below, gain, shift, groups, per, colp):
    _, rows, cols, depth = pixels.shape
    c1 = depth // groups
    size = packing(rows + 2, colp, c1)[3]
    block = jax.ShapeDtypeStruct((per * size, 128), BF16)
    half = jax.ShapeDtypeStruct((per, rows * cols // 4, depth), F32)
    return pl.pallas_call(
        functools.partial(pack_kernel, groups, per, c1, colp),
        out_shape=[block] * groups + [half],
        in_specs=[whole(pltpu.SMEM)] + [whole()] * 5,
        out_specs=[whole()] * (groups + 1),
        scratch_shapes=[
            pltpu.VMEM((groups, per * size, 128), BF16),
            pltpu.VMEM((depth // 128, cols, 128), F32),
        ],
        name="pack",
        compiler_params=pltpu.CompilerParams(vmem_limit_bytes=14 << 20),
        cost_estimate=pl.CostEstimate(
            flops=4 * rows * cols * depth, bytes_accessed=6 * rows * cols * depth, transcendentals=0
        ),
    )(ids, pixels, above, below, gain, shift)


def stage_kernel(groups, per, rows, cols, colp, c1, *refs):
    blocks, kernel = refs[:groups], refs[groups]
    outs = refs[groups + 1 : 2 * groups + 1]
    flat, taps, squeezed = refs[2 * groups + 1 :]
    main, rest, deep, size = packing(rows + 2, colp, c1)
    tiles = main + (1 if rest else 0)
    orows, ocols = rows // 2, cols // 2
    base, wide = 8, (rows + 2) * colp
    half = colp // 2
    flat[...] = jnp.zeros(flat.shape, F32)
    for k in range(groups):
        for p in range(per):
            for t in range(tiles):
                lanes = 128 if t < main else rest
                if t < main:
                    at = p * size + t * wide
                    flat[t, base : base + wide, :] = blocks[k][at : at + wide, :].astype(F32)
                else:
                    for r in range(rows + 2):
                        at = p * size + main * wide + (r % deep) * colp
                        lane = (r // deep) * rest
                        flat[t, base + r * colp : base + (r + 1) * colp, 0:rest] = blocks[k][
                            at : at + colp, lane : lane + rest
                        ].astype(F32)
                span = (rows + 1) * colp + base + 8
                tall = flat[t, 0:span, :] + flat[t, colp : colp + span, :]
                flat[tiles, 0:span, :] = tall
                both = flat[tiles, 0 : span - 8, :] + flat[tiles, 1 : span - 7, :]
                flat[tiles + 1, 0 : span - 8, :] = both * 0.25
                plane = flat.at[tiles + 1]
                for tap in range(9):
                    ty, tx = tap // 3, tap % 3
                    for i in range(orows):
                        q = base + (2 * i + ty) * colp + tx - 1
                        value = plane[pl.ds(q, half, stride=2), :].astype(BF16)
                        row = ((k * per + p) * orows + i) * half
                        taps[tap, row : row + half, t * 128 : t * 128 + lanes] = value[:, :lanes]
    total = jnp.dot(taps[0], kernel[0], preferred_element_type=F32)
    for tap in range(1, 9):
        total = total + jnp.dot(taps[tap], kernel[tap], preferred_element_type=F32)
    for k in range(groups):
        for p in range(per):
            for i in range(orows):
                row = ((k * per + p) * orows + i) * half
                at = (p * orows + i) * ocols
                squeezed[at : at + ocols, :] = total[row : row + ocols]
        outs[k][...] = squeezed[...].astype(outs[k].dtype)


def stage(blocks, kernel, per, rows, cols, colp):
    groups = len(blocks)
    taps, c1, depth = kernel.shape
    tiles = -(-c1 // 128)
    px = per * rows * cols // 4
    count = groups * per * (rows // 2) * (colp // 2)
    return pl.pallas_call(
        functools.partial(stage_kernel, groups, per, rows, cols, colp, c1),
        out_shape=[jax.ShapeDtypeStruct((px, depth), F32)]
        + [jax.ShapeDtypeStruct((px, depth), BF16)] * (groups - 1),
        in_specs=[whole()] * (groups + 1),
        out_specs=[whole()] * groups,
        scratch_shapes=[
            pltpu.VMEM((tiles + 2, (rows + 3) * colp + 32, 128), F32),
            pltpu.VMEM((taps, count, c1), BF16),
            pltpu.VMEM((px, depth), F32),
        ],
        name="stage",
        compiler_params=pltpu.CompilerParams(vmem_limit_bytes=12 << 20),
        cost_estimate=pl.CostEstimate(
            flops=2 * count * taps * c1 * depth, bytes_accessed=4 * groups * px * depth, transcendentals=0
        ),
    )(*blocks, kernel)


def body(pixels, first_gain, first_shift, first_kernel, projection, second_gain, second_shift, second_kernel):
    sec = lax.axis_index("section")
    z = lax.axis_index("img")
    ch = lax.axis_index("ch")
    sections = lax.axis_size("section")
    groups = lax.axis_size("img")
    shards = lax.axis_size("ch")
    pairs = shards // 2
    y, core = ch // 2, ch % 2
    per = pixels.shape[0] // sections
    _, rows, cols, depth = pixels.shape
    orows, ocols = rows // 2, cols // 2
    wide = second_gain.shape[0]
    slab = wide // groups
    kc = slab // pairs
    kd = kc // 2
    c1 = depth // groups

    other_kernel = swap(second_kernel, "ch", 1)

    ids = jnp.stack([sec, z, ch, jnp.int32(shards - 1), y, core, z * pairs + y]).astype(jnp.int32)
    colp = -(-(cols + 2) // 16) * 16
    tails = lax.dynamic_slice_in_dim(pixels[:, -1:], sec * per, per, 0)
    heads = lax.dynamic_slice_in_dim(pixels[:, :1], sec * per, per, 0)
    pixels, tails, heads = lax.optimization_barrier((pixels, tails, heads))
    above = lax.ppermute(tails, "ch", [(i, i + 1) for i in range(shards - 1)])
    below = lax.ppermute(heads, "ch", [(i + 1, i) for i in range(shards - 1)])
    packed = pack(
        ids,
        pixels,
        above,
        below,
        first_gain.reshape(1, -1),
        first_shift.reshape(1, -1),
        groups,
        per,
        colp,
    )
    blocks, mean = packed[:groups], packed[groups]
    got = [blocks[0]] + [swap(blocks[k], "img", k) for k in range(1, groups)]

    cuts = cut(ids, projection, groups, shards)
    proj_z = join([cuts[0]] + [swap(cuts[k], "img", k) for k in range(1, groups)])
    proj_own = [proj_z] + [swap(proj_z, "ch", k, 2) for k in range(1, pairs)]
    proj_twin = [swap(part, "ch", 1) for part in proj_own]

    total, *sent = stage(got, first_kernel.reshape(9, c1, depth), per, rows, cols, colp)
    came = [swap(sent[k - 1], "img", k) for k in range(1, groups)]
    pooled = pool(total, mean, came)
    pooled_all = [pooled] + [swap(pooled, "img", k) for k in range(1, groups)]
    px = per * orows * ocols
    imgs = groups * per
    out_px = orows * ocols
    made = project(ids, pooled_all, proj_own, proj_twin)
    back, chip = made[:groups], made[groups:]

    chip = [chip[0]] + [swap(chip[k], "ch", k, 2) for k in range(1, pairs)]
    twin = [swap(chip[0], "ch", 1)]
    twin += [swap(part, "ch", 1) for part in chip[1:]]
    back = [back[0]] + [swap(back[k], "img", k) for k in range(1, groups)]
    w_own = streamed(second_kernel.reshape(9 * kd, wide))
    w_other = streamed(other_kernel.reshape(9 * kd, wide))

    unit = wide // 10
    plan = ((0, 4), (1, 3), (0, 3))
    names = [("ch", 1 << i, 2) for i in range(pairs.bit_length() - 1)]
    names_z = [("img", 1 << i, 1) for i in range(groups.bit_length() - 1)]
    values, first = [], 0
    for j, (kind, n) in enumerate(plan):
        hops = names_z + names if kind else names + names_z
        keys = [(a, b) for a in range(pairs) for b in range(groups)]

        def split(keys, hop):
            axis, k, _ = hop
            bit = [key[0] & k if axis == "ch" else key[1] & k for key in keys]
            rows = ([i for i, x in enumerate(bit) if x], [i for i, x in enumerate(bit) if not x])
            return rows, [key for key, x in zip(keys, bit) if not x]

        rows, keys = split(keys, hops[0])
        if j == 0:
            a_own, a_other, w_own, w_other, sent, kept = unfold(
                ids,
                second_gain.reshape(groups * pairs, kc),
                second_shift.reshape(groups * pairs, kc),
                [c.reshape(imgs, out_px, kc) for c in chip],
                [c.reshape(imgs, out_px, kc) for c in twin],
                ocols,
                w_own,
                w_other,
                first,
                n * unit,
                unit,
                rows,
                px,
            )
        else:
            sent, kept = mix(a_own, a_other, w_own, w_other, first, n * unit, unit, rows, px)
        for h, hop in enumerate(hops):
            axis, k, size = hop
            came = swap(sent, axis, k, size)
            if h + 1 < len(hops):
                rows, keys = split(keys, hops[h + 1])
                sent, kept = merge(kept, came, rows, px)
        values.append((kept, came, first, n * unit))
        first += n * unit

    mine_projected = spread(ids, back)
    far_projected = lax.ppermute(mine_projected, "section", [(1, 0)])
    outs, fars = [], []
    for j, some in enumerate((values[:2], values[2:])):
        outs.append(finish([v[:2] for v in some], mine_projected, some[0][2]))
        fars.append(lax.ppermute(outs[j], "section", [(0, 1)]))
    block = final(ids, mine_projected, far_projected, outs, fars, per, orows, ocols)
    return block.transpose(0, 2, 1, 3)[None]


def solution(mesh):
    placed = (
        P("img", "ch", None, None),
        P(),
        P(),
        P(None, None, "img", None),
        P("img", None),
        P(),
        P(),
        P(None, None, ("img", "ch"), None),
    )

    return jax.shard_map(
        body,
        mesh=mesh,
        in_specs=placed,
        out_specs=P("section", "img", "ch", None, None),
        check_vma=False,
    )
```

```python
import functools

import jax
import jax.numpy as jnp
from jax import lax
from jax.experimental import pallas as pl
from jax.experimental.pallas import tpu as pltpu
from jax.sharding import PartitionSpec as P


BF16 = jnp.bfloat16
F32 = jnp.float32


def swap(array, axis, k, unit=1):
    count = lax.axis_size(axis)
    return lax.ppermute(array, axis, [(i, i ^ (k * unit)) for i in range(count)])


def streamed(array):
    return pltpu.with_memory_space_constraint(array, pltpu.HBM)


def whole(memory_space=pltpu.VMEM):
    return pl.BlockSpec(memory_space=memory_space)


def unfold_kernel(pairs, imgs, ocols, kd, rows, px, first, step, ids, gains, shifts, *refs):
    w_own, w_other = refs[2 * pairs : 2 * pairs + 2]
    a_own, a_other, held_own, held_other, sent, kept = refs[2 * pairs + 2 : 2 * pairs + 8]
    scratch, partial, sems = refs[2 * pairs + 8 : -2], refs[-2], refs[-1]
    pieces = sems.shape[0] // 2
    deep = w_own.shape[0] // pieces
    copies = []
    for i in range(2 * pieces):
        source, target = ((w_own, held_own), (w_other, held_other))[i // pieces]
        if pieces > 1:
            some = pl.ds((i % pieces) * deep, deep)
            source, target = source.at[some], target.at[some]
        copies.append(pltpu.make_async_copy(source, target, sems.at[i]))
        copies[i].start()
    unfold_rows(pairs, imgs, ocols, kd, ids, gains, shifts, *refs[: 2 * pairs], a_own, a_other, *scratch)
    for copy in copies[:pieces]:
        copy.wait()
    count = sent.shape[1]
    cuts = [slice(first + at, first + at + step) for at in range(0, count, step)]
    for i, cut in enumerate(cuts):
        partial[:, i * step : (i + 1) * step] = jnp.dot(a_own[...], held_own[:, cut], preferred_element_type=F32)
    for copy in copies[pieces:]:
        copy.wait()
    for i, cut in enumerate(cuts):
        here = slice(i * step, (i + 1) * step)
        value = partial[:, here] + jnp.dot(a_other[...], held_other[:, cut], preferred_element_type=F32)
        copy_rows(sent.at[:, here], value, rows[0], px)
        copy_rows(kept.at[:, here], value, rows[1], px)


def unfold_rows(pairs, imgs, ocols, kd, ids, gains, shifts, *refs):
    own, other = refs[:pairs], refs[pairs : 2 * pairs]
    out_own, out_other, centre, border, strip = refs[2 * pairs :]
    y, core, group = ids[4], ids[5], ids[6]
    gain, shift = gains[pl.ds(group, 1), :], shifts[pl.ds(group, 1), :]
    px = own[0].shape[1]
    first = core == 0
    base = 24

    def halves(value):
        normed = jax.nn.relu(value.astype(F32) * gain + shift).astype(BF16).astype(F32)
        low, high = normed[:, :kd], normed[:, kd:]
        return jnp.where(first, low, high), jnp.where(first, high, low)

    border[0] = jnp.zeros(border.shape[1:], F32)
    border[pairs + 1] = jnp.zeros(border.shape[1:], F32)
    for k in range(pairs):
        place = jnp.bitwise_xor(y, k)
        for i in range(imgs):
            for half, value in enumerate(halves(own[k][i])):
                centre[place, i, half] = value
            for half, value in enumerate(halves(other[k][i])):
                border[place + 1, i, half, 0] = value[:ocols]
                border[place + 1, i, half, 1] = value[px - ocols :]
    at = lax.broadcasted_iota(jnp.int32, (px, kd), 0) % ocols
    left, right = at == 0, at == ocols - 1
    shift_up = jnp.where(first, 0, 1)
    strip[...] = jnp.zeros(strip.shape, F32)
    for k in range(pairs):
        place = jnp.bitwise_xor(y, k)
        for half, out in enumerate((out_own, out_other)):
            for i in range(0, imgs, 2):
                for m in range(2):
                    strip[m, base : base + px] = centre[place, i + m, half]
                    strip[m, base - ocols : base] = border[place + shift_up, i + m, half, 1]
                    strip[m, base + px : base + px + ocols] = border[place + 1 + shift_up, i + m, half, 0]
                for tap in range(9):
                    dy, dx = tap // 3 - 1, tap % 3 - 1
                    off = base + dy * ocols + dx
                    values = [strip[m, off : off + px] for m in range(2)]
                    if dx == -1:
                        values = [jnp.where(left, 0.0, v) for v in values]
                    if dx == 1:
                        values = [jnp.where(right, 0.0, v) for v in values]
                    row = (k * imgs + i) * px
                    out[row : row + 2 * px, tap * kd : (tap + 1) * kd] = jnp.concatenate(values).astype(BF16)


def unfold(ids, gain, shift, own, other, ocols, w_own, w_other, first, count, step, split, block):
    pairs = len(own)
    imgs, px, kc = own[0].shape
    kd = kc // 2
    rows = pairs * imgs * px
    lanes = -(-kd // 128) * 128
    deep = 9 * kd
    need = 8 * pairs * imgs * px * lanes + 256 * (pairs + 2) * imgs * lanes
    need += 36 * rows * kd + 8 * pairs * imgs * px * lanes
    limit = (4 << 20) + need + need // 4 + 8 * rows * count
    pieces = 3 if deep % 24 == 0 else 1
    sizes = [len(r) * block for r in split]
    return pl.pallas_call(
        functools.partial(unfold_kernel, pairs, imgs, ocols, kd, split, block, first, step),
        out_shape=[pltpu.VMEM((rows, deep), BF16)] * 2
        + [pltpu.VMEM(w_own.shape, BF16)] * 2
        + [
            jax.ShapeDtypeStruct((sizes[0], count), BF16),
            jax.ShapeDtypeStruct((sizes[1], count), F32),
        ],
        in_specs=[whole(pltpu.SMEM)]
        + [whole()] * (2 + 2 * pairs)
        + [pl.BlockSpec(memory_space=pltpu.HBM)] * 2,
        out_specs=[whole()] * 6,
        scratch_shapes=[
            pltpu.VMEM((pairs, imgs, 2, px, kd), F32),
            pltpu.VMEM((pairs + 2, imgs, 2, 2, ocols, kd), F32),
            pltpu.VMEM((2, 24 + px + 24, kd), F32),
            pltpu.VMEM((rows, count), F32),
            pltpu.SemaphoreType.DMA((2 * pieces,)),
        ],
        name="unfold",
        compiler_params=pltpu.CompilerParams(vmem_limit_bytes=min(60 << 20, limit)),
        cost_estimate=pl.CostEstimate(
            flops=4 * rows * deep * count, bytes_accessed=8 * deep * w_own.shape[1], transcendentals=0
        ),
    )(ids, gain, shift, *own, *other, w_own, w_other)


def copy_rows(out, value, rows, px):
    for i, row in enumerate(rows):
        out[i * px : (i + 1) * px, :] = value[row * px : (row + 1) * px].astype(out.dtype)


def mix_kernel(rows, px, first, step, a_own, a_other, w_own, w_other, sent, kept):
    for at in range(0, sent.shape[1], step):
        cut = slice(first + at, first + at + step)
        value = jnp.dot(a_own[...], w_own[:, cut], preferred_element_type=F32)
        value = value + jnp.dot(a_other[...], w_other[:, cut], preferred_element_type=F32)
        here = slice(at, at + step)
        copy_rows(sent.at[:, here], value, rows[0], px)
        copy_rows(kept.at[:, here], value, rows[1], px)


def mix(a_own, a_other, w_own, w_other, first, count, step, rows, px):
    total, deep = a_own.shape
    sizes = [len(r) * px for r in rows]
    return pl.pallas_call(
        functools.partial(mix_kernel, rows, px, first, step),
        out_shape=[
            jax.ShapeDtypeStruct((sizes[0], count), BF16),
            jax.ShapeDtypeStruct((sizes[1], count), F32),
        ],
        in_specs=[whole()] * 4,
        out_specs=[whole()] * 2,
        name="mix",
        compiler_params=pltpu.CompilerParams(vmem_limit_bytes=12 << 20),
        cost_estimate=pl.CostEstimate(
            flops=4 * total * deep * count, bytes_accessed=3 * total * count, transcendentals=0
        ),
    )(a_own, a_other, w_own, w_other)


def merge_kernel(rows, px, kept, came, *outs):
    value = kept[...] + came[...].astype(F32)
    for out, some in zip(outs, rows):
        copy_rows(out, value, some, px)


def merge(kept, came, rows, px):
    count = kept.shape[1]
    return pl.pallas_call(
        functools.partial(merge_kernel, rows, px),
        out_shape=[jax.ShapeDtypeStruct((len(r) * px, count), t) for r, t in zip(rows, (BF16, F32))],
        in_specs=[whole()] * 2,
        out_specs=[whole()] * 2,
        name="merge",
        compiler_params=pltpu.CompilerParams(vmem_limit_bytes=10 << 20),
        cost_estimate=pl.CostEstimate(flops=kept.size, bytes_accessed=10 * kept.size, transcendentals=0),
    )(kept, came)


def finish_kernel(first, count, *refs):
    extra, out = refs[2 * count :]
    at = 0
    for i in range(count):
        kept, came = refs[2 * i : 2 * i + 2]
        n = kept.shape[1]
        value = kept[...] + came[...].astype(F32) + extra[:, first + at : first + at + n].astype(F32)
        out[:, at : at + n] = value.astype(BF16)
        at += n


def finish(parts, extra, first):
    flat = [array for part in parts for array in part]
    px = flat[0].shape[0]
    wide = sum(part[0].shape[1] for part in parts)
    return pl.pallas_call(
        functools.partial(finish_kernel, first, len(parts)),
        out_shape=jax.ShapeDtypeStruct((px, wide), BF16),
        in_specs=[whole()] * (2 * len(parts) + 1),
        out_specs=whole(),
        name="finish",
        compiler_params=pltpu.CompilerParams(vmem_limit_bytes=6 << 20),
        cost_estimate=pl.CostEstimate(flops=2 * px * wide, bytes_accessed=10 * px * wide, transcendentals=0),
    )(*flat, extra)


def pool_kernel(total, mean, *refs):
    value = total[...] + mean[...].reshape(total.shape)
    for ref in refs[:-1]:
        value = value + ref[...].astype(F32)
    refs[-1][...] = value.astype(BF16)


def pool(total, mean, came):
    return pl.pallas_call(
        pool_kernel,
        out_shape=jax.ShapeDtypeStruct(total.shape, BF16),
        in_specs=[whole()] * (2 + len(came)),
        out_specs=whole(),
        name="pool",
        compiler_params=pltpu.CompilerParams(vmem_limit_bytes=4 << 20),
    )(total, mean, *came)


def join_kernel(*refs):
    for i, ref in enumerate(refs[:-1]):
        refs[-1][i] = ref[...]


def join(parts):
    return pl.pallas_call(
        join_kernel,
        out_shape=jax.ShapeDtypeStruct((len(parts),) + parts[0].shape, parts[0].dtype),
        in_specs=[whole()] * len(parts),
        out_specs=whole(),
        name="join",
        compiler_params=pltpu.CompilerParams(vmem_limit_bytes=6 << 20),
    )(*parts)


def project_kernel(groups, pairs, ids, *refs):
    pooled = refs[:groups]
    own, twin = refs[groups : groups + pairs], refs[groups + pairs : groups + 2 * pairs]
    backs = refs[groups + 2 * pairs : 2 * groups + 2 * pairs]
    parts = refs[2 * groups + 2 * pairs : 2 * groups + 3 * pairs]
    weight, held = refs[2 * groups + 3 * pairs :]
    z, y, core = ids[1], ids[4], ids[5]
    px, depth = pooled[0].shape
    for k in range(groups):
        for j in range(pairs):
            for half, source in enumerate((own, twin)):
                place = (jnp.bitwise_xor(z, k) * pairs + jnp.bitwise_xor(y, j)) * 2 + jnp.bitwise_xor(core, half)
                weight[place] = source[j][k].astype(F32)
    slab = weight[...].reshape(depth, weight.shape[2]).astype(BF16)
    kc = weight.shape[2] // pairs
    rows = jnp.concatenate([ref[...].astype(F32) for ref in pooled]).astype(BF16)
    value = jnp.dot(rows, slab, preferred_element_type=F32)
    for k in range(groups):
        backs[k][...] = value[k * px : (k + 1) * px].astype(BF16)
    for j in range(pairs):
        held[j] = value[:, j * kc : (j + 1) * kc].astype(BF16)
    for j in range(pairs):
        parts[j][...] = held[jnp.bitwise_xor(y, j)]


def project(ids, pooled, own, twin):
    groups, pairs = len(pooled), len(own)
    px, depth = pooled[0].shape
    _, deep, slab = own[0].shape
    kc = slab // pairs
    back = jax.ShapeDtypeStruct((px, slab), BF16)
    part = jax.ShapeDtypeStruct((groups * px, kc), BF16)
    return pl.pallas_call(
        functools.partial(project_kernel, groups, pairs),
        out_shape=[back] * groups + [part] * pairs,
        in_specs=[whole(pltpu.SMEM)] + [whole()] * (groups + 2 * pairs),
        out_specs=[whole()] * (groups + pairs),
        scratch_shapes=[
            pltpu.VMEM((groups * pairs * 2, deep, slab), F32),
            pltpu.VMEM((pairs, groups * px, kc), BF16),
        ],
        name="project",
        compiler_params=pltpu.CompilerParams(vmem_limit_bytes=14 << 20),
        cost_estimate=pl.CostEstimate(
            flops=2 * groups * px * depth * slab, bytes_accessed=4 * depth * slab, transcendentals=0
        ),
    )(ids, *pooled, *own, *twin)


def packing(rows, colp, c1):
    main = c1 // 128
    rest = c1 - main * 128
    fit = 128 // rest if rest else 1
    deep = -(-rows // fit) if rest else 0
    return main, rest, deep, main * rows * colp + deep * colp


def cut_kernel(ids, projection, *refs):
    cuts, strip = refs[:-1], refs[-1]
    z, ch = ids[1], ids[2]
    deep, slab = cuts[0].shape
    groups = len(cuts)
    for i in range(projection.shape[0] // deep):
        for g in range(groups):
            strip[i, g] = projection[i * deep : (i + 1) * deep, g * slab : (g + 1) * slab].astype(F32)
    for k in range(groups):
        cuts[k][...] = strip[ch, jnp.bitwise_xor(z, k)].astype(BF16)


def cut(ids, projection, groups, shards):
    deep, slab = projection.shape[0] // shards, projection.shape[1] // groups
    return pl.pallas_call(
        cut_kernel,
        out_shape=[jax.ShapeDtypeStruct((deep, slab), BF16)] * groups,
        in_specs=[whole(pltpu.SMEM), whole()],
        out_specs=[whole()] * groups,
        scratch_shapes=[pltpu.VMEM((shards, groups, deep, slab), F32)],
        name="cut",
        compiler_params=pltpu.CompilerParams(vmem_limit_bytes=8 << 20),
    )(ids, projection)


def spread_kernel(groups, ids, *refs):
    backs, out, held = refs[:groups], refs[groups], refs[groups + 1]
    slab = backs[0].shape[1]
    for k in range(groups):
        held[jnp.bitwise_xor(ids[1], k)] = backs[k][...]
    for g in range(groups):
        out[:, g * slab : (g + 1) * slab] = held[g]


def spread(ids, backs):
    px, slab = backs[0].shape
    groups = len(backs)
    return pl.pallas_call(
        functools.partial(spread_kernel, groups),
        out_shape=jax.ShapeDtypeStruct((px, groups * slab), BF16),
        in_specs=[whole(pltpu.SMEM)] + [whole()] * groups,
        out_specs=whole(),
        scratch_shapes=[pltpu.VMEM((groups, px, slab), BF16)],
        name="spread",
        compiler_params=pltpu.CompilerParams(vmem_limit_bytes=6 << 20),
    )(ids, *backs)


def final_kernel(parts, per, orows, ocols, ids, mine, far_mine, *refs):
    own, far = refs[:parts], refs[parts : 2 * parts]
    out, held = refs[2 * parts :]
    first = ids[0] == 0
    for half in range(2):
        at = 0
        for i in range(parts):
            count = own[i].shape[1]
            for lane in range(0, count, 128):
                here = slice(lane, lane + 128)
                there = slice(at + lane, at + lane + 128)
                a = mine[:, there] if half == 0 else far_mine[:, there]
                b = far[i][:, here] if half == 0 else own[i][:, here]
                held[...] = jnp.where(first, a.astype(F32), b.astype(F32))
                for p in range(per):
                    for c in range(ocols):
                        some = held[pl.ds(p * orows * ocols + c, orows, stride=ocols), :]
                        out[half * per + p, c, :, there] = some.astype(BF16)
            at += count


def final(ids, mine, far_mine, own, far, per, orows, ocols):
    wide = mine.shape[1]
    return pl.pallas_call(
        functools.partial(final_kernel, len(own), per, orows, ocols),
        out_shape=jax.ShapeDtypeStruct((2 * per, ocols, orows, wide), BF16),
        in_specs=[whole(pltpu.SMEM)] + [whole()] * (2 + 2 * len(own)),
        out_specs=whole(),
        scratch_shapes=[pltpu.VMEM((mine.shape[0], 128), F32)],
        name="final",
        compiler_params=pltpu.CompilerParams(vmem_limit_bytes=10 << 20),
    )(ids, mine, far_mine, *own, *far)


def pack_kernel(groups, per, c1, colp, ids, pixels, above, below, gain, shift, *refs):
    outs, mean = refs[:groups], refs[groups]
    held, pair = refs[groups + 1 :]
    sec, z, ch, last = ids[0], ids[1], ids[2], ids[3]
    _, rows, cols, depth = pixels.shape
    main, rest, deep, size = packing(rows + 2, colp, c1)
    scale, offset = gain[...], shift[...]
    filler = jnp.zeros((colp - cols, depth), F32)
    for p in range(per):
        for r in range(rows + 2):
            if r == 0:
                value = above[p, 0].astype(F32)
            elif r == rows + 1:
                value = below[p, 0].astype(F32)
            else:
                value = pixels[sec * per + p, r - 1].astype(F32)
            if 1 <= r <= rows:
                i, half = (r - 1) // 2, cols // 2
                for t in range(depth // 128):
                    lanes = slice(t * 128, (t + 1) * 128)
                    if r % 2 == 1:
                        pair[t] = value[:, lanes]
                    else:
                        pair[t] = pair[t] + value[:, lanes]
                        both = pair.at[t]
                        total = both[pl.ds(0, half, stride=2), :] + both[pl.ds(1, half, stride=2), :]
                        mean[p, i * half : (i + 1) * half, lanes] = total * 0.25
            value = jax.nn.relu(value * scale + offset)
            if r == 0:
                value = jnp.where(ch == 0, 0.0, value)
            if r == rows + 1:
                value = jnp.where(ch == last, 0.0, value)
            value = jnp.concatenate([value, filler]).astype(BF16)
            for g in range(groups):
                for m in range(main):
                    at = p * size + (m * (rows + 2) + r) * colp
                    lane = g * c1 + m * 128
                    held[g, at : at + colp, :] = value[:, lane : lane + 128]
                if rest:
                    at = p * size + main * (rows + 2) * colp + (r % deep) * colp
                    lane = g * c1 + main * 128
                    into = (r // deep) * rest
                    held[g, at : at + colp, into : into + rest] = value[:, lane : lane + rest]
    for k in range(groups):
        outs[k][...] = held[jnp.bitwise_xor(z, k)]


def pack(ids, pixels, above, below, gain, shift, groups, per, colp):
    _, rows, cols, depth = pixels.shape
    c1 = depth // groups
    size = packing(rows + 2, colp, c1)[3]
    block = jax.ShapeDtypeStruct((per * size, 128), BF16)
    half = jax.ShapeDtypeStruct((per, rows * cols // 4, depth), F32)
    return pl.pallas_call(
        functools.partial(pack_kernel, groups, per, c1, colp),
        out_shape=[block] * groups + [half],
        in_specs=[whole(pltpu.SMEM)] + [whole()] * 5,
        out_specs=[whole()] * (groups + 1),
        scratch_shapes=[
            pltpu.VMEM((groups, per * size, 128), BF16),
            pltpu.VMEM((depth // 128, cols, 128), F32),
        ],
        name="pack",
        compiler_params=pltpu.CompilerParams(vmem_limit_bytes=14 << 20),
        cost_estimate=pl.CostEstimate(
            flops=4 * rows * cols * depth, bytes_accessed=6 * rows * cols * depth, transcendentals=0
        ),
    )(ids, pixels, above, below, gain, shift)


def stage_kernel(groups, per, rows, cols, colp, c1, *refs):
    blocks, source = refs[:groups], refs[groups]
    outs = refs[groups + 1 : 2 * groups + 1]
    flat, taps, squeezed, kernel, sem = refs[2 * groups + 1 :]
    load = pltpu.make_async_copy(source, kernel, sem)
    load.start()
    main, rest, deep, size = packing(rows + 2, colp, c1)
    tiles = main + (1 if rest else 0)
    orows, ocols = rows // 2, cols // 2
    base, wide = 8, (rows + 2) * colp
    half = colp // 2
    flat[...] = jnp.zeros(flat.shape, F32)
    for k in range(groups):
        for p in range(per):
            for t in range(tiles):
                lanes = 128 if t < main else rest
                if t < main:
                    at = p * size + t * wide
                    flat[t, base : base + wide, :] = blocks[k][at : at + wide, :].astype(F32)
                else:
                    for r in range(rows + 2):
                        at = p * size + main * wide + (r % deep) * colp
                        lane = (r // deep) * rest
                        flat[t, base + r * colp : base + (r + 1) * colp, 0:rest] = blocks[k][
                            at : at + colp, lane : lane + rest
                        ].astype(F32)
                span = (rows + 1) * colp + base + 8
                tall = flat[t, 0:span, :] + flat[t, colp : colp + span, :]
                flat[tiles, 0:span, :] = tall
                both = flat[tiles, 0 : span - 8, :] + flat[tiles, 1 : span - 7, :]
                flat[tiles + 1, 0 : span - 8, :] = both * 0.25
                plane = flat.at[tiles + 1]
                for tap in range(9):
                    ty, tx = tap // 3, tap % 3
                    for i in range(orows):
                        q = base + (2 * i + ty) * colp + tx - 1
                        value = plane[pl.ds(q, half, stride=2), :].astype(BF16)
                        row = ((k * per + p) * orows + i) * half
                        taps[tap, row : row + half, t * 128 : t * 128 + lanes] = value[:, :lanes]
    load.wait()
    total = jnp.dot(taps[0], kernel[0], preferred_element_type=F32)
    for tap in range(1, 9):
        total = total + jnp.dot(taps[tap], kernel[tap], preferred_element_type=F32)
    for k in range(groups):
        for p in range(per):
            for i in range(orows):
                row = ((k * per + p) * orows + i) * half
                at = (p * orows + i) * ocols
                squeezed[at : at + ocols, :] = total[row : row + ocols]
        outs[k][...] = squeezed[...].astype(outs[k].dtype)


def stage(blocks, kernel, per, rows, cols, colp):
    groups = len(blocks)
    taps, c1, depth = kernel.shape
    tiles = -(-c1 // 128)
    px = per * rows * cols // 4
    count = groups * per * (rows // 2) * (colp // 2)
    return pl.pallas_call(
        functools.partial(stage_kernel, groups, per, rows, cols, colp, c1),
        out_shape=[jax.ShapeDtypeStruct((px, depth), F32)]
        + [jax.ShapeDtypeStruct((px, depth), BF16)] * (groups - 1),
        in_specs=[whole()] * groups + [pl.BlockSpec(memory_space=pltpu.HBM)],
        out_specs=[whole()] * groups,
        scratch_shapes=[
            pltpu.VMEM((tiles + 2, (rows + 3) * colp + 32, 128), F32),
            pltpu.VMEM((taps, count, c1), BF16),
            pltpu.VMEM((px, depth), F32),
            pltpu.VMEM(kernel.shape, BF16),
            pltpu.SemaphoreType.DMA,
        ],
        name="stage",
        compiler_params=pltpu.CompilerParams(vmem_limit_bytes=12 << 20),
        cost_estimate=pl.CostEstimate(
            flops=2 * count * taps * c1 * depth, bytes_accessed=4 * groups * px * depth, transcendentals=0
        ),
    )(*blocks, streamed(kernel))


def body(pixels, first_gain, first_shift, first_kernel, projection, second_gain, second_shift, second_kernel):
    sec = lax.axis_index("section")
    z = lax.axis_index("img")
    ch = lax.axis_index("ch")
    sections = lax.axis_size("section")
    groups = lax.axis_size("img")
    shards = lax.axis_size("ch")
    pairs = shards // 2
    y, core = ch // 2, ch % 2
    per = pixels.shape[0] // sections
    _, rows, cols, depth = pixels.shape
    orows, ocols = rows // 2, cols // 2
    wide = second_gain.shape[0]
    slab = wide // groups
    kc = slab // pairs
    kd = kc // 2
    c1 = depth // groups

    other_kernel = swap(second_kernel, "ch", 1)

    ids = jnp.stack([sec, z, ch, jnp.int32(shards - 1), y, core, z * pairs + y]).astype(jnp.int32)
    colp = -(-(cols + 2) // 16) * 16
    tails = lax.dynamic_slice_in_dim(pixels[:, -1:], sec * per, per, 0)
    heads = lax.dynamic_slice_in_dim(pixels[:, :1], sec * per, per, 0)
    pixels, tails, heads = lax.optimization_barrier((pixels, tails, heads))
    above = lax.ppermute(tails, "ch", [(i, i + 1) for i in range(shards - 1)])
    below = lax.ppermute(heads, "ch", [(i + 1, i) for i in range(shards - 1)])
    packed = pack(
        ids,
        pixels,
        above,
        below,
        first_gain.reshape(1, -1),
        first_shift.reshape(1, -1),
        groups,
        per,
        colp,
    )
    blocks, mean = packed[:groups], packed[groups]
    got = [blocks[0]] + [swap(blocks[k], "img", k) for k in range(1, groups)]

    cuts = cut(ids, projection, groups, shards)
    proj_z = join([cuts[0]] + [swap(cuts[k], "img", k) for k in range(1, groups)])
    proj_own = [proj_z] + [swap(proj_z, "ch", k, 2) for k in range(1, pairs)]
    proj_twin = [swap(part, "ch", 1) for part in proj_own]

    total, *sent = stage(got, first_kernel.reshape(9, c1, depth), per, rows, cols, colp)
    came = [swap(sent[k - 1], "img", k) for k in range(1, groups)]
    pooled = pool(total, mean, came)
    pooled_all = [pooled] + [swap(pooled, "img", k) for k in range(1, groups)]
    px = per * orows * ocols
    imgs = groups * per
    out_px = orows * ocols
    made = project(ids, pooled_all, proj_own, proj_twin)
    back, chip = made[:groups], made[groups:]

    chip = [chip[0]] + [swap(chip[k], "ch", k, 2) for k in range(1, pairs)]
    twin = [swap(chip[0], "ch", 1)]
    twin += [swap(part, "ch", 1) for part in chip[1:]]
    back = [back[0]] + [swap(back[k], "img", k) for k in range(1, groups)]
    w_own = streamed(second_kernel.reshape(9 * kd, wide))
    w_other = streamed(other_kernel.reshape(9 * kd, wide))

    unit = wide // 10
    plan = ((0, 4, 0), (1, 4, 6), (0, 2, 4))
    names = [("ch", 1 << i, 2) for i in range(pairs.bit_length() - 1)]
    names_z = [("img", 1 << i, 1) for i in range(groups.bit_length() - 1)]
    values = []
    for j, (kind, n, first) in enumerate(plan):
        first *= unit
        hops = names_z + names if kind else names + names_z
        keys = [(a, b) for a in range(pairs) for b in range(groups)]

        def split(keys, hop):
            axis, k, _ = hop
            bit = [key[0] & k if axis == "ch" else key[1] & k for key in keys]
            rows = ([i for i, x in enumerate(bit) if x], [i for i, x in enumerate(bit) if not x])
            return rows, [key for key, x in zip(keys, bit) if not x]

        rows, keys = split(keys, hops[0])
        if j == 0:
            a_own, a_other, w_own, w_other, sent, kept = unfold(
                ids,
                second_gain.reshape(groups * pairs, kc),
                second_shift.reshape(groups * pairs, kc),
                [c.reshape(imgs, out_px, kc) for c in chip],
                [c.reshape(imgs, out_px, kc) for c in twin],
                ocols,
                w_own,
                w_other,
                first,
                n * unit,
                unit,
                rows,
                px,
            )
        else:
            sent, kept = mix(a_own, a_other, w_own, w_other, first, n * unit, unit, rows, px)
        for h, hop in enumerate(hops):
            axis, k, size = hop
            came = swap(sent, axis, k, size)
            if h + 1 < len(hops):
                rows, keys = split(keys, hops[h + 1])
                sent, kept = merge(kept, came, rows, px)
        values.append((kept, came, first, n * unit))

    mine_projected = spread(ids, back)
    far_projected = lax.ppermute(mine_projected, "section", [(1, 0)])
    outs, fars = [], []
    for j, some in enumerate(([values[0], values[2]], [values[1]])):
        outs.append(finish([v[:2] for v in some], mine_projected, some[0][2]))
        fars.append(lax.ppermute(outs[j], "section", [(0, 1)]))
    block = final(ids, mine_projected, far_projected, outs, fars, per, orows, ocols)
    return block.transpose(0, 2, 1, 3)[None]


def solution(mesh):
    placed = (
        P("img", "ch", None, None),
        P(),
        P(),
        P(None, None, "img", None),
        P("img", None),
        P(),
        P(),
        P(None, None, ("img", "ch"), None),
    )

    return jax.shard_map(
        body,
        mesh=mesh,
        in_specs=placed,
        out_specs=P("section", "img", "ch", None, None),
        check_vma=False,
    )
```

```python
import functools

import jax
import jax.numpy as jnp
from jax import lax
from jax.experimental import pallas as pl
from jax.experimental.pallas import tpu as pltpu
from jax.sharding import PartitionSpec as P


BF16 = jnp.bfloat16
F32 = jnp.float32


def swap(array, axis, k, unit=1):
    count = lax.axis_size(axis)
    return lax.ppermute(array, axis, [(i, i ^ (k * unit)) for i in range(count)])


def streamed(array):
    return pltpu.with_memory_space_constraint(array, pltpu.HBM)


def whole(memory_space=pltpu.VMEM):
    return pl.BlockSpec(memory_space=memory_space)


def unfold_kernel(pairs, imgs, ocols, kd, rows, px, first, step, ids, gains, shifts, *refs):
    w_own, w_other = refs[2 * pairs : 2 * pairs + 2]
    a_own, a_other, held_own, held_other, sent, kept = refs[2 * pairs + 2 : 2 * pairs + 8]
    scratch, partial, sems = refs[2 * pairs + 8 : -2], refs[-2], refs[-1]
    bounds = row_pieces(w_own.shape[0])
    pieces = len(bounds)
    copies = []
    for i in range(2 * pieces):
        source, target = ((w_own, held_own), (w_other, held_other))[i // pieces]
        if pieces > 1:
            low, high = bounds[i % pieces]
            source, target = source.at[pl.ds(low, high - low)], target.at[pl.ds(low, high - low)]
        copies.append(pltpu.make_async_copy(source, target, sems.at[i]))
        copies[i].start()
    unfold_rows(pairs, imgs, ocols, kd, ids, gains, shifts, *refs[: 2 * pairs], a_own, a_other, *scratch)
    for copy in copies[:pieces]:
        copy.wait()
    count = sent.shape[1]
    for at in range(0, count, step):
        cut = slice(first + at, first + at + step)
        partial[:, at : at + step] = jnp.dot(a_own[...], held_own[:, cut], preferred_element_type=F32)
    for i, (low, high) in enumerate(bounds):
        copies[pieces + i].wait()
        for at in range(0, count, step):
            here, cut = slice(at, at + step), slice(first + at, first + at + step)
            more = jnp.dot(a_other[:, low:high], held_other[low:high, cut], preferred_element_type=F32)
            if i + 1 < pieces:
                partial[:, here] = partial[:, here] + more
            else:
                value = partial[:, here] + more
                copy_rows(sent.at[:, here], value, rows[0], px)
                copy_rows(kept.at[:, here], value, rows[1], px)


def row_pieces(deep):
    size = 512 if deep % 8 == 0 else deep
    return [(low, min(low + size, deep)) for low in range(0, deep, size)]


def unfold_rows(pairs, imgs, ocols, kd, ids, gains, shifts, *refs):
    own, other = refs[:pairs], refs[pairs : 2 * pairs]
    out_own, out_other, centre, border, strip = refs[2 * pairs :]
    y, core, group = ids[4], ids[5], ids[6]
    gain, shift = gains[pl.ds(group, 1), :], shifts[pl.ds(group, 1), :]
    px = own[0].shape[1]
    first = core == 0
    base = 24

    def halves(value):
        normed = jax.nn.relu(value.astype(F32) * gain + shift).astype(BF16).astype(F32)
        low, high = normed[:, :kd], normed[:, kd:]
        return jnp.where(first, low, high), jnp.where(first, high, low)

    border[0] = jnp.zeros(border.shape[1:], F32)
    border[pairs + 1] = jnp.zeros(border.shape[1:], F32)
    for k in range(pairs):
        place = jnp.bitwise_xor(y, k)
        for i in range(imgs):
            for half, value in enumerate(halves(own[k][i])):
                centre[place, i, half] = value
            for half, value in enumerate(halves(other[k][i])):
                border[place + 1, i, half, 0] = value[:ocols]
                border[place + 1, i, half, 1] = value[px - ocols :]
    at = lax.broadcasted_iota(jnp.int32, (px, kd), 0) % ocols
    left, right = at == 0, at == ocols - 1
    shift_up = jnp.where(first, 0, 1)
    strip[...] = jnp.zeros(strip.shape, F32)
    for k in range(pairs):
        place = jnp.bitwise_xor(y, k)
        for half, out in enumerate((out_own, out_other)):
            for i in range(0, imgs, 2):
                for m in range(2):
                    strip[m, base : base + px] = centre[place, i + m, half]
                    strip[m, base - ocols : base] = border[place + shift_up, i + m, half, 1]
                    strip[m, base + px : base + px + ocols] = border[place + 1 + shift_up, i + m, half, 0]
                for tap in range(9):
                    dy, dx = tap // 3 - 1, tap % 3 - 1
                    off = base + dy * ocols + dx
                    values = [strip[m, off : off + px] for m in range(2)]
                    if dx == -1:
                        values = [jnp.where(left, 0.0, v) for v in values]
                    if dx == 1:
                        values = [jnp.where(right, 0.0, v) for v in values]
                    row = (k * imgs + i) * px
                    out[row : row + 2 * px, tap * kd : (tap + 1) * kd] = jnp.concatenate(values).astype(BF16)


def unfold(ids, gain, shift, own, other, ocols, w_own, w_other, first, count, step, split, block):
    pairs = len(own)
    imgs, px, kc = own[0].shape
    kd = kc // 2
    rows = pairs * imgs * px
    lanes = -(-kd // 128) * 128
    deep = 9 * kd
    need = 8 * pairs * imgs * px * lanes + 256 * (pairs + 2) * imgs * lanes
    need += 36 * rows * kd + 8 * pairs * imgs * px * lanes
    limit = (4 << 20) + need + need // 4 + 8 * rows * count
    pieces = len(row_pieces(deep))
    sizes = [len(r) * block for r in split]
    return pl.pallas_call(
        functools.partial(unfold_kernel, pairs, imgs, ocols, kd, split, block, first, step),
        out_shape=[pltpu.VMEM((rows, deep), BF16)] * 2
        + [pltpu.VMEM(w_own.shape, BF16)] * 2
        + [
            jax.ShapeDtypeStruct((sizes[0], count), BF16),
            jax.ShapeDtypeStruct((sizes[1], count), F32),
        ],
        in_specs=[whole(pltpu.SMEM)]
        + [whole()] * (2 + 2 * pairs)
        + [pl.BlockSpec(memory_space=pltpu.HBM)] * 2,
        out_specs=[whole()] * 6,
        scratch_shapes=[
            pltpu.VMEM((pairs, imgs, 2, px, kd), F32),
            pltpu.VMEM((pairs + 2, imgs, 2, 2, ocols, kd), F32),
            pltpu.VMEM((2, 24 + px + 24, kd), F32),
            pltpu.VMEM((rows, count), F32),
            pltpu.SemaphoreType.DMA((2 * pieces,)),
        ],
        name="unfold",
        compiler_params=pltpu.CompilerParams(vmem_limit_bytes=min(60 << 20, limit)),
        cost_estimate=pl.CostEstimate(
            flops=4 * rows * deep * count, bytes_accessed=8 * deep * w_own.shape[1], transcendentals=0
        ),
    )(ids, gain, shift, *own, *other, w_own, w_other)


def copy_rows(out, value, rows, px):
    for i, row in enumerate(rows):
        out[i * px : (i + 1) * px, :] = value[row * px : (row + 1) * px].astype(out.dtype)


def mix_kernel(rows, px, first, step, a_own, a_other, w_own, w_other, sent, kept):
    for at in range(0, sent.shape[1], step):
        cut = slice(first + at, first + at + step)
        value = jnp.dot(a_own[...], w_own[:, cut], preferred_element_type=F32)
        value = value + jnp.dot(a_other[...], w_other[:, cut], preferred_element_type=F32)
        here = slice(at, at + step)
        copy_rows(sent.at[:, here], value, rows[0], px)
        copy_rows(kept.at[:, here], value, rows[1], px)


def mix(a_own, a_other, w_own, w_other, first, count, step, rows, px):
    total, deep = a_own.shape
    sizes = [len(r) * px for r in rows]
    return pl.pallas_call(
        functools.partial(mix_kernel, rows, px, first, step),
        out_shape=[
            jax.ShapeDtypeStruct((sizes[0], count), BF16),
            jax.ShapeDtypeStruct((sizes[1], count), F32),
        ],
        in_specs=[whole()] * 4,
        out_specs=[whole()] * 2,
        name="mix",
        compiler_params=pltpu.CompilerParams(vmem_limit_bytes=12 << 20),
        cost_estimate=pl.CostEstimate(
            flops=4 * total * deep * count, bytes_accessed=3 * total * count, transcendentals=0
        ),
    )(a_own, a_other, w_own, w_other)


def merge_kernel(rows, px, kept, came, *outs):
    value = kept[...] + came[...].astype(F32)
    for out, some in zip(outs, rows):
        copy_rows(out, value, some, px)


def merge(kept, came, rows, px):
    count = kept.shape[1]
    return pl.pallas_call(
        functools.partial(merge_kernel, rows, px),
        out_shape=[jax.ShapeDtypeStruct((len(r) * px, count), t) for r, t in zip(rows, (BF16, F32))],
        in_specs=[whole()] * 2,
        out_specs=[whole()] * 2,
        name="merge",
        compiler_params=pltpu.CompilerParams(vmem_limit_bytes=10 << 20),
        cost_estimate=pl.CostEstimate(flops=kept.size, bytes_accessed=10 * kept.size, transcendentals=0),
    )(kept, came)


def finish_kernel(first, count, *refs):
    extra, out = refs[2 * count :]
    at = 0
    for i in range(count):
        kept, came = refs[2 * i : 2 * i + 2]
        n = kept.shape[1]
        value = kept[...] + came[...].astype(F32) + extra[:, first + at : first + at + n].astype(F32)
        out[:, at : at + n] = value.astype(BF16)
        at += n


def finish(parts, extra, first):
    flat = [array for part in parts for array in part]
    px = flat[0].shape[0]
    wide = sum(part[0].shape[1] for part in parts)
    return pl.pallas_call(
        functools.partial(finish_kernel, first, len(parts)),
        out_shape=jax.ShapeDtypeStruct((px, wide), BF16),
        in_specs=[whole()] * (2 * len(parts) + 1),
        out_specs=whole(),
        name="finish",
        compiler_params=pltpu.CompilerParams(vmem_limit_bytes=6 << 20),
        cost_estimate=pl.CostEstimate(flops=2 * px * wide, bytes_accessed=10 * px * wide, transcendentals=0),
    )(*flat, extra)


def pool_kernel(total, mean, *refs):
    value = total[...] + mean[...].reshape(total.shape)
    for ref in refs[:-1]:
        value = value + ref[...].astype(F32)
    refs[-1][...] = value.astype(BF16)


def pool(total, mean, came):
    return pl.pallas_call(
        pool_kernel,
        out_shape=jax.ShapeDtypeStruct(total.shape, BF16),
        in_specs=[whole()] * (2 + len(came)),
        out_specs=whole(),
        name="pool",
        compiler_params=pltpu.CompilerParams(vmem_limit_bytes=4 << 20),
    )(total, mean, *came)


def join_kernel(*refs):
    for i, ref in enumerate(refs[:-1]):
        refs[-1][i] = ref[...]


def join(parts):
    return pl.pallas_call(
        join_kernel,
        out_shape=jax.ShapeDtypeStruct((len(parts),) + parts[0].shape, parts[0].dtype),
        in_specs=[whole()] * len(parts),
        out_specs=whole(),
        name="join",
        compiler_params=pltpu.CompilerParams(vmem_limit_bytes=6 << 20),
    )(*parts)


def project_kernel(groups, pairs, ids, *refs):
    pooled = refs[:groups]
    own, twin = refs[groups : groups + pairs], refs[groups + pairs : groups + 2 * pairs]
    backs = refs[groups + 2 * pairs : 2 * groups + 2 * pairs]
    parts = refs[2 * groups + 2 * pairs : 2 * groups + 3 * pairs]
    weight, held = refs[2 * groups + 3 * pairs :]
    z, y, core = ids[1], ids[4], ids[5]
    px, depth = pooled[0].shape
    for k in range(groups):
        for j in range(pairs):
            for half, source in enumerate((own, twin)):
                place = (jnp.bitwise_xor(z, k) * pairs + jnp.bitwise_xor(y, j)) * 2 + jnp.bitwise_xor(core, half)
                weight[place] = source[j][k].astype(F32)
    slab = weight[...].reshape(depth, weight.shape[2]).astype(BF16)
    kc = weight.shape[2] // pairs
    rows = jnp.concatenate([ref[...].astype(F32) for ref in pooled]).astype(BF16)
    value = jnp.dot(rows, slab, preferred_element_type=F32)
    for k in range(groups):
        backs[k][...] = value[k * px : (k + 1) * px].astype(BF16)
    for j in range(pairs):
        held[j] = value[:, j * kc : (j + 1) * kc].astype(BF16)
    for j in range(pairs):
        parts[j][...] = held[jnp.bitwise_xor(y, j)]


def project(ids, pooled, own, twin):
    groups, pairs = len(pooled), len(own)
    px, depth = pooled[0].shape
    _, deep, slab = own[0].shape
    kc = slab // pairs
    back = jax.ShapeDtypeStruct((px, slab), BF16)
    part = jax.ShapeDtypeStruct((groups * px, kc), BF16)
    return pl.pallas_call(
        functools.partial(project_kernel, groups, pairs),
        out_shape=[back] * groups + [part] * pairs,
        in_specs=[whole(pltpu.SMEM)] + [whole()] * (groups + 2 * pairs),
        out_specs=[whole()] * (groups + pairs),
        scratch_shapes=[
            pltpu.VMEM((groups * pairs * 2, deep, slab), F32),
            pltpu.VMEM((pairs, groups * px, kc), BF16),
        ],
        name="project",
        compiler_params=pltpu.CompilerParams(vmem_limit_bytes=14 << 20),
        cost_estimate=pl.CostEstimate(
            flops=2 * groups * px * depth * slab, bytes_accessed=4 * depth * slab, transcendentals=0
        ),
    )(ids, *pooled, *own, *twin)


def packing(rows, colp, c1):
    main = c1 // 128
    rest = c1 - main * 128
    fit = 128 // rest if rest else 1
    deep = -(-rows // fit) if rest else 0
    return main, rest, deep, main * rows * colp + deep * colp


def cut_kernel(ids, projection, *refs):
    cuts, strip = refs[:-1], refs[-1]
    z, ch = ids[1], ids[2]
    deep, slab = cuts[0].shape
    groups = len(cuts)
    for i in range(projection.shape[0] // deep):
        for g in range(groups):
            strip[i, g] = projection[i * deep : (i + 1) * deep, g * slab : (g + 1) * slab].astype(F32)
    for k in range(groups):
        cuts[k][...] = strip[ch, jnp.bitwise_xor(z, k)].astype(BF16)


def cut(ids, projection, groups, shards):
    deep, slab = projection.shape[0] // shards, projection.shape[1] // groups
    return pl.pallas_call(
        cut_kernel,
        out_shape=[jax.ShapeDtypeStruct((deep, slab), BF16)] * groups,
        in_specs=[whole(pltpu.SMEM), whole()],
        out_specs=[whole()] * groups,
        scratch_shapes=[pltpu.VMEM((shards, groups, deep, slab), F32)],
        name="cut",
        compiler_params=pltpu.CompilerParams(vmem_limit_bytes=8 << 20),
    )(ids, projection)


def spread_kernel(groups, ids, *refs):
    backs, out, held = refs[:groups], refs[groups], refs[groups + 1]
    slab = backs[0].shape[1]
    for k in range(groups):
        held[jnp.bitwise_xor(ids[1], k)] = backs[k][...]
    for g in range(groups):
        out[:, g * slab : (g + 1) * slab] = held[g]


def spread(ids, backs):
    px, slab = backs[0].shape
    groups = len(backs)
    return pl.pallas_call(
        functools.partial(spread_kernel, groups),
        out_shape=jax.ShapeDtypeStruct((px, groups * slab), BF16),
        in_specs=[whole(pltpu.SMEM)] + [whole()] * groups,
        out_specs=whole(),
        scratch_shapes=[pltpu.VMEM((groups, px, slab), BF16)],
        name="spread",
        compiler_params=pltpu.CompilerParams(vmem_limit_bytes=6 << 20),
    )(ids, *backs)


def final_kernel(parts, per, orows, ocols, ids, mine, far_mine, *refs):
    own, far = refs[:parts], refs[parts : 2 * parts]
    out, held = refs[2 * parts :]
    first = ids[0] == 0
    for half in range(2):
        at = 0
        for i in range(parts):
            count = own[i].shape[1]
            for lane in range(0, count, 128):
                here = slice(lane, lane + 128)
                there = slice(at + lane, at + lane + 128)
                a = mine[:, there] if half == 0 else far_mine[:, there]
                b = far[i][:, here] if half == 0 else own[i][:, here]
                held[...] = jnp.where(first, a.astype(F32), b.astype(F32))
                for p in range(per):
                    for c in range(ocols):
                        some = held[pl.ds(p * orows * ocols + c, orows, stride=ocols), :]
                        out[half * per + p, c, :, there] = some.astype(BF16)
            at += count


def final(ids, mine, far_mine, own, far, per, orows, ocols):
    wide = mine.shape[1]
    return pl.pallas_call(
        functools.partial(final_kernel, len(own), per, orows, ocols),
        out_shape=jax.ShapeDtypeStruct((2 * per, ocols, orows, wide), BF16),
        in_specs=[whole(pltpu.SMEM)] + [whole()] * (2 + 2 * len(own)),
        out_specs=whole(),
        scratch_shapes=[pltpu.VMEM((mine.shape[0], 128), F32)],
        name="final",
        compiler_params=pltpu.CompilerParams(vmem_limit_bytes=10 << 20),
    )(ids, mine, far_mine, *own, *far)


def pack_kernel(groups, per, c1, colp, ids, pixels, above, below, gain, shift, *refs):
    outs, mean = refs[:groups], refs[groups]
    held, pair = refs[groups + 1 :]
    sec, z, ch, last = ids[0], ids[1], ids[2], ids[3]
    _, rows, cols, depth = pixels.shape
    main, rest, deep, size = packing(rows + 2, colp, c1)
    scale, offset = gain[...], shift[...]
    filler = jnp.zeros((colp - cols, depth), F32)
    for p in range(per):
        for r in range(rows + 2):
            if r == 0:
                value = above[p, 0].astype(F32)
            elif r == rows + 1:
                value = below[p, 0].astype(F32)
            else:
                value = pixels[sec * per + p, r - 1].astype(F32)
            if 1 <= r <= rows:
                i, half = (r - 1) // 2, cols // 2
                for t in range(depth // 128):
                    lanes = slice(t * 128, (t + 1) * 128)
                    if r % 2 == 1:
                        pair[t] = value[:, lanes]
                    else:
                        pair[t] = pair[t] + value[:, lanes]
                        both = pair.at[t]
                        total = both[pl.ds(0, half, stride=2), :] + both[pl.ds(1, half, stride=2), :]
                        mean[p, i * half : (i + 1) * half, lanes] = total * 0.25
            value = jax.nn.relu(value * scale + offset)
            if r == 0:
                value = jnp.where(ch == 0, 0.0, value)
            if r == rows + 1:
                value = jnp.where(ch == last, 0.0, value)
            value = jnp.concatenate([value, filler]).astype(BF16)
            for g in range(groups):
                for m in range(main):
                    at = p * size + (m * (rows + 2) + r) * colp
                    lane = g * c1 + m * 128
                    held[g, at : at + colp, :] = value[:, lane : lane + 128]
                if rest:
                    at = p * size + main * (rows + 2) * colp + (r % deep) * colp
                    lane = g * c1 + main * 128
                    into = (r // deep) * rest
                    held[g, at : at + colp, into : into + rest] = value[:, lane : lane + rest]
    for k in range(groups):
        outs[k][...] = held[jnp.bitwise_xor(z, k)]


def pack(ids, pixels, above, below, gain, shift, groups, per, colp):
    _, rows, cols, depth = pixels.shape
    c1 = depth // groups
    size = packing(rows + 2, colp, c1)[3]
    block = jax.ShapeDtypeStruct((per * size, 128), BF16)
    half = jax.ShapeDtypeStruct((per, rows * cols // 4, depth), F32)
    return pl.pallas_call(
        functools.partial(pack_kernel, groups, per, c1, colp),
        out_shape=[block] * groups + [half],
        in_specs=[whole(pltpu.SMEM)] + [whole()] * 5,
        out_specs=[whole()] * (groups + 1),
        scratch_shapes=[
            pltpu.VMEM((groups, per * size, 128), BF16),
            pltpu.VMEM((depth // 128, cols, 128), F32),
        ],
        name="pack",
        compiler_params=pltpu.CompilerParams(vmem_limit_bytes=14 << 20),
        cost_estimate=pl.CostEstimate(
            flops=4 * rows * cols * depth, bytes_accessed=6 * rows * cols * depth, transcendentals=0
        ),
    )(ids, pixels, above, below, gain, shift)


def stage_kernel(groups, per, rows, cols, colp, c1, *refs):
    blocks, source = refs[:groups], refs[groups]
    outs = refs[groups + 1 : 2 * groups + 1]
    flat, taps, squeezed, kernel, sem = refs[2 * groups + 1 :]
    load = pltpu.make_async_copy(source, kernel, sem)
    load.start()
    main, rest, deep, size = packing(rows + 2, colp, c1)
    tiles = main + (1 if rest else 0)
    orows, ocols = rows // 2, cols // 2
    base, wide = 8, (rows + 2) * colp
    half = colp // 2
    flat[...] = jnp.zeros(flat.shape, F32)
    for k in range(groups):
        for p in range(per):
            for t in range(tiles):
                lanes = 128 if t < main else rest
                if t < main:
                    at = p * size + t * wide
                    flat[t, base : base + wide, :] = blocks[k][at : at + wide, :].astype(F32)
                else:
                    for r in range(rows + 2):
                        at = p * size + main * wide + (r % deep) * colp
                        lane = (r // deep) * rest
                        flat[t, base + r * colp : base + (r + 1) * colp, 0:rest] = blocks[k][
                            at : at + colp, lane : lane + rest
                        ].astype(F32)
                span = (rows + 1) * colp + base + 8
                tall = flat[t, 0:span, :] + flat[t, colp : colp + span, :]
                flat[tiles, 0:span, :] = tall
                both = flat[tiles, 0 : span - 8, :] + flat[tiles, 1 : span - 7, :]
                flat[tiles + 1, 0 : span - 8, :] = both * 0.25
                plane = flat.at[tiles + 1]
                for tap in range(9):
                    ty, tx = tap // 3, tap % 3
                    for i in range(orows):
                        q = base + (2 * i + ty) * colp + tx - 1
                        value = plane[pl.ds(q, half, stride=2), :].astype(BF16)
                        row = ((k * per + p) * orows + i) * half
                        taps[tap, row : row + half, t * 128 : t * 128 + lanes] = value[:, :lanes]
    load.wait()
    total = jnp.dot(taps[0], kernel[0], preferred_element_type=F32)
    for tap in range(1, 9):
        total = total + jnp.dot(taps[tap], kernel[tap], preferred_element_type=F32)
    for k in range(groups):
        for p in range(per):
            for i in range(orows):
                row = ((k * per + p) * orows + i) * half
                at = (p * orows + i) * ocols
                squeezed[at : at + ocols, :] = total[row : row + ocols]
        outs[k][...] = squeezed[...].astype(outs[k].dtype)


def stage(blocks, kernel, per, rows, cols, colp):
    groups = len(blocks)
    taps, c1, depth = kernel.shape
    tiles = -(-c1 // 128)
    px = per * rows * cols // 4
    count = groups * per * (rows // 2) * (colp // 2)
    return pl.pallas_call(
        functools.partial(stage_kernel, groups, per, rows, cols, colp, c1),
        out_shape=[jax.ShapeDtypeStruct((px, depth), F32)]
        + [jax.ShapeDtypeStruct((px, depth), BF16)] * (groups - 1),
        in_specs=[whole()] * groups + [pl.BlockSpec(memory_space=pltpu.HBM)],
        out_specs=[whole()] * groups,
        scratch_shapes=[
            pltpu.VMEM((tiles + 2, (rows + 3) * colp + 32, 128), F32),
            pltpu.VMEM((taps, count, c1), BF16),
            pltpu.VMEM((px, depth), F32),
            pltpu.VMEM(kernel.shape, BF16),
            pltpu.SemaphoreType.DMA,
        ],
        name="stage",
        compiler_params=pltpu.CompilerParams(vmem_limit_bytes=12 << 20),
        cost_estimate=pl.CostEstimate(
            flops=2 * count * taps * c1 * depth, bytes_accessed=4 * groups * px * depth, transcendentals=0
        ),
    )(*blocks, streamed(kernel))


def body(pixels, first_gain, first_shift, first_kernel, projection, second_gain, second_shift, second_kernel):
    sec = lax.axis_index("section")
    z = lax.axis_index("img")
    ch = lax.axis_index("ch")
    sections = lax.axis_size("section")
    groups = lax.axis_size("img")
    shards = lax.axis_size("ch")
    pairs = shards // 2
    y, core = ch // 2, ch % 2
    per = pixels.shape[0] // sections
    _, rows, cols, depth = pixels.shape
    orows, ocols = rows // 2, cols // 2
    wide = second_gain.shape[0]
    slab = wide // groups
    kc = slab // pairs
    kd = kc // 2
    c1 = depth // groups

    other_kernel = swap(second_kernel, "ch", 1)

    ids = jnp.stack([sec, z, ch, jnp.int32(shards - 1), y, core, z * pairs + y]).astype(jnp.int32)
    colp = -(-(cols + 2) // 16) * 16
    tails = lax.dynamic_slice_in_dim(pixels[:, -1:], sec * per, per, 0)
    heads = lax.dynamic_slice_in_dim(pixels[:, :1], sec * per, per, 0)
    pixels, tails, heads = lax.optimization_barrier((pixels, tails, heads))
    above = lax.ppermute(tails, "ch", [(i, i + 1) for i in range(shards - 1)])
    below = lax.ppermute(heads, "ch", [(i + 1, i) for i in range(shards - 1)])
    packed = pack(
        ids,
        pixels,
        above,
        below,
        first_gain.reshape(1, -1),
        first_shift.reshape(1, -1),
        groups,
        per,
        colp,
    )
    blocks, mean = packed[:groups], packed[groups]
    got = [blocks[0]] + [swap(blocks[k], "img", k) for k in range(1, groups)]

    cuts = cut(ids, projection, groups, shards)
    proj_z = join([cuts[0]] + [swap(cuts[k], "img", k) for k in range(1, groups)])
    proj_own = [proj_z] + [swap(proj_z, "ch", k, 2) for k in range(1, pairs)]
    proj_twin = [swap(part, "ch", 1) for part in proj_own]

    total, *sent = stage(got, first_kernel.reshape(9, c1, depth), per, rows, cols, colp)
    came = [swap(sent[k - 1], "img", k) for k in range(1, groups)]
    pooled = pool(total, mean, came)
    pooled_all = [pooled] + [swap(pooled, "img", k) for k in range(1, groups)]
    px = per * orows * ocols
    imgs = groups * per
    out_px = orows * ocols
    made = project(ids, pooled_all, proj_own, proj_twin)
    back, chip = made[:groups], made[groups:]

    chip = [chip[0]] + [swap(chip[k], "ch", k, 2) for k in range(1, pairs)]
    twin = [swap(chip[0], "ch", 1)]
    twin += [swap(part, "ch", 1) for part in chip[1:]]
    back = [back[0]] + [swap(back[k], "img", k) for k in range(1, groups)]
    w_own = streamed(second_kernel.reshape(9 * kd, wide))
    w_other = streamed(other_kernel.reshape(9 * kd, wide))

    unit = wide // 10
    plan = ((0, 4, 0), (1, 3, 4), (0, 3, 7))
    names = [("ch", 1 << i, 2) for i in range(pairs.bit_length() - 1)]
    names_z = [("img", 1 << i, 1) for i in range(groups.bit_length() - 1)]
    values = []
    for j, (kind, n, first) in enumerate(plan):
        first *= unit
        hops = names_z + names if kind else names + names_z
        keys = [(a, b) for a in range(pairs) for b in range(groups)]

        def split(keys, hop):
            axis, k, _ = hop
            bit = [key[0] & k if axis == "ch" else key[1] & k for key in keys]
            rows = ([i for i, x in enumerate(bit) if x], [i for i, x in enumerate(bit) if not x])
            return rows, [key for key, x in zip(keys, bit) if not x]

        rows, keys = split(keys, hops[0])
        if j == 0:
            a_own, a_other, w_own, w_other, sent, kept = unfold(
                ids,
                second_gain.reshape(groups * pairs, kc),
                second_shift.reshape(groups * pairs, kc),
                [c.reshape(imgs, out_px, kc) for c in chip],
                [c.reshape(imgs, out_px, kc) for c in twin],
                ocols,
                w_own,
                w_other,
                first,
                n * unit,
                unit,
                rows,
                px,
            )
        else:
            sent, kept = mix(a_own, a_other, w_own, w_other, first, n * unit, unit, rows, px)
        for h, hop in enumerate(hops):
            axis, k, size = hop
            came = swap(sent, axis, k, size)
            if h + 1 < len(hops):
                rows, keys = split(keys, hops[h + 1])
                sent, kept = merge(kept, came, rows, px)
        values.append((kept, came, first, n * unit))

    mine_projected = spread(ids, back)
    far_projected = lax.ppermute(mine_projected, "section", [(1, 0)])
    outs, fars = [], []
    for j, some in enumerate((values[:2], values[2:])):
        outs.append(finish([v[:2] for v in some], mine_projected, some[0][2]))
        fars.append(lax.ppermute(outs[j], "section", [(0, 1)]))
    block = final(ids, mine_projected, far_projected, outs, fars, per, orows, ocols)
    return block.transpose(0, 2, 1, 3)[None]


def solution(mesh):
    placed = (
        P("img", "ch", None, None),
        P(),
        P(),
        P(None, None, "img", None),
        P("img", None),
        P(),
        P(),
        P(None, None, ("img", "ch"), None),
    )

    return jax.shard_map(
        body,
        mesh=mesh,
        in_specs=placed,
        out_specs=P("section", "img", "ch", None, None),
        check_vma=False,
    )
```
